32 devices in a mesh: sub: 8 (over y, x, core), coarse: 4 (over z).
Axes of the slice: x: 2, y: 2, z: 4, core: 2. Of those that a mesh axis runs over, the one named last changes fastest.
Arguments:
- right_side: float32 [8, 4, 128, 128], P('sub', 'coarse'), may hold values from -150 to 150
- diagonal: float32 [8, 4, 128, 128], P('sub', 'coarse'), may hold values from 2 to 8
- cell_link: float32 [8, 4, 128, 128], P('sub', 'coarse'), may hold values from 0.2 to 0.9
- block_inverse: float32 [8, 4, 128, 128, 128], P('sub', 'coarse'), may hold values from -1 to 1
- coupling: float32 [8, 4, 4, 128, 128], P('sub', 'coarse'), may hold values from -0.26516503 to 0.26516503
- coarse_basis: float32 [8, 4, 128, 128], P('sub', 'coarse'), may hold values from -6 to 6
- coarse_inverse: float32 [512, 512], P('coarse'), may hold values from -0.25 to 0.25
- partner: int32 [8, 4], P('sub'), may hold values from 0 to 7, as said below
- margin_width: int32 [8, 4], P('sub'), may hold values from 4 to 8, as said below
- margin_blocks: int32 [8, 4, 4, 8], P('sub', 'coarse'), may hold values from 0 to 127
- aggregate: int32 [8, 4, 128], P('sub', 'coarse'), may hold values from 0 to 511, as said below
Outputs:
- solution: float32 [8, 4, 128, 128], P('sub', 'coarse')
The draws below stay inside these ranges and needn't reach their ends.
Inputs may be any that keep to these rules, and one draw needn't show every extreme that they name: partner[s, r] differs from s, partner[partner[s, r], r] = s, and the 4 partners of one subdomain are distinct. margin_width[partner[s, r], r] = margin_width[s, r]; every colour round has a pair with width 8. `margin_blocks`: entries with w >= margin_width[s, r] are not used. aggregate[s, c, b] lies in (s * 4 + c) * 16 to (s * 4 + c + 1) * 16 - 1, and every one of these 16 aggregates has a block of part [s, c].
All inputs are finite; a program needn't handle non-finite values.
Results may differ from the reference program's by a relative error of at most 0.0003.
Values sent between devices are 32-bit elements; how exact they have to be, the bound alone decides.
No kernel may reach another device: no remote copies, remote signals or barrier semaphores. Data moves between devices by JAX's collectives and lax.ppermute only.
A program may use at most 64 MiB of HBM per device.

```python
import math
import jax
import jax.numpy as jnp
from jax import lax

BS = 128
BPD = 128
AGG_DEV = 16
ITERS = 4
NSUB = 8
NCO = 4
ROUNDS = 4
WMAX = 8
NAGG = 512


def colour_rounds(key):
    base_key = jax.random.fold_in(key, 41)
    key_perm, key_pick, key_width, key_full = jax.random.split(base_key, 4)
    labels = jax.random.permutation(key_perm, NSUB)
    places = jnp.argsort(labels)
    chosen = jax.random.permutation(key_pick, NSUB - 1)[:ROUNDS]
    position = places[:, None]
    column = chosen[None, :]
    final_slot = NSUB - 1
    other_place = jnp.where(position == final_slot, column, jnp.where(position == column, final_slot, jnp.remainder(2 * column - position, NSUB - 1)))
    paired = labels[other_place]
    own_index = jnp.arange(NSUB)[:, None]
    raw_widths = jax.random.randint(key_width, (NSUB, ROUNDS), max(1, WMAX // 2), WMAX + 1)
    lower_side = jnp.minimum(own_index, paired)
    widths = jnp.take_along_axis(raw_widths, lower_side, axis=0)
    special = jax.random.randint(key_full, (1, ROUNDS), 0, NSUB)
    widths = jnp.where((own_index == special) | (paired == special), WMAX, widths)
    return (paired.astype(jnp.int32), widths.astype(jnp.int32))


def draw_partner(key, part):
    return colour_rounds(key)[0]


def draw_margin_width(key, part):
    return colour_rounds(key)[1]


def draw_aggregate(key, part):
    raw_local = jax.random.randint(jax.random.fold_in(key, 77), (NSUB, NCO, BPD), 0, AGG_DEV)
    block_index = jnp.arange(BPD)[None, None, :]
    local_ids = jnp.where(block_index < AGG_DEV, block_index, raw_local)
    offsets = (jnp.arange(NSUB)[:, None] * NCO + jnp.arange(NCO)[None, :]) * AGG_DEV
    return (offsets[:, :, None] + local_ids).astype(jnp.int32)


def draw_right_side(key, part):
    key_base, key_scale = jax.random.split(jax.random.fold_in(key, 5), 2)
    array_shape = (NSUB, NCO, BPD, BS)
    block_scale = jnp.exp(jax.random.uniform(key_scale, (NSUB, NCO, BPD, 1), jnp.float32, 0.0, math.log(10.0)))
    order = (jnp.arange(NSUB)[:, None] * NCO + jnp.arange(NCO)[None, :]).astype(jnp.float32) / (NSUB * NCO - 1)
    ramp = jnp.exp(order * math.log(3.0))[:, :, None, None]
    base_values = jnp.clip(jax.random.normal(key_base, array_shape, jnp.float32), -5.0, 5.0)
    return base_values * block_scale * ramp


def draw_block_inverse(key, part):
    key_diag, key_off = jax.random.split(jax.random.fold_in(key, 9), 2)
    array_shape = (NSUB, NCO, BPD, BS, BS)
    diagonal_part = jax.random.uniform(key_diag, (NSUB, NCO, BPD, BS, 1), jnp.float32, 0.3, 0.6)
    spread = jnp.clip(jax.random.normal(key_off, array_shape, jnp.float32), -5.0, 5.0) * (0.25 / BS)
    identity = jnp.arange(BS)[:, None] == jnp.arange(BS)[None, :]
    return jnp.where(identity, diagonal_part, spread)


def place_ends(values, key, smallest, top_value):
    spot = [jax.random.randint(jax.random.fold_in(key, axis), (), 0, length) for axis, length in enumerate(values.shape)]
    main_axis = values.shape.index(max(values.shape))
    beside = spot[:main_axis] + [(spot[main_axis] + 1) % values.shape[main_axis]] + spot[main_axis + 1:]
    return values.at[tuple(spot)].set(smallest).at[tuple(beside)].set(top_value)


def block_levels(own_key, shape, shards, low, largest):
    def one(dim, parts):
        steps = jax.random.uniform(jax.random.fold_in(jax.random.fold_in(own_key, 6), dim), (parts,), jnp.float32, low / len(shards), largest / len(shards))
        return jnp.repeat(jnp.exp(steps), shape[dim] // parts).reshape((-1,) + (1,) * (len(shape) - dim - 1))

    loudness = one(*shards[0])
    for cut in shards[1:]:
        loudness = loudness * one(*cut)
    return loudness


def gaussian(own_key, extent, scale, limit, shards=(), kind=jnp.bfloat16):
    values = scale * jax.random.normal(own_key, extent, jnp.float32)
    if shards:
        values = values * block_levels(own_key, extent, shards, -0.22, 0.18)
    return jnp.clip(values, -limit, limit).astype(kind)


def setup_inputs(seed: int = 0) -> dict:
    arg_keys = jax.random.split(jax.random.key(seed), 12)
    right_side = draw_right_side(jax.random.fold_in(arg_keys[11], 71), 0)
    diagonal = jnp.clip(jnp.exp(math.log(8.0) - 1.3862944 * jax.random.uniform(arg_keys[1], (NSUB, NCO, BPD, BS), jnp.float32) ** block_levels(arg_keys[1], (NSUB, NCO, BPD, BS), ((0, 8), (1, 4)), -0.2, 0.2)), 2.0, 8.0)
    cell_link = jnp.clip(0.2 + 0.7 * jax.random.uniform(arg_keys[2], (NSUB, NCO, BPD, BS), jnp.float32) ** block_levels(arg_keys[2], (NSUB, NCO, BPD, BS), ((0, 8), (1, 4)), -0.2, 0.2), 0.2, 0.9)
    block_inverse = draw_block_inverse(jax.random.fold_in(arg_keys[11], 71), 0)
    coupling = gaussian(arg_keys[4], (NSUB, NCO, ROUNDS, BS, BS), (0.5 / BS ** 0.5), 0.26516503, ((0, 8), (1, 4)), jnp.float32)
    coarse_basis = gaussian(arg_keys[5], (NSUB, NCO, BPD, BS), 1.0, 6.0, ((0, 8), (1, 4)), jnp.float32)
    coarse_inverse = gaussian(arg_keys[6], (NAGG, NAGG), NAGG ** -0.5, 0.25, ((0, 4),), jnp.float32)
    partner = draw_partner(jax.random.fold_in(arg_keys[11], 71), 0)
    margin_width = draw_margin_width(jax.random.fold_in(arg_keys[11], 71), 0)
    margin_blocks = place_ends(jax.random.randint(arg_keys[9], (NSUB, NCO, ROUNDS, WMAX), 0, BPD), jax.random.fold_in(arg_keys[9], 1), 0, BPD - 1).astype(jnp.int32)
    aggregate = draw_aggregate(jax.random.fold_in(arg_keys[11], 71), 0)
    return {"right_side": right_side, "diagonal": diagonal, "cell_link": cell_link, "block_inverse": block_inverse, "coupling": coupling, "coarse_basis": coarse_basis, "coarse_inverse": coarse_inverse, "partner": partner, "margin_width": margin_width, "margin_blocks": margin_blocks, "aggregate": aggregate}


def margin_sum(values, partner, margin_width, margin_blocks, coupling):
    block_count = values.shape[2]
    widest = margin_blocks.shape[3]
    result = jnp.zeros_like(values)
    for round_id in range(margin_blocks.shape[2]):
        paired = partner[:, round_id]
        source = margin_blocks[paired, :, round_id, :]
        remote = values[paired]
        picked = jnp.take_along_axis(remote, source[:, :, :, None], axis=2)
        mapped = jnp.einsum('scij,scwj->scwi', coupling[:, :, round_id], picked, precision=lax.Precision.HIGHEST)
        live_mask = (jnp.arange(widest)[None, :] < margin_width[:, round_id][:, None]).astype(values.dtype)
        mapped = mapped * live_mask[:, None, :, None]
        target = (margin_blocks[:, :, round_id, :, None] == jnp.arange(block_count)[None, None, None, :]).astype(values.dtype)
        result = result + jnp.einsum('scwb,scwi->scbi', target, mapped, precision=lax.Precision.HIGHEST)
    return result

def line_operator(values, diagonal, cell_link):
    full_shape = values.shape
    flat_line = values.reshape(full_shape[0], full_shape[1], -1)
    link_line = cell_link.reshape(full_shape[0], full_shape[1], -1)
    zero_pad = jnp.zeros((full_shape[0], full_shape[1], 1), values.dtype)
    ahead_terms = jnp.concatenate([flat_line[:, :, 1:], zero_pad], axis=2) * link_line
    behind_terms = jnp.concatenate([zero_pad, (link_line * flat_line)[:, :, :-1]], axis=2)
    return diagonal * values - (ahead_terms + behind_terms).reshape(full_shape)

def givens_solve(columns, beta):
    steps_count = len(columns)
    cosines = []
    sines = []
    side_terms = [beta] + [jnp.zeros_like(beta) for unused in range(steps_count)]
    triangle = []
    for column_id in range(steps_count):
        column = list(columns[column_id])
        for row_id in range(column_id):
            upper = column[row_id]
            lower = column[row_id + 1]
            column[row_id] = cosines[row_id] * upper + sines[row_id] * lower
            column[row_id + 1] = cosines[row_id] * lower - sines[row_id] * upper
        upper = column[column_id]
        lower = column[column_id + 1]
        radius = jnp.sqrt(upper * upper + lower * lower)
        cosine = upper / radius
        sine_value = lower / radius
        column[column_id] = radius
        cosines.append(cosine)
        sines.append(sine_value)
        side_terms[column_id + 1] = -sine_value * side_terms[column_id]
        side_terms[column_id] = cosine * side_terms[column_id]
        triangle.append(column)
    weights = [None] * steps_count
    for column_id in reversed(range(steps_count)):
        running = side_terms[column_id]
        for later_col in range(column_id + 1, steps_count):
            running = running - triangle[later_col][column_id] * weights[later_col]
        weights[column_id] = running / triangle[column_id][column_id]
    return weights

def reference(right_side, diagonal, cell_link, block_inverse, coupling, coarse_basis, coarse_inverse, partner, margin_width, margin_blocks, aggregate):
    highest = lax.Precision.HIGHEST
    factor = (BS * BPD / AGG_DEV) ** (-0.5)

    def margin(values):
        return margin_sum(values, partner, margin_width, margin_blocks, coupling)

    def precondition(values):
        local_part = jnp.einsum('scbij,scbj->scbi', block_inverse, values + margin(values), precision=highest)
        inner = lax.optimization_barrier(jnp.sum(coarse_basis * values, axis=3))
        restricted = jax.ops.segment_sum(inner.reshape(-1), aggregate.reshape(-1), num_segments=NAGG) * factor
        coarse = jnp.dot(coarse_inverse, restricted, precision=highest)
        return local_part + coarse[aggregate][..., None] * coarse_basis

    def operator(values):
        return line_operator(values, diagonal, cell_link) - margin(values)
    beta = jnp.sqrt(jnp.sum(right_side * right_side))
    basis_list = [right_side / beta]
    directions = []
    columns = []
    for krylov_step in range(ITERS):
        current = basis_list[-1]
        direction = precondition(current)
        directions.append(direction)
        product = operator(direction)
        projected = [jnp.sum(vector * product) for vector in basis_list]
        for position in range(len(projected)):
            product = product - projected[position] * basis_list[position]
        norm_new = jnp.sqrt(jnp.sum(product * product))
        columns.append(projected + [norm_new])
        basis_list.append(product / norm_new)
    weights = givens_solve(columns, beta)
    solution = weights[0] * directions[0]
    for position in range(1, ITERS):
        solution = solution + weights[position] * directions[position]
    return solution
```

```python
import jax
import jax.numpy as jnp
from jax import lax
from jax.experimental import pallas as pl
from jax.experimental.pallas import tpu as pltpu
from jax.sharding import PartitionSpec as P

BS = 128
BPD = 128
AGG_DEV = 16
ITERS = 4
LANES = 128
ROWS = 8
BF16 = jnp.bfloat16
F32 = jnp.float32


def split(values):
    high = values.astype(BF16)
    low = (values - high.astype(F32)).astype(BF16)
    return high, low


def dot_rows(left, right):
    return lax.dot_general(left, right, (((1,), (1,)), ((), ())), preferred_element_type=F32)


def dot_plain(left, right):
    return lax.dot_general(left, right, (((1,), (0,)), ((), ())), preferred_element_type=F32)


def paired_rows(values):
    high, low = split(values)
    return jnp.concatenate(
        [
            jnp.concatenate([high, high], axis=1),
            jnp.concatenate([low, jnp.zeros_like(low)], axis=1),
        ],
        axis=0,
    )


def pick(selector, values):
    high, low = split(values)
    return dot_plain(selector, jnp.concatenate([high, low], axis=0))


def couple(arrived, coupling_ref, target_ref):
    count = arrived.shape[0]
    left = paired_rows(arrived)
    highs = []
    lows = []
    for round_id in range(coupling_ref.shape[0]):
        both = dot_rows(left, coupling_ref[round_id])
        high, low = split(both[:count] + both[count:])
        highs.append(high)
        lows.append(low)
    return dot_plain(target_ref[...], jnp.concatenate(highs + lows, axis=0))


def column_sum(values):
    return jnp.sum(values, axis=0, keepdims=True)


def line_product(values, diagonal, link):
    rows = values.shape[0]
    lanes = values.shape[1]
    row = lax.broadcasted_iota(jnp.int32, values.shape, 0)
    lane = lax.broadcasted_iota(jnp.int32, values.shape, 1)
    next_lane = pltpu.roll(values, lanes - 1, 1)
    next_row = pltpu.roll(next_lane, rows - 1, 0)
    ahead = jnp.where(lane < lanes - 1, next_lane, jnp.where(row < rows - 1, next_row, 0.0))
    scaled = link * values
    last_lane = pltpu.roll(scaled, 1, 1)
    last_row = pltpu.roll(last_lane, 1, 0)
    behind = jnp.where(lane > 0, last_lane, jnp.where(row > 0, last_row, 0.0))
    return diagonal * values - (ahead * link + behind)


def restriction_rows(vector, basis, member, own_row, factor):
    inner = jnp.sum(basis * vector, axis=1, keepdims=True)
    return own_row * (column_sum(inner * member) * factor)


def vmem(shape, dtype=F32):
    return pltpu.VMEM(shape, dtype)


def call(kernel, outs, *args, name):
    spec = pl.BlockSpec(memory_space=pltpu.VMEM)
    return pl.pallas_call(
        kernel,
        out_shape=outs,
        in_specs=[spec] * len(args),
        out_specs=[spec] * len(outs),
        name=name,
        compiler_params=pltpu.CompilerParams(vmem_limit_bytes=48 * 1024 * 1024),
    )(*args)


def on_device(
    right_side,
    diagonal,
    cell_link,
    block_inverse,
    coupling,
    coarse_basis,
    coarse_inverse,
    partner,
    margin_width,
    margin_blocks,
    aggregate,
):
    subs = lax.axis_size("sub")
    parts = lax.axis_size("coarse")
    devices = subs * parts
    own_sub = lax.axis_index("sub")
    own_part = lax.axis_index("coarse")
    block_count = right_side.shape[2]
    unknowns = right_side.shape[3]
    rounds = margin_blocks.shape[2]
    widest = margin_blocks.shape[3]
    aggregates = coarse_inverse.shape[1]
    own_aggregates = aggregates // devices
    sub_aggregates = subs * own_aggregates
    factor = (BS * BPD / AGG_DEV) ** (-0.5)
    coarse_rows = aggregates // LANES
    stat_rows = -(-(coarse_rows + ITERS) // ROWS) * ROWS
    slot_rows = subs * widest
    full = (block_count, unknowns)

    basis = coarse_basis[0, 0]
    diagonal_local = diagonal[0, 0]
    link_local = cell_link[0, 0]
    start_vector = right_side[0, 0]
    paired = partner[0]
    widths = margin_width[0]
    blocks = margin_blocks[0, 0]
    member_of = aggregate[0, 0]

    block_ids = jnp.arange(block_count)
    meets = paired[:, None] == jnp.arange(subs)[None, :]
    at_block = blocks[:, :, None] == block_ids[None, None, :]
    selector = jnp.sum(
        (meets[:, :, None, None] & at_block[:, None, :, :]).astype(F32), axis=0
    ).reshape(slot_rows, block_count)
    selector = jnp.concatenate([selector, selector], axis=1).astype(BF16)
    live = jnp.arange(widest)[None, :] < widths[:, None]
    wanted = jnp.where(
        meets[:, :, None] & live[:, None, :], blocks[:, None, :], -1
    ).reshape(rounds * slot_rows)
    target = (block_ids[:, None] == wanted[None, :]).astype(BF16)
    target = jnp.concatenate([target, target], axis=1)
    own_first = (own_sub * parts + own_part) * own_aggregates
    lanes = jnp.arange(LANES)
    member = ((member_of % LANES)[:, None] == lanes[None, :]).astype(F32)
    own_row = jnp.broadcast_to(
        (jnp.arange(coarse_rows) == own_first // LANES)[:, None], (coarse_rows, LANES)
    ).astype(F32)
    sub_lane = member_of - own_first + own_sub * own_aggregates
    sub_member = (sub_lane[:, None] == jnp.arange(sub_aggregates)[None, :]).astype(F32)
    sub_member_lane = ((sub_lane % LANES)[:, None] == lanes[None, :]).astype(F32)
    part_mask = jnp.broadcast_to(
        (jnp.arange(parts) == own_part)[:, None, None], (parts, widest, LANES)
    ).astype(F32)

    sent_rows = coarse_inverse.reshape(subs // parts, parts, own_aggregates, aggregates)
    sent_rows = sent_rows.transpose(1, 0, 2, 3).reshape(parts, -1, aggregates)
    coarse_block = lax.all_to_all(sent_rows, "coarse", 0, 0).reshape(sub_aggregates, aggregates)

    def prepare(inverse_ref, coupling_ref, weight_ref, coupling_pair_ref):
        def step(position, carry):
            for offset in range(2):
                high, low = split(inverse_ref[position * 2 + offset])
                rows = pl.ds(offset * unknowns, unknowns)
                weight_ref[position, rows, 0:unknowns] = high
                weight_ref[position, rows, unknowns : 2 * unknowns] = low
            return carry

        lax.fori_loop(0, block_count // 2, step, 0, unroll=2)
        for round_id in range(rounds):
            high, low = split(coupling_ref[round_id])
            coupling_pair_ref[round_id, :, 0:unknowns] = high
            coupling_pair_ref[round_id, :, unknowns : 2 * unknowns] = low

    weights, coupling_pairs = call(
        prepare,
        [
            vmem((block_count // 2, 2 * unknowns, 2 * unknowns), BF16),
            vmem((rounds, unknowns, 2 * unknowns), BF16),
        ],
        block_inverse[0, 0],
        coupling[0, 0],
        name="prepare",
    )

    def write_statistics(stat_ref, vector, basis_value, member_value, own_row_value, dots):
        stat_ref[...] = jnp.zeros_like(stat_ref)
        stat_ref[0:coarse_rows, :] = restriction_rows(
            vector, basis_value, member_value, own_row_value, factor
        )
        for position, other in enumerate(dots):
            stat_ref[coarse_rows + position : coarse_rows + position + 1, :] = column_sum(
                other * vector
            )

    def begin(start_ref, basis_ref, member_ref, row_ref, lane_ref, selector_ref, out_ref, stat_ref):
        start = start_ref[...]
        basis_value = basis_ref[...]
        table = selector_ref[...]
        out_ref[:, 0:widest, :] = pick(table, start).reshape(subs, widest, unknowns)
        out_ref[:, widest : 2 * widest, :] = pick(table, basis_value).reshape(
            subs, widest, unknowns
        )
        out_ref[:, 2 * widest : 3 * widest, :] = pick(table, lane_ref[...]).reshape(
            subs, widest, LANES
        )
        write_statistics(stat_ref, start, basis_value, member_ref[...], row_ref[...], [start])

    outgoing, statistics = call(
        begin,
        [vmem((subs, 3 * widest, unknowns)), vmem((stat_rows, LANES))],
        start_vector,
        basis,
        member,
        own_row,
        sub_member_lane,
        selector,
        name="begin",
    )

    def smooth(arrived, vector_ref, stat_ref, weight_ref, pair_ref, target_ref, selector_ref, mask_ref, out_ref, slot_ref):
        shifted = vector_ref[...] + couple(arrived, pair_ref, target_ref)
        out_ref[...] = shifted
        row = lax.broadcasted_iota(jnp.int32, (ROWS, unknowns), 0)

        def step(group, carry):
            rows = pl.ds(pl.multiple_of(group * ROWS, ROWS), ROWS)
            left = paired_rows(out_ref[rows, :])
            total = jnp.zeros((ROWS, unknowns), F32)
            for offset in range(ROWS // 2):
                both = dot_rows(left, weight_ref[group * (ROWS // 2) + offset])
                both = both[:ROWS] + both[ROWS:]
                total = jnp.where(row == 2 * offset, both[:, :unknowns], total)
                total = jnp.where(row == 2 * offset + 1, both[:, unknowns:], total)
            out_ref[rows, :] = total
            return carry

        lax.fori_loop(0, block_count // ROWS, step, 0, unroll=2)
        margin_rows = pick(selector_ref[...], out_ref[...]).reshape(subs, widest, unknowns)
        statistic = stat_ref[...]
        for sub_id in range(subs):
            for part_id in range(parts):
                slot = sub_id * parts + part_id
                slot_ref[slot, 0:widest, :] = margin_rows[sub_id] * mask_ref[part_id]
                slot_ref[slot, widest:, :] = statistic

    def smooth_first(arrived_ref, *refs):
        *rest, basis_ref, lane_ref = refs
        smooth(arrived_ref[:, 0:widest, :].reshape(slot_rows, unknowns), *rest)
        basis_ref[...] = arrived_ref[:, widest : 2 * widest, :].reshape(slot_rows, unknowns)
        lane_ref[...] = arrived_ref[:, 2 * widest : 3 * widest, :].reshape(slot_rows, LANES)

    def smooth_later(arrived_ref, *refs):
        smooth(arrived_ref[...].reshape(slot_rows, unknowns), *refs)

    def advance(step_id):
        last = step_id == ITERS - 1

        def kernel(*refs):
            (
                arrived_ref,
                smoothed_ref,
                vector_ref,
                coarse_ref,
                sub_member_ref,
                member_ref,
                row_ref,
                basis_ref,
                margin_basis_ref,
                margin_lane_ref,
                pair_ref,
                target_ref,
                selector_ref,
                diagonal_ref,
                link_ref,
            ) = refs[:15]
            earlier = refs[15 : 15 + 3 * step_id]
            v_refs = earlier[:step_id]
            z_refs = earlier[step_id : 2 * step_id]
            m_refs = earlier[2 * step_id :]
            outs = refs[15 + 3 * step_id :]
            total = arrived_ref[0, widest:, :]
            for slot in range(1, devices):
                total = total + arrived_ref[slot, widest:, :]
            products = jnp.sum(total[coarse_rows : coarse_rows + step_id + 1], axis=1, keepdims=True)
            heads = [products[i : i + 1] for i in range(step_id)]
            square = products[step_id : step_id + 1]
            remaining = square
            for head in heads:
                remaining = remaining - head * head
            length = jnp.sqrt(jnp.maximum(remaining, square * 1e-12))
            scale = 1.0 / length
            gathered = coarse_ref[:, 0:LANES] * total[0:1]
            for chunk in range(1, coarse_rows):
                gathered = gathered + (
                    coarse_ref[:, chunk * LANES : (chunk + 1) * LANES] * total[chunk : chunk + 1]
                )
            column = jnp.sum(gathered, axis=1, keepdims=True)
            same = lax.broadcasted_iota(jnp.int32, (LANES, LANES), 0) == lax.broadcasted_iota(
                jnp.int32, (LANES, LANES), 1
            )
            coarse_lines = [
                column_sum(jnp.where(same, column[start : start + LANES], 0.0))
                for start in range(0, sub_aggregates, LANES)
            ]
            own_coarse = jnp.zeros((block_count, LANES), F32)
            for chunk, line in enumerate(coarse_lines):
                own_coarse = own_coarse + (
                    sub_member_ref[:, chunk * LANES : (chunk + 1) * LANES] * line
                )
            own_coarse = jnp.sum(own_coarse, axis=1, keepdims=True)
            basis_value = basis_ref[...]
            direction = smoothed_ref[...] + own_coarse * basis_value
            for head, z_ref in zip(heads, z_refs):
                direction = direction - head * z_ref[...]
            direction = direction * scale
            pieces = []
            for sub_id in range(subs):
                piece = arrived_ref[sub_id * parts, 0:widest, :]
                for part_id in range(1, parts):
                    piece = piece + arrived_ref[sub_id * parts + part_id, 0:widest, :]
                line = coarse_lines[sub_id * own_aggregates // LANES]
                rows = pl.ds(sub_id * widest, widest)
                weight = jnp.sum(margin_lane_ref[rows, :] * line, axis=1, keepdims=True)
                pieces.append(piece + weight * margin_basis_ref[rows, :])
            margin_rows = jnp.concatenate(pieces, axis=0)
            for head, m_ref in zip(heads, m_refs):
                margin_rows = margin_rows - head * m_ref[...]
            margin_rows = margin_rows * scale
            vector = vector_ref[...]
            for head, v_ref in zip(heads, v_refs):
                vector = vector - head * v_ref[...]
            vector = vector * scale
            product = line_product(direction, diagonal_ref[...], link_ref[...]) - couple(
                margin_rows, pair_ref, target_ref
            )
            against = [v_ref[...] for v_ref in v_refs] + [vector, product]
            if last:
                direction_ref, head_ref, out_ref = outs
                block = jnp.concatenate(
                    [column_sum(other * product) for other in against]
                    + [jnp.zeros((ROWS - len(against), LANES), F32)],
                    axis=0,
                )
                for slot in range(devices):
                    out_ref[slot] = block
            else:
                direction_ref, head_ref, new_v_ref, margin_ref, product_ref, out_ref, stat_ref = outs
                new_v_ref[...] = vector
                margin_ref[...] = margin_rows
                product_ref[...] = product
                out_ref[...] = pick(selector_ref[...], product).reshape(subs, widest, unknowns)
                write_statistics(
                    stat_ref, product, basis_value, member_ref[...], row_ref[...], against
                )
            direction_ref[...] = direction
            head_ref[...] = jnp.broadcast_to(
                jnp.concatenate(
                    heads + [length] + [jnp.zeros((ROWS - step_id - 1, 1), F32)], axis=0
                ),
                (ROWS, LANES),
            )

        return kernel

    v_list = []
    z_list = []
    m_list = []
    head_list = []
    vector = start_vector
    margin_basis = margin_lane = None
    for step_id in range(ITERS):
        arrived = lax.all_to_all(outgoing, "sub", 0, 0)
        outs = [vmem(full), vmem((devices, widest + stat_rows, unknowns))]
        if step_id == 0:
            outs += [vmem((slot_rows, unknowns)), vmem((slot_rows, LANES))]
        made = call(
            smooth_first if step_id == 0 else smooth_later,
            outs,
            arrived,
            vector,
            statistics,
            weights,
            coupling_pairs,
            target,
            selector,
            part_mask,
            name=f"smooth{step_id}",
        )
        smoothed, slots = made[:2]
        if step_id == 0:
            margin_basis, margin_lane = made[2:]
        arrived = lax.all_to_all(slots, ("sub", "coarse"), 0, 0)
        outs = [vmem(full), vmem((ROWS, LANES))]
        if step_id == ITERS - 1:
            outs += [vmem((devices, ROWS, LANES))]
        else:
            outs += [
                vmem(full),
                vmem((slot_rows, unknowns)),
                vmem(full),
                vmem((subs, widest, unknowns)),
                vmem((stat_rows, LANES)),
            ]
        made = call(
            advance(step_id),
            outs,
            arrived,
            smoothed,
            vector,
            coarse_block,
            sub_member,
            member,
            own_row,
            basis,
            margin_basis,
            margin_lane,
            coupling_pairs,
            target,
            selector,
            diagonal_local,
            link_local,
            *v_list,
            *z_list,
            *m_list,
            name=f"advance{step_id}",
        )
        z_list.append(made[0])
        head_list.append(made[1])
        if step_id < ITERS - 1:
            v_list.append(made[2])
            m_list.append(made[3])
            vector, outgoing, statistics = made[4:]
        else:
            slots = made[2]
    arrived = lax.all_to_all(slots, ("sub", "coarse"), 0, 0)

    def finish(arrived_ref, *refs):
        head_refs = refs[:ITERS]
        z_refs = refs[ITERS : 2 * ITERS]
        out_ref = refs[2 * ITERS]
        total = arrived_ref[0]
        for slot in range(1, devices):
            total = total + arrived_ref[slot]
        products = jnp.sum(total, axis=1, keepdims=True)
        heads = [products[i : i + 1] for i in range(ITERS)]
        square = products[ITERS : ITERS + 1]
        remaining = square
        for head in heads:
            remaining = remaining - head * head
        length = jnp.sqrt(jnp.maximum(remaining, square * 1e-12))
        beta = head_refs[0][0:1, 0:1]
        columns = []
        for column_id in range(1, ITERS):
            columns.append([head_refs[column_id][i : i + 1, 0:1] for i in range(column_id + 1)])
        columns.append(heads + [length])
        weights_found = givens_solve(columns, beta)
        result = weights_found[0] * z_refs[0][...]
        for position in range(1, ITERS):
            result = result + weights_found[position] * z_refs[position][...]
        out_ref[...] = result

    (answer,) = call(
        finish, [jax.ShapeDtypeStruct(full, F32)], arrived, *head_list, *z_list, name="finish"
    )
    return answer.reshape(right_side.shape)


def givens_solve(columns, beta):
    steps_count = len(columns)
    cosines = []
    sines = []
    side_terms = [beta] + [jnp.zeros_like(beta) for unused in range(steps_count)]
    triangle = []
    for column_id in range(steps_count):
        column = list(columns[column_id])
        for row_id in range(column_id):
            upper = column[row_id]
            lower = column[row_id + 1]
            column[row_id] = cosines[row_id] * upper + sines[row_id] * lower
            column[row_id + 1] = cosines[row_id] * lower - sines[row_id] * upper
        upper = column[column_id]
        lower = column[column_id + 1]
        radius = jnp.sqrt(upper * upper + lower * lower)
        cosine = upper / radius
        sine_value = lower / radius
        column[column_id] = radius
        cosines.append(cosine)
        sines.append(sine_value)
        side_terms[column_id + 1] = -sine_value * side_terms[column_id]
        side_terms[column_id] = cosine * side_terms[column_id]
        triangle.append(column)
    weights = [None] * steps_count
    for column_id in reversed(range(steps_count)):
        running = side_terms[column_id]
        for later_col in range(column_id + 1, steps_count):
            running = running - triangle[later_col][column_id] * weights[later_col]
        weights[column_id] = running / triangle[column_id][column_id]
    return weights


def solution(mesh):
    placed = (
        P("sub", "coarse", None, None),
        P("sub", "coarse", None, None),
        P("sub", "coarse", None, None),
        P("sub", "coarse", None, None, None),
        P("sub", "coarse", None, None, None),
        P("sub", "coarse", None, None),
        P("coarse", None),
        P("sub", None),
        P("sub", None),
        P("sub", "coarse", None, None),
        P("sub", "coarse", None),
    )
    return jax.shard_map(
        on_device,
        mesh=mesh,
        in_specs=placed,
        out_specs=P("sub", "coarse", None, None),
        check_vma=False,
    )
```

```python
import jax
import jax.numpy as jnp
from jax import lax
from jax.experimental import pallas as pl
from jax.experimental.pallas import tpu as pltpu
from jax.sharding import PartitionSpec as P

BS = 128
BPD = 128
AGG_DEV = 16
ITERS = 4
LANES = 128
ROWS = 8
BF16 = jnp.bfloat16
F32 = jnp.float32


def split(values):
    high = values.astype(BF16)
    low = (values - high.astype(F32)).astype(BF16)
    return high, low


def dot_rows(left, right):
    return lax.dot_general(left, right, (((1,), (1,)), ((), ())), preferred_element_type=F32)


def dot_plain(left, right):
    return lax.dot_general(left, right, (((1,), (0,)), ((), ())), preferred_element_type=F32)


def paired_rows(values):
    high, low = split(values)
    return jnp.concatenate(
        [
            jnp.concatenate([high, high], axis=1),
            jnp.concatenate([low, jnp.zeros_like(low)], axis=1),
        ],
        axis=0,
    )


def pick(selector, values):
    high, low = split(values)
    return dot_plain(selector, jnp.concatenate([high, low], axis=0))


def column_sum(values):
    return jnp.sum(values, axis=0, keepdims=True)


def line_product(values, diagonal, link):
    rows = values.shape[0]
    lanes = values.shape[1]
    row = lax.broadcasted_iota(jnp.int32, values.shape, 0)
    lane = lax.broadcasted_iota(jnp.int32, values.shape, 1)
    next_lane = pltpu.roll(values, lanes - 1, 1)
    next_row = pltpu.roll(next_lane, rows - 1, 0)
    ahead = jnp.where(lane < lanes - 1, next_lane, jnp.where(row < rows - 1, next_row, 0.0))
    scaled = link * values
    last_lane = pltpu.roll(scaled, 1, 1)
    last_row = pltpu.roll(last_lane, 1, 0)
    behind = jnp.where(lane > 0, last_lane, jnp.where(row > 0, last_row, 0.0))
    return diagonal * values - (ahead * link + behind)


def couple(arrived, pair_ref, live):
    rounds = pair_ref.shape[0]
    widest = arrived.shape[0] // rounds
    pieces = []
    for round_id in range(rounds):
        left = paired_rows(arrived[round_id * widest : (round_id + 1) * widest])
        both = dot_rows(left, pair_ref[round_id])
        pieces.append(both[:widest] + both[widest:])
    return jnp.concatenate(pieces, axis=0) * live


def gather_rounds(slots, route, rounds):
    pieces = []
    for round_id in range(rounds):
        total = None
        for sub_id, piece in enumerate(slots):
            at = round_id * len(slots) + sub_id
            term = route[at : at + 1] * piece
            total = term if total is None else total + term
        pieces.append(total)
    return jnp.concatenate(pieces, axis=0)


def spread_rounds(values, route, subs, rounds):
    widest = values.shape[0] // rounds
    slots = []
    for sub_id in range(subs):
        total = None
        for round_id in range(rounds):
            at = round_id * subs + sub_id
            term = route[at : at + 1] * values[round_id * widest : (round_id + 1) * widest]
            total = term if total is None else total + term
        slots.append(total)
    return slots


def vmem(shape, dtype=F32):
    return pltpu.VMEM(shape, dtype)


def call(kernel, outs, *args, name, scalars=0):
    spec = pl.BlockSpec(memory_space=pltpu.VMEM)
    scalar_spec = pl.BlockSpec(memory_space=pltpu.SMEM)
    return pl.pallas_call(
        kernel,
        out_shape=outs,
        in_specs=[scalar_spec] * scalars + [spec] * (len(args) - scalars),
        out_specs=[spec] * len(outs),
        name=name,
        compiler_params=pltpu.CompilerParams(vmem_limit_bytes=16 * 1024 * 1024),
    )(*args)


def on_device(
    right_side,
    diagonal,
    cell_link,
    block_inverse,
    coupling,
    coarse_basis,
    coarse_inverse,
    partner,
    margin_width,
    margin_blocks,
    aggregate,
):
    subs = lax.axis_size("sub")
    parts = lax.axis_size("coarse")
    devices = subs * parts
    block_count = right_side.shape[2]
    unknowns = right_side.shape[3]
    rounds = margin_blocks.shape[2]
    widest = margin_blocks.shape[3]
    aggregates = coarse_inverse.shape[1]
    held_rows = coarse_inverse.shape[0]
    own_aggregates = aggregates // devices
    sub_aggregates = subs * own_aggregates
    sub_chunks = sub_aggregates // LANES
    piece_rows = own_aggregates // parts
    factor = (BS * BPD / AGG_DEV) ** (-0.5)
    coarse_rows = aggregates // LANES
    stat_rows = -(-(coarse_rows + ITERS) // ROWS) * ROWS
    slot_rows = max(widest, stat_rows)
    extra_rows = -(-piece_rows * coarse_rows // ROWS) * ROWS
    margin_rows = rounds * widest
    table_rows = -(-2 * margin_rows // LANES) * LANES
    full = (block_count, unknowns)

    basis = coarse_basis[0, 0]
    diagonal_local = diagonal[0, 0]
    link_local = cell_link[0, 0]
    start_vector = right_side[0, 0]
    inverse_blocks = block_inverse[0, 0]
    blocks = margin_blocks[0, 0]
    member_of = aggregate[0]
    own_bits = own_aggregates.bit_length() - 1
    part_bits = parts.bit_length() - 1
    piece_bits = piece_rows.bit_length() - 1
    lane_bits = LANES.bit_length() - 1
    assert own_aggregates == 1 << own_bits and parts == 1 << part_bits
    assert piece_rows == 1 << piece_bits

    def iota(shape, dim):
        return lax.broadcasted_iota(jnp.int32, shape, dim)

    def hot(condition):
        return jnp.where(condition, 1.0, 0.0).astype(F32)

    def statistics_block(vector, basis_value, member_value, home, dots, rows, count):
        inner = jnp.sum(basis_value * vector, axis=1, keepdims=True)
        line = column_sum(inner * member_value) * factor
        lines = [home[chunk : chunk + 1] * line for chunk in range(count)]
        lines += [column_sum(other * vector) for other in dots]
        if len(lines) < rows:
            lines.append(jnp.zeros((rows - len(lines), LANES), F32))
        return jnp.concatenate(lines, axis=0)

    def begin(
        blocks_ref,
        partner_ref,
        width_ref,
        start_ref,
        basis_ref,
        member_of_ref,
        slot_ref,
        selector_ref,
        route_ref,
        live_ref,
        member_ref,
        home_ref,
    ):
        start = start_ref[...]
        basis_value = basis_ref[...]
        numbers = member_of_ref[...]
        row = iota((widest, LANES), 0)
        lane = iota((widest, LANES), 1)
        tables = []
        for round_id in range(rounds):
            wanted = jnp.zeros((widest, LANES), jnp.int32)
            for position in range(widest):
                wanted = jnp.where(row == position, blocks_ref[round_id, position], wanted)
            tables.append(hot(lane == wanted))
            live_ref[round_id * widest : (round_id + 1) * widest, :] = hot(
                row < width_ref[0, round_id]
            )
            sub_row = iota((subs, LANES), 0)
            route_ref[round_id * subs : (round_id + 1) * subs, :] = hot(
                sub_row == partner_ref[0, round_id]
            )
        table = jnp.concatenate(tables, axis=0)
        table = jnp.concatenate([table, table], axis=1).astype(BF16)
        selector_ref[...] = table
        route = route_ref[...]
        member = hot((numbers & (LANES - 1)) == iota((LANES, block_count), 0)).T
        member_ref[...] = member
        home = hot((numbers >> lane_bits) == iota((coarse_rows, LANES), 0))
        home_ref[...] = home
        own_sub = numbers >> (own_bits + part_bits)
        sub_lane = own_sub * own_aggregates + (numbers & (own_aggregates - 1))
        sub_table = hot((sub_lane & (LANES - 1)) == iota((LANES, block_count), 0)).astype(BF16)
        rows_start = spread_rounds(pick(table, start), route, subs, rounds)
        rows_basis = spread_rounds(pick(table, basis_value), route, subs, rounds)
        rows_lane = spread_rounds(
            dot_rows(table[:, :block_count], sub_table), route, subs, rounds
        )
        statistic = statistics_block(
            start, basis_value, member, home, [start], stat_rows, coarse_rows
        )
        for sub_id in range(subs):
            slot_ref[sub_id, 0:widest, :] = rows_start[sub_id]
            slot_ref[sub_id, widest : widest + stat_rows, :] = statistic
            at = widest + stat_rows
            slot_ref[sub_id, at : at + widest, :] = rows_basis[sub_id]
            slot_ref[sub_id, at + widest : at + 2 * widest, :] = rows_lane[sub_id]

    (outgoing, selector, route, live, member, home) = call(
        begin,
        [
            vmem((subs, 3 * widest + stat_rows, unknowns)),
            vmem((margin_rows, 2 * block_count), BF16),
            vmem((rounds * subs, LANES)),
            vmem((margin_rows, LANES)),
            vmem((block_count, LANES)),
            vmem((coarse_rows, LANES)),
        ],
        blocks,
        partner,
        margin_width,
        start_vector,
        basis,
        member_of,
        name="begin",
        scalars=3,
    )

    def prepare(
        blocks_ref,
        inverse_ref,
        coupling_ref,
        selector_ref,
        member_of_ref,
        weight_ref,
        pair_ref,
        target_ref,
        sub_member_ref,
        part_ref,
        piece_ref,
    ):
        for round_id in range(rounds):
            high, low = split(coupling_ref[round_id])
            pair_ref[round_id, :, 0:unknowns] = high
            pair_ref[round_id, :, unknowns : 2 * unknowns] = low
            for position in range(widest):
                at = round_id * widest + position
                high, low = split(inverse_ref[blocks_ref[round_id, position]])
                rows = slice((at % 2) * unknowns, (at % 2 + 1) * unknowns)
                weight_ref[at // 2, rows, 0:unknowns] = high
                weight_ref[at // 2, rows, unknowns : 2 * unknowns] = low
        table = selector_ref[:, 0:block_count].astype(F32)
        pieces = [table, table]
        if table_rows > 2 * margin_rows:
            pieces.append(jnp.zeros((table_rows - 2 * margin_rows, block_count), F32))
        table = jnp.concatenate(pieces, axis=0)
        target_ref[...] = jnp.concatenate(
            [table[start : start + LANES].T for start in range(0, table_rows, LANES)], axis=1
        ).astype(BF16)
        numbers = member_of_ref[...]
        own_device = numbers >> own_bits
        own_part = own_device & (parts - 1)
        own_sub = own_device >> part_bits
        sub_lane = own_sub * own_aggregates + (numbers & (own_aggregates - 1))
        for chunk in range(sub_chunks):
            sub_member_ref[:, chunk * LANES : (chunk + 1) * LANES] = hot(
                sub_lane == iota((LANES, block_count), 0) + chunk * LANES
            ).T
        part_ref[...] = hot(own_part == iota((ROWS, LANES), 0))
        order = iota((parts * piece_rows, LANES), 0)
        first = (
            ((own_sub >> part_bits) << (part_bits + own_bits))
            + ((order >> piece_bits) << own_bits)
            + ((own_sub & (parts - 1)) << piece_bits)
            + (order & (piece_rows - 1))
        )
        for chunk in range(held_rows // LANES):
            at_row = hot(first == iota((parts * piece_rows, LANES), 1) + chunk * LANES)
            at_row = at_row.astype(BF16)
            piece_ref[:, chunk * LANES : (chunk + 1) * LANES] = at_row
            piece_ref[:, held_rows + chunk * LANES : held_rows + (chunk + 1) * LANES] = at_row

    weights, pairs, target, sub_member, part_table, piece_table = call(
        prepare,
        [
            vmem((margin_rows // 2, 2 * unknowns, 2 * unknowns), BF16),
            vmem((rounds, unknowns, 2 * unknowns), BF16),
            vmem((block_count, table_rows), BF16),
            vmem((block_count, sub_aggregates)),
            vmem((ROWS, LANES)),
            vmem((parts * piece_rows, 2 * held_rows), BF16),
        ],
        blocks,
        inverse_blocks,
        coupling[0, 0],
        selector,
        member_of,
        name="prepare",
        scalars=1,
    )

    def put(target_value, values):
        high, low = split(values)
        pieces = [high, low]
        if table_rows > 2 * margin_rows:
            pieces.append(jnp.zeros((table_rows - 2 * margin_rows, unknowns), BF16))
        return dot_plain(target_value, jnp.concatenate(pieces, axis=0))

    def solve(vector_ref, inverse_ref, out_ref):
        def step(group, carry):
            rows = pl.ds(pl.multiple_of(group * ROWS, ROWS), ROWS)
            values = vector_ref[rows, :]
            lines = []
            for offset in range(ROWS):
                scaled = inverse_ref[group * ROWS + offset] * values[offset : offset + 1, :]
                lines.append(jnp.sum(scaled, axis=1)[None, :])
            out_ref[rows, :] = jnp.concatenate(lines, axis=0)
            return carry

        lax.fori_loop(0, block_count // ROWS, step, 0)

    def smooth(first):
        def kernel(
            arrived_ref,
            solved_ref,
            weight_ref,
            pair_ref,
            target_ref,
            selector_ref,
            route_ref,
            live_ref,
            part_ref,
            stat_ref,
            *refs,
        ):
            if first:
                coarse_ref, piece_ref, out_ref, slot_ref, sum_ref, basis_rows_ref, lane_rows_ref = refs
            else:
                out_ref, slot_ref, sum_ref = refs
            route = route_ref[...]
            arrived = gather_rounds(
                [arrived_ref[sub_id, 0:widest, :] for sub_id in range(subs)], route, rounds
            )
            mapped = couple(arrived, pair_ref, live_ref[...])
            row = iota((widest, unknowns), 0)
            pieces = []
            for round_id in range(rounds):
                left = paired_rows(mapped[round_id * widest : (round_id + 1) * widest])
                total = jnp.zeros((widest, unknowns), F32)
                for offset in range(widest // 2):
                    both = dot_rows(left, weight_ref[round_id * (widest // 2) + offset])
                    both = both[:widest] + both[widest:]
                    total = jnp.where(row == 2 * offset, both[:, :unknowns], total)
                    total = jnp.where(row == 2 * offset + 1, both[:, unknowns:], total)
                pieces.append(total)
            out = solved_ref[...] + put(target_ref[...], jnp.concatenate(pieces, axis=0))
            out_ref[...] = out
            slots = spread_rounds(pick(selector_ref[...], out), route, subs, rounds)
            statistic = stat_ref[0, widest : widest + stat_rows, :]
            if stat_rows < slot_rows:
                statistic = jnp.concatenate(
                    [statistic, jnp.zeros((slot_rows - stat_rows, LANES), F32)], axis=0
                )
            if first:
                passed = pick(piece_ref[...], coarse_ref[...])
            for sub_id in range(subs):
                piece = slots[sub_id]
                if widest < slot_rows:
                    piece = jnp.concatenate(
                        [piece, jnp.zeros((slot_rows - widest, unknowns), F32)], axis=0
                    )
                for part_id in range(parts):
                    slot = sub_id * parts + part_id
                    slot_ref[slot, 0:slot_rows, :] = jnp.where(
                        part_ref[part_id : part_id + 1, :] > 0.5, piece, statistic
                    )
                    if first:
                        for chunk in range(coarse_rows):
                            at = slot_rows + chunk * piece_rows
                            slot_ref[slot, at : at + piece_rows, :] = passed[
                                part_id * piece_rows : (part_id + 1) * piece_rows,
                                chunk * LANES : (chunk + 1) * LANES,
                            ]
            total = arrived_ref[0, widest : widest + stat_rows, :]
            for sub_id in range(1, subs):
                total = total + arrived_ref[sub_id, widest : widest + stat_rows, :]
            sum_ref[...] = total
            if first:
                at = widest + stat_rows
                basis_rows_ref[...] = gather_rounds(
                    [arrived_ref[sub_id, at : at + widest, :] for sub_id in range(subs)],
                    route,
                    rounds,
                )
                at = at + widest
                for chunk in range(sub_chunks):
                    lo = chunk * subs // sub_chunks
                    hi = (chunk + 1) * subs // sub_chunks
                    lane_rows_ref[chunk] = gather_rounds(
                        [
                            arrived_ref[sub_id, at : at + widest, :]
                            if lo <= sub_id < hi
                            else jnp.zeros((widest, LANES), F32)
                            for sub_id in range(subs)
                        ],
                        route,
                        rounds,
                    )

        return kernel

    def advance(step_id):
        first = step_id == 0
        last = step_id == ITERS - 1

        def kernel(*refs):
            (
                arrived_ref,
                sum_ref,
                smoothed_ref,
                vector_ref,
                sub_member_ref,
                member_ref,
                home_ref,
                basis_ref,
                basis_rows_ref,
                lane_rows_ref,
                pair_ref,
                target_ref,
                selector_ref,
                route_ref,
                live_ref,
                part_ref,
                diagonal_ref,
                link_ref,
            ) = refs[:18]
            refs = refs[18:]
            v_refs = refs[:step_id]
            z_refs = refs[step_id : 2 * step_id]
            m_refs = refs[2 * step_id : 3 * step_id]
            outs = list(refs[3 * step_id :])
            if first:
                coarse_ref = outs.pop()
                for sub_id in range(subs):
                    for part_id in range(parts):
                        row = (part_id * subs + sub_id) * piece_rows
                        for chunk in range(coarse_rows):
                            at = slot_rows + chunk * piece_rows
                            coarse_ref[
                                row : row + piece_rows, chunk * LANES : (chunk + 1) * LANES
                            ] = arrived_ref[sub_id * parts + part_id, at : at + piece_rows, :]
            else:
                coarse_ref = outs.pop(0)
            total = sum_ref[...]
            pieces = []
            for sub_id in range(subs):
                piece = jnp.zeros((widest, unknowns), F32)
                for part_id in range(parts):
                    slot = sub_id * parts + part_id
                    own = part_ref[part_id : part_id + 1, :] > 0.5
                    total = total + jnp.where(own, 0.0, arrived_ref[slot, 0:stat_rows, :])
                    piece = piece + jnp.where(own, arrived_ref[slot, 0:widest, :], 0.0)
                pieces.append(piece)
            products = jnp.sum(total[coarse_rows : coarse_rows + step_id + 1], axis=1, keepdims=True)
            heads = [products[i : i + 1] for i in range(step_id)]
            square = products[step_id : step_id + 1]
            remaining = square
            for head in heads:
                remaining = remaining - head * head
            length = jnp.sqrt(jnp.maximum(remaining, square * 1e-12))
            scale = 1.0 / length
            gathered = coarse_ref[:, 0:LANES] * total[0:1]
            for chunk in range(1, coarse_rows):
                gathered = gathered + (
                    coarse_ref[:, chunk * LANES : (chunk + 1) * LANES] * total[chunk : chunk + 1]
                )
            column = jnp.sum(gathered, axis=1, keepdims=True)
            same = iota((LANES, LANES), 0) == iota((LANES, LANES), 1)
            lines = [
                column_sum(jnp.where(same, column[start : start + LANES], 0.0))
                for start in range(0, sub_aggregates, LANES)
            ]
            own_coarse = sub_member_ref[:, 0:LANES] * lines[0]
            row_coarse = lane_rows_ref[0] * lines[0]
            for chunk in range(1, sub_chunks):
                own_coarse = own_coarse + (
                    sub_member_ref[:, chunk * LANES : (chunk + 1) * LANES] * lines[chunk]
                )
                row_coarse = row_coarse + lane_rows_ref[chunk] * lines[chunk]
            own_coarse = jnp.sum(own_coarse, axis=1, keepdims=True)
            row_coarse = jnp.sum(row_coarse, axis=1, keepdims=True)
            basis_value = basis_ref[...]
            direction = smoothed_ref[...] + own_coarse * basis_value
            for head, z_ref in zip(heads, z_refs):
                direction = direction - head * z_ref[...]
            direction = direction * scale
            route = route_ref[...]
            rows = gather_rounds(pieces, route, rounds) + row_coarse * basis_rows_ref[...]
            for head, m_ref in zip(heads, m_refs):
                rows = rows - head * m_ref[...]
            rows = rows * scale
            vector = vector_ref[...]
            for head, v_ref in zip(heads, v_refs):
                vector = vector - head * v_ref[...]
            vector = vector * scale
            product = line_product(direction, diagonal_ref[...], link_ref[...]) - put(
                target_ref[...], couple(rows, pair_ref, live_ref[...])
            )
            against = [v_ref[...] for v_ref in v_refs] + [vector, product]
            if last:
                direction_ref, head_ref, slot_ref = outs
                block = statistics_block(
                    product, basis_value, member_ref[...], home_ref[...], against, ROWS, 0
                )
                for slot in range(devices):
                    slot_ref[slot] = block
            else:
                direction_ref, head_ref, new_v_ref, margin_ref, product_ref, slot_ref = outs
                new_v_ref[...] = vector
                margin_ref[...] = rows
                product_ref[...] = product
                slots = spread_rounds(pick(selector_ref[...], product), route, subs, rounds)
                block = statistics_block(
                    product,
                    basis_value,
                    member_ref[...],
                    home_ref[...],
                    against,
                    stat_rows,
                    coarse_rows,
                )
                for sub_id in range(subs):
                    slot_ref[sub_id, 0:widest, :] = slots[sub_id]
                    slot_ref[sub_id, widest:, :] = block
            direction_ref[...] = direction
            head_ref[...] = jnp.broadcast_to(
                jnp.concatenate(
                    heads + [length] + [jnp.zeros((ROWS - step_id - 1, 1), F32)], axis=0
                ),
                (ROWS, LANES),
            )

        return kernel

    v_list = []
    z_list = []
    m_list = []
    head_list = []
    vector = start_vector
    basis_rows = lane_rows = coarse_block = None
    for step_id in range(ITERS):
        first = step_id == 0
        last = step_id == ITERS - 1
        arrived = lax.all_to_all(outgoing, "sub", 0, 0)
        (solved,) = call(solve, [vmem(full)], vector, inverse_blocks, name=f"solve{step_id}")
        outs = [
            vmem(full),
            vmem((devices, slot_rows + (extra_rows if first else 0), unknowns)),
            vmem((stat_rows, LANES)),
        ]
        if first:
            outs += [vmem((margin_rows, unknowns)), vmem((sub_chunks, margin_rows, LANES))]
        made = call(
            smooth(first),
            outs,
            arrived,
            solved,
            weights,
            pairs,
            target,
            selector,
            route,
            live,
            part_table,
            outgoing,
            *([coarse_inverse, piece_table] if first else []),
            name=f"smooth{step_id}",
        )
        smoothed, slots, sums = made[:3]
        if first:
            basis_rows, lane_rows = made[3:]
        arrived = lax.all_to_all(slots, ("sub", "coarse"), 0, 0)
        outs = [vmem(full), vmem((ROWS, LANES))]
        if last:
            outs += [vmem((devices, ROWS, LANES))]
        else:
            outs += [
                vmem(full),
                vmem((margin_rows, unknowns)),
                vmem(full),
                vmem((subs, widest + stat_rows, unknowns)),
            ]
        if first:
            outs += [vmem((sub_aggregates, aggregates))]
        made = call(
            advance(step_id),
            outs,
            arrived,
            sums,
            smoothed,
            vector,
            sub_member,
            member,
            home,
            basis,
            basis_rows,
            lane_rows,
            pairs,
            target,
            selector,
            route,
            live,
            part_table,
            diagonal_local,
            link_local,
            *v_list,
            *z_list,
            *m_list,
            *([] if first else [coarse_block]),
            name=f"advance{step_id}",
        )
        if first:
            *made, coarse_block = made
        z_list.append(made[0])
        head_list.append(made[1])
        if last:
            slots = made[2]
        else:
            v_list.append(made[2])
            m_list.append(made[3])
            vector, outgoing = made[4:]
    arrived = lax.all_to_all(slots, ("sub", "coarse"), 0, 0)

    def finish(arrived_ref, *refs):
        head_refs = refs[:ITERS]
        z_refs = refs[ITERS : 2 * ITERS]
        out_ref = refs[2 * ITERS]
        total = arrived_ref[0]
        for slot in range(1, devices):
            total = total + arrived_ref[slot]
        products = jnp.sum(total, axis=1, keepdims=True)
        heads = [products[i : i + 1] for i in range(ITERS)]
        square = products[ITERS : ITERS + 1]
        remaining = square
        for head in heads:
            remaining = remaining - head * head
        length = jnp.sqrt(jnp.maximum(remaining, square * 1e-12))
        beta = head_refs[0][0:1, 0:1]
        columns = []
        for column_id in range(1, ITERS):
            columns.append([head_refs[column_id][i : i + 1, 0:1] for i in range(column_id + 1)])
        columns.append(heads + [length])
        weights_found = givens_solve(columns, beta)
        result = weights_found[0] * z_refs[0][...]
        for position in range(1, ITERS):
            result = result + weights_found[position] * z_refs[position][...]
        out_ref[...] = result

    (answer,) = call(
        finish, [jax.ShapeDtypeStruct(full, F32)], arrived, *head_list, *z_list, name="finish"
    )
    return answer.reshape(right_side.shape)


def givens_solve(columns, beta):
    steps_count = len(columns)
    cosines = []
    sines = []
    side_terms = [beta] + [jnp.zeros_like(beta) for unused in range(steps_count)]
    triangle = []
    for column_id in range(steps_count):
        column = list(columns[column_id])
        for row_id in range(column_id):
            upper = column[row_id]
            lower = column[row_id + 1]
            column[row_id] = cosines[row_id] * upper + sines[row_id] * lower
            column[row_id + 1] = cosines[row_id] * lower - sines[row_id] * upper
        upper = column[column_id]
        lower = column[column_id + 1]
        radius = jnp.sqrt(upper * upper + lower * lower)
        cosine = upper / radius
        sine_value = lower / radius
        column[column_id] = radius
        cosines.append(cosine)
        sines.append(sine_value)
        side_terms[column_id + 1] = -sine_value * side_terms[column_id]
        side_terms[column_id] = cosine * side_terms[column_id]
        triangle.append(column)
    weights = [None] * steps_count
    for column_id in reversed(range(steps_count)):
        running = side_terms[column_id]
        for later_col in range(column_id + 1, steps_count):
            running = running - triangle[later_col][column_id] * weights[later_col]
        weights[column_id] = running / triangle[column_id][column_id]
    return weights


def solution(mesh):
    placed = (
        P("sub", "coarse", None, None),
        P("sub", "coarse", None, None),
        P("sub", "coarse", None, None),
        P("sub", "coarse", None, None, None),
        P("sub", "coarse", None, None, None),
        P("sub", "coarse", None, None),
        P("coarse", None),
        P("sub", None),
        P("sub", None),
        P("sub", "coarse", None, None),
        P("sub", "coarse", None),
    )
    return jax.shard_map(
        on_device,
        mesh=mesh,
        in_specs=placed,
        out_specs=P("sub", "coarse", None, None),
        check_vma=False,
    )
```

```python
import jax
import jax.numpy as jnp
from jax import lax
from jax.experimental import pallas as pl
from jax.experimental.pallas import tpu as pltpu
from jax.sharding import PartitionSpec as P

BS = 128
BPD = 128
AGG_DEV = 16
ITERS = 4
LANES = 128
ROWS = 8
BF16 = jnp.bfloat16
F32 = jnp.float32


def split(values):
    high = values.astype(BF16)
    low = (values - high.astype(F32)).astype(BF16)
    return high, low


def dot_rows(left, right):
    return lax.dot_general(left, right, (((1,), (1,)), ((), ())), preferred_element_type=F32)


def dot_plain(left, right):
    return lax.dot_general(left, right, (((1,), (0,)), ((), ())), preferred_element_type=F32)


def paired_rows(values):
    high, low = split(values)
    return jnp.concatenate(
        [
            jnp.concatenate([high, high], axis=1),
            jnp.concatenate([low, jnp.zeros_like(low)], axis=1),
        ],
        axis=0,
    )


def pick(selector, values):
    high, low = split(values)
    return dot_plain(selector, jnp.concatenate([high, low], axis=0))


def column_sum(values):
    return jnp.sum(values, axis=0, keepdims=True)


def line_product(values, diagonal, link):
    rows = values.shape[0]
    lanes = values.shape[1]
    row = lax.broadcasted_iota(jnp.int32, values.shape, 0)
    lane = lax.broadcasted_iota(jnp.int32, values.shape, 1)
    next_lane = pltpu.roll(values, lanes - 1, 1)
    next_row = pltpu.roll(next_lane, rows - 1, 0)
    ahead = jnp.where(lane < lanes - 1, next_lane, jnp.where(row < rows - 1, next_row, 0.0))
    scaled = link * values
    last_lane = pltpu.roll(scaled, 1, 1)
    last_row = pltpu.roll(last_lane, 1, 0)
    behind = jnp.where(lane > 0, last_lane, jnp.where(row > 0, last_row, 0.0))
    return diagonal * values - (ahead * link + behind)


def couple(arrived, pair_ref, live):
    rounds = pair_ref.shape[0]
    widest = arrived.shape[0] // rounds
    pieces = []
    for round_id in range(rounds):
        left = paired_rows(arrived[round_id * widest : (round_id + 1) * widest])
        both = dot_rows(left, pair_ref[round_id])
        pieces.append(both[:widest] + both[widest:])
    return jnp.concatenate(pieces, axis=0) * live


def gather_rounds(slots, route, rounds):
    pieces = []
    for round_id in range(rounds):
        total = None
        for sub_id, piece in enumerate(slots):
            at = round_id * len(slots) + sub_id
            term = route[at : at + 1] * piece
            total = term if total is None else total + term
        pieces.append(total)
    return jnp.concatenate(pieces, axis=0)


def spread_rounds(values, route, subs, rounds):
    widest = values.shape[0] // rounds
    slots = []
    for sub_id in range(subs):
        total = None
        for round_id in range(rounds):
            at = round_id * subs + sub_id
            term = route[at : at + 1] * values[round_id * widest : (round_id + 1) * widest]
            total = term if total is None else total + term
        slots.append(total)
    return slots


def vmem(shape, dtype=F32):
    return pltpu.VMEM(shape, dtype)


def call(kernel, outs, *args, name, places="", out_places="", aliases=None, scratch=()):
    places = places + "v" * (len(args) - len(places))
    spaces = {"s": pltpu.SMEM, "h": pltpu.HBM, "v": pltpu.VMEM}
    return pl.pallas_call(
        kernel,
        out_shape=outs,
        in_specs=[pl.BlockSpec(memory_space=spaces[place]) for place in places],
        out_specs=[
            pl.BlockSpec(memory_space=pltpu.HBM if place == "h" else pltpu.VMEM)
            for place in (out_places or "v" * len(outs))
        ],
        input_output_aliases=aliases or {},
        scratch_shapes=list(scratch),
        name=name,
        compiler_params=pltpu.CompilerParams(vmem_limit_bytes=16 * 1024 * 1024),
    )(
        *[
            pltpu.with_memory_space_constraint(
                arg, pltpu.VMEM if place == "v" else pltpu.HBM
            )
            for arg, place in zip(args, places)
        ]
    )


def on_device(
    right_side,
    diagonal,
    cell_link,
    block_inverse,
    coupling,
    coarse_basis,
    coarse_inverse,
    partner,
    margin_width,
    margin_blocks,
    aggregate,
):
    subs = lax.axis_size("sub")
    parts = lax.axis_size("coarse")
    devices = subs * parts
    block_count = right_side.shape[2]
    unknowns = right_side.shape[3]
    rounds = margin_blocks.shape[2]
    widest = margin_blocks.shape[3]
    aggregates = coarse_inverse.shape[1]
    own_aggregates = aggregates // devices
    sub_aggregates = subs * own_aggregates
    sub_chunks = sub_aggregates // LANES
    sub_span = subs // parts
    chunk_rows = sub_span * own_aggregates
    factor = (BS * BPD / AGG_DEV) ** (-0.5)
    coarse_rows = aggregates // LANES
    stat_rows = -(-(coarse_rows + ITERS) // ROWS) * ROWS
    slot_rows = max(widest, stat_rows)
    margin_rows = rounds * widest
    table_rows = -(-2 * margin_rows // LANES) * LANES
    full = (block_count, unknowns)

    v_at = 0
    m_at = v_at + (ITERS - 1) * block_count
    head_at = m_at + (ITERS - 1) * margin_rows
    state_rows = head_at + ITERS * ROWS
    blocks = margin_blocks[0, 0]
    member_of = aggregate[0]
    own_bits = own_aggregates.bit_length() - 1
    part_bits = parts.bit_length() - 1
    span_bits = sub_span.bit_length() - 1
    lane_bits = LANES.bit_length() - 1
    assert own_aggregates == 1 << own_bits and parts == 1 << part_bits
    assert sub_span == 1 << span_bits and sub_span * parts == subs

    def iota(shape, dim):
        return lax.broadcasted_iota(jnp.int32, shape, dim)

    def hot(condition):
        return jnp.where(condition, 1.0, 0.0).astype(F32)

    def coarse_lane(numbers):
        own_device = numbers >> own_bits
        own_part = own_device & (parts - 1)
        own_sub = own_device >> part_bits
        turn = (own_part - (own_sub >> span_bits)) & (parts - 1)
        return (
            turn * chunk_rows
            + (own_sub & (sub_span - 1)) * own_aggregates
            + (numbers & (own_aggregates - 1))
        )

    def statistics_block(vector, basis_value, member_value, home, dots, rows, count):
        lines = []
        if count:
            inner = jnp.sum(basis_value * vector, axis=1, keepdims=True)
            line = column_sum(inner * member_value) * factor
            lines = [home[chunk : chunk + 1] * line for chunk in range(count)]
        lines += [column_sum(other * vector) for other in dots]
        if len(lines) < rows:
            lines.append(jnp.zeros((rows - len(lines), LANES), F32))
        return jnp.concatenate(lines, axis=0)

    def begin(
        blocks_ref,
        partner_ref,
        width_ref,
        number_ref,
        start_hbm,
        basis_hbm,
        member_of_hbm,
        coarse_hbm,
        *refs,
    ):
        (
            slot_ref,
            selector_ref,
            route_ref,
            live_ref,
            member_ref,
            home_ref,
            start_ref,
            basis_ref,
            member_of_ref,
        ) = refs[:9]
        chunk_refs = refs[9 : 9 + parts]
        semaphores = refs[9 + parts]
        copies = [
            pltpu.make_async_copy(source, to, semaphores.at[position])
            for position, (source, to) in enumerate(
                [(start_hbm, start_ref), (basis_hbm, basis_ref), (member_of_hbm, member_of_ref)]
            )
        ]
        own_part = (number_ref[0, 0] >> own_bits) & (parts - 1)
        chunk_copies = []
        for turn, chunk_ref in enumerate(chunk_refs):
            to_part = (own_part + turn) & (parts - 1)
            for span in range(sub_span):
                first = pl.multiple_of((span * parts + to_part) * own_aggregates, own_aggregates)
                chunk_copies.append(
                    pltpu.make_async_copy(
                        coarse_hbm.at[pl.ds(first, own_aggregates), :],
                        chunk_ref.at[pl.ds(span * own_aggregates, own_aggregates), :],
                        semaphores.at[3 + turn * sub_span + span],
                    )
                )
        for copy in copies + chunk_copies:
            copy.start()
        row = iota((widest, LANES), 0)
        lane = iota((widest, LANES), 1)
        tables = []
        for round_id in range(rounds):
            wanted = jnp.zeros((widest, LANES), jnp.int32)
            for position in range(widest):
                wanted = jnp.where(row == position, blocks_ref[round_id, position], wanted)
            tables.append(hot(lane == wanted))
            live_ref[round_id * widest : (round_id + 1) * widest, :] = hot(
                row < width_ref[0, round_id]
            )
            sub_row = iota((subs, LANES), 0)
            route_ref[round_id * subs : (round_id + 1) * subs, :] = hot(
                sub_row == partner_ref[0, round_id]
            )
        for copy in copies:
            copy.wait()
        start = start_ref[...]
        basis_value = basis_ref[...]
        numbers = member_of_ref[...]
        table = jnp.concatenate(tables, axis=0)
        table = jnp.concatenate([table, table], axis=1).astype(BF16)
        selector_ref[...] = table
        route = route_ref[...]
        member = hot((numbers & (LANES - 1)) == iota((LANES, block_count), 0)).T
        member_ref[...] = member.astype(BF16)
        home = hot((numbers >> lane_bits) == iota((coarse_rows, LANES), 0))
        home_ref[...] = home
        own_lane = coarse_lane(numbers)
        rows_start = spread_rounds(pick(table, start), route, subs, rounds)
        rows_basis = spread_rounds(pick(table, basis_value), route, subs, rounds)
        rows_lane = []
        for chunk in range(sub_chunks):
            lane_table = hot(own_lane == iota((LANES, block_count), 0) + chunk * LANES)
            rows_lane.append(
                spread_rounds(
                    dot_rows(table[:, :block_count], lane_table.astype(BF16)), route, subs, rounds
                )
            )
        statistic = statistics_block(
            start, basis_value, member, home, [start], stat_rows, coarse_rows
        )
        for sub_id in range(subs):
            slot_ref[sub_id, 0:widest, :] = rows_start[sub_id]
            slot_ref[sub_id, widest : widest + stat_rows, :] = statistic
            at = widest + stat_rows
            slot_ref[sub_id, at : at + widest, :] = rows_basis[sub_id]
            for chunk in range(sub_chunks):
                at = at + widest
                slot_ref[sub_id, at : at + widest, :] = rows_lane[chunk][sub_id]
        for copy in chunk_copies:
            copy.wait()

    (
        outgoing,
        selector,
        route,
        live,
        member,
        home,
        start_vector,
        basis,
        member_of,
        *coarse_chunks,
    ) = call(
        begin,
        [
            vmem((subs, (2 + sub_chunks) * widest + stat_rows, unknowns)),
            vmem((margin_rows, 2 * block_count), BF16),
            vmem((rounds * subs, LANES)),
            vmem((margin_rows, LANES)),
            vmem((block_count, LANES), BF16),
            vmem((coarse_rows, LANES)),
            vmem(full),
            vmem(full),
            vmem((1, block_count), jnp.int32),
        ]
        + [vmem((chunk_rows, aggregates))] * parts,
        blocks,
        partner,
        margin_width,
        aggregate[0],
        right_side[0, 0],
        coarse_basis[0, 0],
        aggregate[0],
        coarse_inverse,
        name="begin",
        places="sssshhhh",
        scratch=[pltpu.SemaphoreType.DMA((3 + parts * sub_span,))],
    )
    for turn in range(1, parts):
        coarse_chunks[turn] = lax.ppermute(
            coarse_chunks[turn], "coarse", [(i, (i + turn) % parts) for i in range(parts)]
        )

    def solve_group(group, vector_ref, inverse_ref, out_ref):
        rows = pl.ds(pl.multiple_of(group * ROWS, ROWS), ROWS)
        values = vector_ref[rows, :]
        lines = []
        for offset in range(ROWS):
            scaled = inverse_ref[group * ROWS + offset] * values[offset : offset + 1, :]
            lines.append(jnp.sum(scaled, axis=1)[None, :])
        out_ref[rows, :] = jnp.concatenate(lines, axis=0)

    def solve(vector_ref, inverse_hbm, out_ref, inverse_ref, semaphores):
        def group_copy(group):
            rows = pl.ds(group * ROWS, ROWS)
            return pltpu.make_async_copy(
                inverse_hbm.at[rows], inverse_ref.at[rows], semaphores.at[group]
            )

        for group in range(block_count // ROWS):
            group_copy(group).start()

        def step(group, carry):
            group_copy(group).wait()
            solve_group(group, vector_ref, inverse_ref, out_ref)
            return carry

        lax.fori_loop(0, block_count // ROWS, step, 0)

    def prepare(
        blocks_ref,
        inverse_hbm,
        coupling_hbm,
        diagonal_hbm,
        link_hbm,
        selector_ref,
        member_of_ref,
        weight_ref,
        pair_ref,
        target_ref,
        sub_member_ref,
        part_ref,
        diagonal_ref,
        link_ref,
        inverse_ref,
        coupling_ref,
        semaphores,
        block_semaphores,
    ):
        copies = [
            pltpu.make_async_copy(source, to, semaphores.at[position])
            for position, (source, to) in enumerate(
                [
                    (coupling_hbm, coupling_ref),
                    (diagonal_hbm, diagonal_ref),
                    (link_hbm, link_ref),
                ]
            )
        ]
        block_copies = [
            pltpu.make_async_copy(
                inverse_hbm.at[blocks_ref[at // widest, at % widest]],
                inverse_ref.at[at],
                block_semaphores.at[at],
            )
            for at in range(margin_rows)
        ]
        for copy in copies + block_copies:
            copy.start()
        table = selector_ref[:, 0:block_count].astype(F32)
        pieces = [table, table]
        if table_rows > 2 * margin_rows:
            pieces.append(jnp.zeros((table_rows - 2 * margin_rows, block_count), F32))
        table = jnp.concatenate(pieces, axis=0)
        target_ref[...] = jnp.concatenate(
            [table[start : start + LANES].T for start in range(0, table_rows, LANES)], axis=1
        ).astype(BF16)
        numbers = member_of_ref[...]
        own_lane = coarse_lane(numbers)
        for chunk in range(sub_chunks):
            sub_member_ref[:, chunk * LANES : (chunk + 1) * LANES] = hot(
                own_lane == iota((LANES, block_count), 0) + chunk * LANES
            ).T.astype(BF16)
        part_ref[...] = hot(
            ((numbers >> own_bits) & (parts - 1)) == iota((ROWS, LANES), 0)
        )
        copies[0].wait()
        for round_id in range(rounds):
            high, low = split(coupling_ref[round_id])
            pair_ref[round_id, :, 0:unknowns] = high
            pair_ref[round_id, :, unknowns : 2 * unknowns] = low
        for at in range(margin_rows):
            block_copies[at].wait()
            high, low = split(inverse_ref[at])
            rows = slice((at % 2) * unknowns, (at % 2 + 1) * unknowns)
            weight_ref[at // 2, rows, 0:unknowns] = high
            weight_ref[at // 2, rows, unknowns : 2 * unknowns] = low
        for copy in copies[1:]:
            copy.wait()

    inverse_blocks = block_inverse[0, 0]
    weights, pairs, target, sub_member, part_table, diagonal_local, link_local = call(
        prepare,
        [
            vmem((margin_rows // 2, 2 * unknowns, 2 * unknowns), BF16),
            vmem((rounds, unknowns, 2 * unknowns), BF16),
            vmem((block_count, table_rows), BF16),
            vmem((block_count, sub_aggregates), BF16),
            vmem((ROWS, LANES)),
            vmem(full),
            vmem(full),
        ],
        blocks,
        inverse_blocks,
        coupling[0, 0],
        diagonal[0, 0],
        cell_link[0, 0],
        selector,
        member_of,
        name="prepare",
        places="shhhh",
        scratch=[
            vmem((margin_rows, unknowns, unknowns)),
            vmem((rounds, unknowns, unknowns)),
            pltpu.SemaphoreType.DMA((3,)),
            pltpu.SemaphoreType.DMA((margin_rows,)),
        ],
    )

    def put(target_value, values):
        high, low = split(values)
        pieces = [high, low]
        if table_rows > 2 * margin_rows:
            pieces.append(jnp.zeros((table_rows - 2 * margin_rows, unknowns), BF16))
        return dot_plain(target_value, jnp.concatenate(pieces, axis=0))

    def smooth(first):
        def kernel(
            arrived_ref,
            solved_ref,
            weight_ref,
            pair_ref,
            target_ref,
            selector_ref,
            route_ref,
            live_ref,
            part_ref,
            stat_ref,
            *refs,
        ):
            if first:
                out_ref, slot_ref, sum_ref, basis_rows_ref, lane_rows_ref = refs
            else:
                unused_in, out_ref, slot_ref, sum_ref, unused_out = refs
            route = route_ref[...]
            arrived = gather_rounds(
                [arrived_ref[sub_id, 0:widest, :] for sub_id in range(subs)], route, rounds
            )
            mapped = couple(arrived, pair_ref, live_ref[...])
            row = iota((widest, unknowns), 0)
            pieces = []
            for round_id in range(rounds):
                left = paired_rows(mapped[round_id * widest : (round_id + 1) * widest])
                total = jnp.zeros((widest, unknowns), F32)
                for offset in range(widest // 2):
                    both = dot_rows(left, weight_ref[round_id * (widest // 2) + offset])
                    both = both[:widest] + both[widest:]
                    total = jnp.where(row == 2 * offset, both[:, :unknowns], total)
                    total = jnp.where(row == 2 * offset + 1, both[:, unknowns:], total)
                pieces.append(total)
            out = solved_ref[...] + put(target_ref[...], jnp.concatenate(pieces, axis=0))
            out_ref[...] = out
            slots = spread_rounds(pick(selector_ref[...], out), route, subs, rounds)
            statistic = stat_ref[0, widest : widest + stat_rows, :]
            if stat_rows < slot_rows:
                statistic = jnp.concatenate(
                    [statistic, jnp.zeros((slot_rows - stat_rows, LANES), F32)], axis=0
                )
            for sub_id in range(subs):
                piece = slots[sub_id]
                if widest < slot_rows:
                    piece = jnp.concatenate(
                        [piece, jnp.zeros((slot_rows - widest, unknowns), F32)], axis=0
                    )
                for part_id in range(parts):
                    slot = sub_id * parts + part_id
                    slot_ref[slot, 0:slot_rows, :] = jnp.where(
                        part_ref[part_id : part_id + 1, :] > 0.5, piece, statistic
                    )
            total = arrived_ref[0, widest : widest + stat_rows, :]
            for sub_id in range(1, subs):
                total = total + arrived_ref[sub_id, widest : widest + stat_rows, :]
            sum_ref[...] = total
            if first:
                at = widest + stat_rows
                basis_rows_ref[...] = gather_rounds(
                    [arrived_ref[sub_id, at : at + widest, :] for sub_id in range(subs)],
                    route,
                    rounds,
                )
                for chunk in range(sub_chunks):
                    at = at + widest
                    lane_rows_ref[chunk] = gather_rounds(
                        [arrived_ref[sub_id, at : at + widest, :] for sub_id in range(subs)],
                        route,
                        rounds,
                    )

        return kernel

    def advance(step_id):
        first = step_id == 0
        last = step_id == ITERS - 1

        def kernel(*refs):
            (
                arrived_ref,
                sum_ref,
                smoothed_ref,
                vector_ref,
                sub_member_ref,
                member_ref,
                home_ref,
                basis_ref,
                basis_rows_ref,
                lane_rows_ref,
                pair_ref,
                target_ref,
                selector_ref,
                route_ref,
                live_ref,
                part_ref,
                diagonal_ref,
                link_ref,
            ) = refs[:18]
            coarse_refs = refs[18 : 18 + parts]
            refs = refs[18 + parts :]
            z_hbms = refs[:step_id]
            if not first:
                state_in = refs[step_id]
                refs = refs[step_id + 1 :]
            *outs, z_hbm, state_ref, z_ref, semaphores = refs
            z_copies = [
                pltpu.make_async_copy(source, z_ref.at[number], semaphores.at[number])
                for number, source in enumerate(z_hbms)
            ]
            for copy in z_copies:
                copy.start()

            def held(at, number, rows):
                return state_in[at + number * rows : at + (number + 1) * rows, :]

            def keep(at, number, values):
                rows = values.shape[0]
                state_ref[at + number * rows : at + (number + 1) * rows, :] = values

            total = sum_ref[...]
            pieces = []
            for sub_id in range(subs):
                piece = jnp.zeros((widest, unknowns), F32)
                for part_id in range(parts):
                    slot = sub_id * parts + part_id
                    own = part_ref[part_id : part_id + 1, :] > 0.5
                    total = total + jnp.where(own, 0.0, arrived_ref[slot, 0:stat_rows, :])
                    piece = piece + jnp.where(own, arrived_ref[slot, 0:widest, :], 0.0)
                pieces.append(piece)
            products = jnp.sum(total[coarse_rows : coarse_rows + step_id + 1], axis=1, keepdims=True)
            heads = [products[i : i + 1] for i in range(step_id)]
            square = products[step_id : step_id + 1]
            remaining = square
            for head in heads:
                remaining = remaining - head * head
            length = jnp.sqrt(jnp.maximum(remaining, square * 1e-12))
            scale = 1.0 / length
            gathered = []
            for coarse_ref in coarse_refs:
                piece = coarse_ref[:, 0:LANES] * total[0:1]
                for chunk in range(1, coarse_rows):
                    piece = piece + (
                        coarse_ref[:, chunk * LANES : (chunk + 1) * LANES] * total[chunk : chunk + 1]
                    )
                gathered.append(piece)
            gathered = jnp.concatenate(gathered, axis=0)
            column = jnp.sum(gathered, axis=1, keepdims=True)
            same = iota((LANES, LANES), 0) == iota((LANES, LANES), 1)
            lines = [
                column_sum(jnp.where(same, column[start : start + LANES], 0.0))
                for start in range(0, sub_aggregates, LANES)
            ]
            own_coarse = sub_member_ref[:, 0:LANES].astype(F32) * lines[0]
            row_coarse = lane_rows_ref[0] * lines[0]
            for chunk in range(1, sub_chunks):
                own_coarse = own_coarse + (
                    sub_member_ref[:, chunk * LANES : (chunk + 1) * LANES].astype(F32) * lines[chunk]
                )
                row_coarse = row_coarse + lane_rows_ref[chunk] * lines[chunk]
            own_coarse = jnp.sum(own_coarse, axis=1, keepdims=True)
            row_coarse = jnp.sum(row_coarse, axis=1, keepdims=True)
            basis_value = basis_ref[...]
            direction = smoothed_ref[...] + own_coarse * basis_value
            for number, head in enumerate(heads):
                z_copies[number].wait()
                direction = direction - head * z_ref[number]
            direction = direction * scale
            z_ref[step_id] = direction
            z_copy = pltpu.make_async_copy(z_ref.at[step_id], z_hbm, semaphores.at[step_id])
            z_copy.start()
            route = route_ref[...]
            rows = gather_rounds(pieces, route, rounds) + row_coarse * basis_rows_ref[...]
            for number, head in enumerate(heads):
                rows = rows - head * held(m_at, number, margin_rows)
            rows = rows * scale
            vector = vector_ref[...]
            earlier = [held(v_at, number, block_count) for number in range(step_id)]
            for head, other in zip(heads, earlier):
                vector = vector - head * other
            vector = vector * scale
            product = line_product(direction, diagonal_ref[...], link_ref[...]) - put(
                target_ref[...], couple(rows, pair_ref, live_ref[...])
            )
            against = earlier + [vector, product]
            if last:
                (slot_ref,) = outs
                block = statistics_block(
                    product, basis_value, None, home_ref[...], against, ROWS, 0
                )
                for slot in range(devices):
                    slot_ref[slot] = block
            else:
                product_ref, slot_ref = outs
                keep(v_at, step_id, vector)
                keep(m_at, step_id, rows)
                product_ref[...] = product
                slots = spread_rounds(pick(selector_ref[...], product), route, subs, rounds)
                block = statistics_block(
                    product,
                    basis_value,
                    member_ref[...].astype(F32),
                    home_ref[...],
                    against,
                    stat_rows,
                    coarse_rows,
                )
                for sub_id in range(subs):
                    slot_ref[sub_id, 0:widest, :] = slots[sub_id]
                    slot_ref[sub_id, widest:, :] = block
            keep(
                head_at,
                step_id,
                jnp.broadcast_to(
                    jnp.concatenate(
                        heads + [length] + [jnp.zeros((ROWS - step_id - 1, 1), F32)], axis=0
                    ),
                    (ROWS, LANES),
                ),
            )
            z_copy.wait()

        return kernel

    vector = start_vector
    state = None
    z_list = []
    state_shape = vmem((state_rows, LANES))
    for step_id in range(ITERS):
        first = step_id == 0
        last = step_id == ITERS - 1
        arrived = lax.all_to_all(outgoing, "sub", 0, 0)
        (solved,) = call(
            solve,
            [vmem(full)],
            vector,
            inverse_blocks,
            name=f"solve{step_id}",
            places="vh",
            scratch=[
                vmem((block_count, unknowns, unknowns)),
                pltpu.SemaphoreType.DMA((block_count // ROWS,)),
            ],
        )
        outs = [vmem(full), vmem((devices, slot_rows, unknowns)), vmem((stat_rows, LANES))]
        if first:
            outs += [vmem((margin_rows, unknowns)), vmem((sub_chunks, margin_rows, LANES))]
        else:
            outs += [state_shape]
        made = call(
            smooth(first),
            outs,
            arrived,
            solved,
            weights,
            pairs,
            target,
            selector,
            route,
            live,
            part_table,
            outgoing,
            *([] if first else [state]),
            name=f"smooth{step_id}",
            aliases={} if first else {10: 3},
        )
        if first:
            smoothed, slots, sums, basis_rows, lane_rows = made
        else:
            smoothed, slots, sums, state = made
        arrived = lax.all_to_all(slots, ("sub", "coarse"), 0, 0)
        if last:
            outs = [vmem((devices, ROWS, LANES))]
        else:
            outs = [vmem(full), vmem((subs, widest + stat_rows, unknowns))]
        outs += [pltpu.HBM(full, F32), state_shape]
        made = call(
            advance(step_id),
            outs,
            arrived,
            sums,
            smoothed,
            vector,
            sub_member,
            member,
            home,
            basis,
            basis_rows,
            lane_rows,
            pairs,
            target,
            selector,
            route,
            live,
            part_table,
            diagonal_local,
            link_local,
            *coarse_chunks,
            *z_list,
            *([] if first else [state]),
            name=f"advance{step_id}",
            places="v" * (18 + parts) + "h" * step_id,
            out_places="v" * (len(outs) - 2) + "hv",
            aliases={} if first else {18 + parts + step_id: len(outs) - 1},
            scratch=[
                vmem((step_id + 1, block_count, unknowns)),
                pltpu.SemaphoreType.DMA((step_id + 1,)),
            ],
        )
        *made, z_new, state = made
        z_list.append(z_new)
        if last:
            (slots,) = made
        else:
            vector, outgoing = made
    arrived = lax.all_to_all(slots, ("sub", "coarse"), 0, 0)

    def finish(arrived_ref, state_ref, *refs):
        z_hbms = refs[:ITERS]
        out_ref, z_ref, semaphores = refs[ITERS:]
        z_copies = [
            pltpu.make_async_copy(source, z_ref.at[number], semaphores.at[number])
            for number, source in enumerate(z_hbms)
        ]
        for copy in z_copies:
            copy.start()
        total = arrived_ref[0]
        for slot in range(1, devices):
            total = total + arrived_ref[slot]
        products = jnp.sum(total, axis=1, keepdims=True)
        heads = [products[i : i + 1] for i in range(ITERS)]
        square = products[ITERS : ITERS + 1]
        remaining = square
        for head in heads:
            remaining = remaining - head * head
        length = jnp.sqrt(jnp.maximum(remaining, square * 1e-12))
        beta = state_ref[head_at : head_at + 1, 0:1]
        columns = []
        for column_id in range(1, ITERS):
            at = head_at + column_id * ROWS
            columns.append([state_ref[at + i : at + i + 1, 0:1] for i in range(column_id + 1)])
        columns.append(heads + [length])
        weights_found = givens_solve(columns, beta)
        result = None
        for position in range(ITERS):
            z_copies[position].wait()
            term = weights_found[position] * z_ref[position]
            result = term if result is None else result + term
        out_ref[...] = result

    (answer,) = call(
        finish,
        [jax.ShapeDtypeStruct(full, F32)],
        arrived,
        state,
        *z_list,
        name="finish",
        places="vv" + "h" * ITERS,
        scratch=[vmem((ITERS,) + full), pltpu.SemaphoreType.DMA((ITERS,))],
    )
    return answer.reshape(right_side.shape)


def givens_solve(columns, beta):
    steps_count = len(columns)
    cosines = []
    sines = []
    side_terms = [beta] + [jnp.zeros_like(beta) for unused in range(steps_count)]
    triangle = []
    for column_id in range(steps_count):
        column = list(columns[column_id])
        for row_id in range(column_id):
            upper = column[row_id]
            lower = column[row_id + 1]
            column[row_id] = cosines[row_id] * upper + sines[row_id] * lower
            column[row_id + 1] = cosines[row_id] * lower - sines[row_id] * upper
        upper = column[column_id]
        lower = column[column_id + 1]
        radius = jnp.sqrt(upper * upper + lower * lower)
        cosine = upper / radius
        sine_value = lower / radius
        column[column_id] = radius
        cosines.append(cosine)
        sines.append(sine_value)
        side_terms[column_id + 1] = -sine_value * side_terms[column_id]
        side_terms[column_id] = cosine * side_terms[column_id]
        triangle.append(column)
    weights = [None] * steps_count
    for column_id in reversed(range(steps_count)):
        running = side_terms[column_id]
        for later_col in range(column_id + 1, steps_count):
            running = running - triangle[later_col][column_id] * weights[later_col]
        weights[column_id] = running / triangle[column_id][column_id]
    return weights


def solution(mesh):
    placed = (
        P("sub", "coarse", None, None),
        P("sub", "coarse", None, None),
        P("sub", "coarse", None, None),
        P("sub", "coarse", None, None, None),
        P("sub", "coarse", None, None, None),
        P("sub", "coarse", None, None),
        P("coarse", None),
        P("sub", None),
        P("sub", None),
        P("sub", "coarse", None, None),
        P("sub", "coarse", None),
    )
    return jax.shard_map(
        on_device,
        mesh=mesh,
        in_specs=placed,
        out_specs=P("sub", "coarse", None, None),
        check_vma=False,
    )
```

```python
import jax
import jax.numpy as jnp
from jax import lax
from jax.experimental import pallas as pl
from jax.experimental.pallas import tpu as pltpu
from jax.sharding import PartitionSpec as P

BS = 128
BPD = 128
AGG_DEV = 16
ITERS = 4
LANES = 128
ROWS = 8
BF16 = jnp.bfloat16
F32 = jnp.float32


def split(values):
    high = values.astype(BF16)
    low = (values - high.astype(F32)).astype(BF16)
    return high, low


def dot_rows(left, right):
    return lax.dot_general(left, right, (((1,), (1,)), ((), ())), preferred_element_type=F32)


def dot_plain(left, right):
    return lax.dot_general(left, right, (((1,), (0,)), ((), ())), preferred_element_type=F32)


def paired_rows(values):
    high, low = split(values)
    return jnp.concatenate(
        [
            jnp.concatenate([high, high], axis=1),
            jnp.concatenate([low, jnp.zeros_like(low)], axis=1),
        ],
        axis=0,
    )


def pick(selector, values):
    high, low = split(values)
    return dot_plain(selector, jnp.concatenate([high, low], axis=0))


def column_sum(values):
    return jnp.sum(values, axis=0, keepdims=True)


def line_product(values, diagonal, link):
    rows = values.shape[0]
    lanes = values.shape[1]
    row = lax.broadcasted_iota(jnp.int32, values.shape, 0)
    lane = lax.broadcasted_iota(jnp.int32, values.shape, 1)
    next_lane = pltpu.roll(values, lanes - 1, 1)
    next_row = pltpu.roll(next_lane, rows - 1, 0)
    ahead = jnp.where(lane < lanes - 1, next_lane, jnp.where(row < rows - 1, next_row, 0.0))
    scaled = link * values
    last_lane = pltpu.roll(scaled, 1, 1)
    last_row = pltpu.roll(last_lane, 1, 0)
    behind = jnp.where(lane > 0, last_lane, jnp.where(row > 0, last_row, 0.0))
    return diagonal * values - (ahead * link + behind)


def couple(arrived, pair_ref, live):
    rounds = pair_ref.shape[0]
    widest = arrived.shape[0] // rounds
    pieces = []
    for round_id in range(rounds):
        left = paired_rows(arrived[round_id * widest : (round_id + 1) * widest])
        both = dot_rows(left, pair_ref[round_id])
        pieces.append(both[:widest] + both[widest:])
    return jnp.concatenate(pieces, axis=0) * live


def gather_rounds(slots, route, rounds):
    pieces = []
    for round_id in range(rounds):
        total = None
        for sub_id, piece in enumerate(slots):
            at = round_id * len(slots) + sub_id
            term = route[at : at + 1] * piece
            total = term if total is None else total + term
        pieces.append(total)
    return jnp.concatenate(pieces, axis=0)


def spread_rounds(values, route, subs, rounds):
    widest = values.shape[0] // rounds
    slots = []
    for sub_id in range(subs):
        total = None
        for round_id in range(rounds):
            at = round_id * subs + sub_id
            term = route[at : at + 1] * values[round_id * widest : (round_id + 1) * widest]
            total = term if total is None else total + term
        slots.append(total)
    return slots


def vmem(shape, dtype=F32):
    return pltpu.VMEM(shape, dtype)


def call(kernel, outs, *args, name, places="", aliases=None, scratch=()):
    places = places + "v" * (len(args) - len(places))
    spaces = {"s": pltpu.SMEM, "h": pltpu.HBM, "v": pltpu.VMEM}
    return pl.pallas_call(
        kernel,
        out_shape=outs,
        in_specs=[pl.BlockSpec(memory_space=spaces[place]) for place in places],
        out_specs=[pl.BlockSpec(memory_space=pltpu.VMEM)] * len(outs),
        input_output_aliases=aliases or {},
        scratch_shapes=list(scratch),
        name=name,
        compiler_params=pltpu.CompilerParams(vmem_limit_bytes=16 * 1024 * 1024),
    )(
        *[
            pltpu.with_memory_space_constraint(
                arg, pltpu.VMEM if place == "v" else pltpu.HBM
            )
            for arg, place in zip(args, places)
        ]
    )


def on_device(
    right_side,
    diagonal,
    cell_link,
    block_inverse,
    coupling,
    coarse_basis,
    coarse_inverse,
    partner,
    margin_width,
    margin_blocks,
    aggregate,
):
    subs = lax.axis_size("sub")
    parts = lax.axis_size("coarse")
    devices = subs * parts
    block_count = right_side.shape[2]
    unknowns = right_side.shape[3]
    rounds = margin_blocks.shape[2]
    widest = margin_blocks.shape[3]
    aggregates = coarse_inverse.shape[1]
    own_aggregates = aggregates // devices
    sub_aggregates = subs * own_aggregates
    sub_chunks = sub_aggregates // LANES
    sub_span = subs // parts
    chunk_rows = sub_span * own_aggregates
    factor = (BS * BPD / AGG_DEV) ** (-0.5)
    coarse_rows = aggregates // LANES
    stat_rows = -(-(coarse_rows + ITERS) // ROWS) * ROWS
    slot_rows = max(widest, stat_rows)
    margin_rows = rounds * widest
    table_rows = -(-2 * margin_rows // LANES) * LANES
    full = (block_count, unknowns)

    v_at = 0
    z_at = v_at + (ITERS - 1) * block_count
    m_at = z_at + ITERS * block_count
    head_at = m_at + (ITERS - 1) * margin_rows
    state_rows = head_at + ITERS * ROWS
    blocks = margin_blocks[0, 0]
    member_of = aggregate[0]
    own_bits = own_aggregates.bit_length() - 1
    part_bits = parts.bit_length() - 1
    span_bits = sub_span.bit_length() - 1
    lane_bits = LANES.bit_length() - 1
    assert own_aggregates == 1 << own_bits and parts == 1 << part_bits
    assert sub_span == 1 << span_bits and sub_span * parts == subs

    def iota(shape, dim):
        return lax.broadcasted_iota(jnp.int32, shape, dim)

    def hot(condition):
        return jnp.where(condition, 1.0, 0.0).astype(F32)

    def coarse_lane(numbers):
        own_device = numbers >> own_bits
        own_part = own_device & (parts - 1)
        own_sub = own_device >> part_bits
        turn = (own_part - (own_sub >> span_bits)) & (parts - 1)
        return (
            turn * chunk_rows
            + (own_sub & (sub_span - 1)) * own_aggregates
            + (numbers & (own_aggregates - 1))
        )

    def statistics_block(vector, basis_value, member_value, home, dots, rows, count):
        inner = jnp.sum(basis_value * vector, axis=1, keepdims=True)
        line = column_sum(inner * member_value) * factor
        lines = [home[chunk : chunk + 1] * line for chunk in range(count)]
        lines += [column_sum(other * vector) for other in dots]
        if len(lines) < rows:
            lines.append(jnp.zeros((rows - len(lines), LANES), F32))
        return jnp.concatenate(lines, axis=0)

    def begin(
        blocks_ref,
        partner_ref,
        width_ref,
        number_ref,
        start_hbm,
        basis_hbm,
        member_of_hbm,
        coarse_hbm,
        *refs,
    ):
        (
            slot_ref,
            selector_ref,
            route_ref,
            live_ref,
            member_ref,
            home_ref,
            start_ref,
            basis_ref,
            member_of_ref,
        ) = refs[:9]
        chunk_refs = refs[9 : 9 + parts]
        semaphores = refs[9 + parts]
        copies = [
            pltpu.make_async_copy(source, to, semaphores.at[position])
            for position, (source, to) in enumerate(
                [(start_hbm, start_ref), (basis_hbm, basis_ref), (member_of_hbm, member_of_ref)]
            )
        ]
        own_part = (number_ref[0, 0] >> own_bits) & (parts - 1)
        chunk_copies = []
        for turn, chunk_ref in enumerate(chunk_refs):
            to_part = (own_part + turn) & (parts - 1)
            for span in range(sub_span):
                first = pl.multiple_of((span * parts + to_part) * own_aggregates, own_aggregates)
                chunk_copies.append(
                    pltpu.make_async_copy(
                        coarse_hbm.at[pl.ds(first, own_aggregates), :],
                        chunk_ref.at[pl.ds(span * own_aggregates, own_aggregates), :],
                        semaphores.at[3 + turn * sub_span + span],
                    )
                )
        for copy in copies + chunk_copies:
            copy.start()
        row = iota((widest, LANES), 0)
        lane = iota((widest, LANES), 1)
        tables = []
        for round_id in range(rounds):
            wanted = jnp.zeros((widest, LANES), jnp.int32)
            for position in range(widest):
                wanted = jnp.where(row == position, blocks_ref[round_id, position], wanted)
            tables.append(hot(lane == wanted))
            live_ref[round_id * widest : (round_id + 1) * widest, :] = hot(
                row < width_ref[0, round_id]
            )
            sub_row = iota((subs, LANES), 0)
            route_ref[round_id * subs : (round_id + 1) * subs, :] = hot(
                sub_row == partner_ref[0, round_id]
            )
        for copy in copies:
            copy.wait()
        start = start_ref[...]
        basis_value = basis_ref[...]
        numbers = member_of_ref[...]
        table = jnp.concatenate(tables, axis=0)
        table = jnp.concatenate([table, table], axis=1).astype(BF16)
        selector_ref[...] = table
        route = route_ref[...]
        member = hot((numbers & (LANES - 1)) == iota((LANES, block_count), 0)).T
        member_ref[...] = member
        home = hot((numbers >> lane_bits) == iota((coarse_rows, LANES), 0))
        home_ref[...] = home
        own_lane = coarse_lane(numbers)
        rows_start = spread_rounds(pick(table, start), route, subs, rounds)
        rows_basis = spread_rounds(pick(table, basis_value), route, subs, rounds)
        rows_lane = []
        for chunk in range(sub_chunks):
            lane_table = hot(own_lane == iota((LANES, block_count), 0) + chunk * LANES)
            rows_lane.append(
                spread_rounds(
                    dot_rows(table[:, :block_count], lane_table.astype(BF16)), route, subs, rounds
                )
            )
        statistic = statistics_block(
            start, basis_value, member, home, [start], stat_rows, coarse_rows
        )
        for sub_id in range(subs):
            slot_ref[sub_id, 0:widest, :] = rows_start[sub_id]
            slot_ref[sub_id, widest : widest + stat_rows, :] = statistic
            at = widest + stat_rows
            slot_ref[sub_id, at : at + widest, :] = rows_basis[sub_id]
            for chunk in range(sub_chunks):
                at = at + widest
                slot_ref[sub_id, at : at + widest, :] = rows_lane[chunk][sub_id]
        for copy in chunk_copies:
            copy.wait()

    (
        outgoing,
        selector,
        route,
        live,
        member,
        home,
        start_vector,
        basis,
        member_of,
        *coarse_chunks,
    ) = call(
        begin,
        [
            vmem((subs, (2 + sub_chunks) * widest + stat_rows, unknowns)),
            vmem((margin_rows, 2 * block_count), BF16),
            vmem((rounds * subs, LANES)),
            vmem((margin_rows, LANES)),
            vmem((block_count, LANES)),
            vmem((coarse_rows, LANES)),
            vmem(full),
            vmem(full),
            vmem((1, block_count), jnp.int32),
        ]
        + [vmem((chunk_rows, aggregates))] * parts,
        blocks,
        partner,
        margin_width,
        aggregate[0],
        right_side[0, 0],
        coarse_basis[0, 0],
        aggregate[0],
        coarse_inverse,
        name="begin",
        places="sssshhhh",
        scratch=[pltpu.SemaphoreType.DMA((3 + parts * sub_span,))],
    )
    for turn in range(1, parts):
        coarse_chunks[turn] = lax.ppermute(
            coarse_chunks[turn], "coarse", [(i, (i + turn) % parts) for i in range(parts)]
        )

    def put(target_value, values):
        high, low = split(values)
        pieces = [high, low]
        if table_rows > 2 * margin_rows:
            pieces.append(jnp.zeros((table_rows - 2 * margin_rows, unknowns), BF16))
        return dot_plain(target_value, jnp.concatenate(pieces, axis=0))

    def smooth_rest(arrived_ref, out, target, selector, route, part_ref, stat_ref, slot_ref, sum_ref):
        slots = spread_rounds(pick(selector, out), route, subs, rounds)
        statistic = stat_ref[0, widest : widest + stat_rows, :]
        if stat_rows < slot_rows:
            statistic = jnp.concatenate(
                [statistic, jnp.zeros((slot_rows - stat_rows, LANES), F32)], axis=0
            )
        for sub_id in range(subs):
            piece = slots[sub_id]
            if widest < slot_rows:
                piece = jnp.concatenate(
                    [piece, jnp.zeros((slot_rows - widest, unknowns), F32)], axis=0
                )
            for part_id in range(parts):
                slot_ref[sub_id * parts + part_id] = jnp.where(
                    part_ref[part_id : part_id + 1, :] > 0.5, piece, statistic
                )
        total = arrived_ref[0, widest : widest + stat_rows, :]
        for sub_id in range(1, subs):
            total = total + arrived_ref[sub_id, widest : widest + stat_rows, :]
        sum_ref[...] = total

    def arrived_rows(arrived_ref, at, route):
        return gather_rounds(
            [arrived_ref[sub_id, at : at + widest, :] for sub_id in range(subs)], route, rounds
        )

    def block_rows(shifted_ref, group):
        rows = pl.ds(pl.multiple_of(group * ROWS, ROWS), ROWS)
        return paired_rows(shifted_ref[rows, :])

    def block_product(left, weight_of):
        row = iota((ROWS, unknowns), 0)
        total = jnp.zeros((ROWS, unknowns), F32)
        for offset in range(ROWS // 2):
            both = dot_plain(left, weight_of(offset))
            both = both[:ROWS] + both[ROWS:]
            total = jnp.where(row == 2 * offset, both[:, :unknowns], total)
            total = jnp.where(row == 2 * offset + 1, both[:, unknowns:], total)
        return total

    def smooth_first(
        arrived_ref,
        vector_ref,
        selector_ref,
        route_ref,
        live_ref,
        member_of_ref,
        stat_ref,
        inverse_hbm,
        coupling_hbm,
        diagonal_hbm,
        link_hbm,
        *refs,
    ):
        chunk_refs = refs[:parts]
        (
            out_ref,
            slot_ref,
            sum_ref,
            basis_rows_ref,
            lane_rows_ref,
            weight_ref,
            pair_ref,
            target_ref,
            sub_member_ref,
            part_ref,
            diagonal_ref,
            link_ref,
            coarse_ref,
            inverse_ref,
            coupling_ref,
            shifted_ref,
            semaphores,
            group_semaphores,
        ) = refs[parts:]
        copies = [
            pltpu.make_async_copy(source, to, semaphores.at[position])
            for position, (source, to) in enumerate(
                [
                    (coupling_hbm, coupling_ref),
                    (diagonal_hbm, diagonal_ref),
                    (link_hbm, link_ref),
                ]
            )
        ]

        def group_copy(group):
            rows = pl.ds(group * ROWS, ROWS)
            return pltpu.make_async_copy(
                inverse_hbm.at[rows], inverse_ref.at[rows], group_semaphores.at[group]
            )

        for copy in copies:
            copy.start()
        for group in range(block_count // ROWS):
            group_copy(group).start()
        route = route_ref[...]
        table = selector_ref[:, 0:block_count].astype(F32)
        pieces = [table, table]
        if table_rows > 2 * margin_rows:
            pieces.append(jnp.zeros((table_rows - 2 * margin_rows, block_count), F32))
        table = jnp.concatenate(pieces, axis=0)
        target_ref[...] = jnp.concatenate(
            [table[start : start + LANES].T for start in range(0, table_rows, LANES)], axis=1
        ).astype(BF16)
        numbers = member_of_ref[...]
        own_lane = coarse_lane(numbers)
        for chunk in range(sub_chunks):
            sub_member_ref[:, chunk * LANES : (chunk + 1) * LANES] = hot(
                own_lane == iota((LANES, block_count), 0) + chunk * LANES
            ).T
        part_ref[...] = hot(((numbers >> own_bits) & (parts - 1)) == iota((ROWS, LANES), 0))
        for turn, chunk_ref in enumerate(chunk_refs):
            coarse_ref[turn * chunk_rows : (turn + 1) * chunk_rows, :] = chunk_ref[...]
        at = widest + stat_rows
        basis_rows_ref[...] = arrived_rows(arrived_ref, at, route)
        for chunk in range(sub_chunks):
            at = at + widest
            lane_rows_ref[chunk] = arrived_rows(arrived_ref, at, route)
        copies[0].wait()
        for round_id in range(rounds):
            high, low = split(coupling_ref[round_id])
            pair_ref[round_id, :, 0:unknowns] = high
            pair_ref[round_id, :, unknowns : 2 * unknowns] = low
        mapped = couple(arrived_rows(arrived_ref, 0, route), pair_ref, live_ref[...])
        shifted_ref[...] = vector_ref[...] + put(target_ref[...], mapped)

        def step(group, carry):
            group_copy(group).wait()
            left = block_rows(shifted_ref, group)

            def weight_of(offset):
                pair = group * (ROWS // 2) + offset
                highs = []
                lows = []
                for position in range(2):
                    high, low = split(inverse_ref[pair * 2 + position].T)
                    lanes = slice(position * unknowns, (position + 1) * unknowns)
                    weight_ref[pair, 0:unknowns, lanes] = high
                    weight_ref[pair, unknowns : 2 * unknowns, lanes] = low
                    highs.append(high)
                    lows.append(low)
                return jnp.concatenate(
                    [jnp.concatenate(highs, axis=1), jnp.concatenate(lows, axis=1)], axis=0
                )

            rows = pl.ds(pl.multiple_of(group * ROWS, ROWS), ROWS)
            out_ref[rows, :] = block_product(left, weight_of)
            return carry

        lax.fori_loop(0, block_count // ROWS, step, 0, unroll=2)
        for copy in copies[1:]:
            copy.wait()
        smooth_rest(
            arrived_ref,
            out_ref[...],
            target_ref[...],
            selector_ref[...],
            route,
            part_ref,
            stat_ref,
            slot_ref,
            sum_ref,
        )

    def smooth(
        arrived_ref,
        vector_ref,
        weight_ref,
        pair_ref,
        target_ref,
        selector_ref,
        route_ref,
        live_ref,
        part_ref,
        stat_ref,
        out_ref,
        slot_ref,
        sum_ref,
    ):
        route = route_ref[...]
        mapped = couple(arrived_rows(arrived_ref, 0, route), pair_ref, live_ref[...])
        shifted = vector_ref[...] + put(target_ref[...], mapped)
        pieces = []
        for group in range(block_count // ROWS):
            left = paired_rows(shifted[group * ROWS : (group + 1) * ROWS])
            pieces.append(
                block_product(left, lambda offset: weight_ref[group * (ROWS // 2) + offset])
            )
        out = jnp.concatenate(pieces, axis=0)
        out_ref[...] = out
        smooth_rest(
            arrived_ref,
            out,
            target_ref[...],
            selector_ref[...],
            route,
            part_ref,
            stat_ref,
            slot_ref,
            sum_ref,
        )

    def advance(step_id):
        first = step_id == 0
        last = step_id == ITERS - 1

        def kernel(*refs):
            (
                arrived_ref,
                sum_ref,
                smoothed_ref,
                vector_ref,
                sub_member_ref,
                member_ref,
                home_ref,
                basis_ref,
                basis_rows_ref,
                lane_rows_ref,
                pair_ref,
                target_ref,
                selector_ref,
                route_ref,
                live_ref,
                part_ref,
                diagonal_ref,
                link_ref,
                coarse_ref,
            ) = refs[:19]
            outs = list(refs[19:])
            if first:
                state_ref = outs.pop()
            else:
                state_in = outs.pop(0)
                state_ref = outs.pop()

                def held(at, number, rows):
                    return state_in[at + number * rows : at + (number + 1) * rows, :]

            def keep(at, number, values):
                rows = values.shape[0]
                state_ref[at + number * rows : at + (number + 1) * rows, :] = values

            total = sum_ref[...]
            pieces = []
            for sub_id in range(subs):
                piece = jnp.zeros((widest, unknowns), F32)
                for part_id in range(parts):
                    slot = sub_id * parts + part_id
                    own = part_ref[part_id : part_id + 1, :] > 0.5
                    total = total + jnp.where(own, 0.0, arrived_ref[slot, 0:stat_rows, :])
                    piece = piece + jnp.where(own, arrived_ref[slot, 0:widest, :], 0.0)
                pieces.append(piece)
            products = jnp.sum(total[coarse_rows : coarse_rows + step_id + 1], axis=1, keepdims=True)
            heads = [products[i : i + 1] for i in range(step_id)]
            square = products[step_id : step_id + 1]
            remaining = square
            for head in heads:
                remaining = remaining - head * head
            length = jnp.sqrt(jnp.maximum(remaining, square * 1e-12))
            scale = 1.0 / length
            gathered = coarse_ref[:, 0:LANES] * total[0:1]
            for chunk in range(1, coarse_rows):
                gathered = gathered + (
                    coarse_ref[:, chunk * LANES : (chunk + 1) * LANES] * total[chunk : chunk + 1]
                )
            column = jnp.sum(gathered, axis=1, keepdims=True)
            same = iota((LANES, LANES), 0) == iota((LANES, LANES), 1)
            lines = [
                column_sum(jnp.where(same, column[start : start + LANES], 0.0))
                for start in range(0, sub_aggregates, LANES)
            ]
            own_coarse = sub_member_ref[:, 0:LANES] * lines[0]
            row_coarse = lane_rows_ref[0] * lines[0]
            for chunk in range(1, sub_chunks):
                own_coarse = own_coarse + (
                    sub_member_ref[:, chunk * LANES : (chunk + 1) * LANES] * lines[chunk]
                )
                row_coarse = row_coarse + lane_rows_ref[chunk] * lines[chunk]
            own_coarse = jnp.sum(own_coarse, axis=1, keepdims=True)
            row_coarse = jnp.sum(row_coarse, axis=1, keepdims=True)
            basis_value = basis_ref[...]
            direction = smoothed_ref[...] + own_coarse * basis_value
            for number, head in enumerate(heads):
                direction = direction - head * held(z_at, number, block_count)
            direction = direction * scale
            route = route_ref[...]
            rows = gather_rounds(pieces, route, rounds) + row_coarse * basis_rows_ref[...]
            for number, head in enumerate(heads):
                rows = rows - head * held(m_at, number, margin_rows)
            rows = rows * scale
            vector = vector_ref[...]
            earlier = [held(v_at, number, block_count) for number in range(step_id)]
            for head, other in zip(heads, earlier):
                vector = vector - head * other
            vector = vector * scale
            product = line_product(direction, diagonal_ref[...], link_ref[...]) - put(
                target_ref[...], couple(rows, pair_ref, live_ref[...])
            )
            against = earlier + [vector, product]
            if last:
                (slot_ref,) = outs
                block = statistics_block(
                    product, basis_value, member_ref[...], home_ref[...], against, ROWS, 0
                )
                for slot in range(devices):
                    slot_ref[slot] = block
            else:
                product_ref, slot_ref = outs
                keep(v_at, step_id, vector)
                keep(m_at, step_id, rows)
                product_ref[...] = product
                slots = spread_rounds(pick(selector_ref[...], product), route, subs, rounds)
                block = statistics_block(
                    product,
                    basis_value,
                    member_ref[...],
                    home_ref[...],
                    against,
                    stat_rows,
                    coarse_rows,
                )
                for sub_id in range(subs):
                    slot_ref[sub_id, 0:widest, :] = slots[sub_id]
                    slot_ref[sub_id, widest:, :] = block
            keep(z_at, step_id, direction)
            keep(
                head_at,
                step_id,
                jnp.broadcast_to(
                    jnp.concatenate(
                        heads + [length] + [jnp.zeros((ROWS - step_id - 1, 1), F32)], axis=0
                    ),
                    (ROWS, LANES),
                ),
            )

        return kernel

    vector = start_vector
    state = None
    state_shape = vmem((state_rows, LANES))
    for step_id in range(ITERS):
        first = step_id == 0
        last = step_id == ITERS - 1
        arrived = lax.all_to_all(outgoing, "sub", 0, 0)
        outs = [vmem(full), vmem((devices, slot_rows, unknowns)), vmem((stat_rows, LANES))]
        if first:
            (
                smoothed,
                slots,
                sums,
                basis_rows,
                lane_rows,
                weights,
                pairs,
                target,
                sub_member,
                part_table,
                diagonal_local,
                link_local,
                coarse_block,
            ) = call(
                smooth_first,
                outs
                + [
                    vmem((margin_rows, unknowns)),
                    vmem((sub_chunks, margin_rows, LANES)),
                    vmem((block_count // 2, 2 * unknowns, 2 * unknowns), BF16),
                    vmem((rounds, unknowns, 2 * unknowns), BF16),
                    vmem((block_count, table_rows), BF16),
                    vmem((block_count, sub_aggregates)),
                    vmem((ROWS, LANES)),
                    vmem(full),
                    vmem(full),
                    vmem((sub_aggregates, aggregates)),
                ],
                arrived,
                vector,
                selector,
                route,
                live,
                member_of,
                outgoing,
                block_inverse[0, 0],
                coupling[0, 0],
                diagonal[0, 0],
                cell_link[0, 0],
                *coarse_chunks,
                name="smooth0",
                places="vvvvvvvhhhh",
                scratch=[
                    vmem((block_count, unknowns, unknowns)),
                    vmem((rounds, unknowns, unknowns)),
                    vmem(full),
                    pltpu.SemaphoreType.DMA((3,)),
                    pltpu.SemaphoreType.DMA((block_count // ROWS,)),
                ],
            )
        else:
            smoothed, slots, sums = call(
                smooth,
                outs,
                arrived,
                vector,
                weights,
                pairs,
                target,
                selector,
                route,
                live,
                part_table,
                outgoing,
                name=f"smooth{step_id}",
            )
        arrived = lax.all_to_all(slots, ("sub", "coarse"), 0, 0)
        if last:
            outs = [vmem((devices, ROWS, LANES)), state_shape]
        else:
            outs = [vmem(full), vmem((subs, widest + stat_rows, unknowns)), state_shape]
        made = call(
            advance(step_id),
            outs,
            arrived,
            sums,
            smoothed,
            vector,
            sub_member,
            member,
            home,
            basis,
            basis_rows,
            lane_rows,
            pairs,
            target,
            selector,
            route,
            live,
            part_table,
            diagonal_local,
            link_local,
            coarse_block,
            *([] if first else [state]),
            name=f"advance{step_id}",
            aliases={} if first else {19: len(outs) - 1},
        )
        if last:
            slots, state = made
        else:
            vector, outgoing, state = made
    arrived = lax.all_to_all(slots, ("sub", "coarse"), 0, 0)

    def finish(arrived_ref, state_ref, out_ref):
        total = arrived_ref[0]
        for slot in range(1, devices):
            total = total + arrived_ref[slot]
        products = jnp.sum(total, axis=1, keepdims=True)
        heads = [products[i : i + 1] for i in range(ITERS)]
        square = products[ITERS : ITERS + 1]
        remaining = square
        for head in heads:
            remaining = remaining - head * head
        length = jnp.sqrt(jnp.maximum(remaining, square * 1e-12))
        beta = state_ref[head_at : head_at + 1, 0:1]
        columns = []
        for column_id in range(1, ITERS):
            at = head_at + column_id * ROWS
            columns.append([state_ref[at + i : at + i + 1, 0:1] for i in range(column_id + 1)])
        columns.append(heads + [length])
        weights_found = givens_solve(columns, beta)
        result = weights_found[0] * state_ref[z_at : z_at + block_count, :]
        for position in range(1, ITERS):
            at = z_at + position * block_count
            result = result + weights_found[position] * state_ref[at : at + block_count, :]
        out_ref[...] = result

    (answer,) = call(finish, [jax.ShapeDtypeStruct(full, F32)], arrived, state, name="finish")
    return answer.reshape(right_side.shape)


def givens_solve(columns, beta):
    steps_count = len(columns)
    cosines = []
    sines = []
    side_terms = [beta] + [jnp.zeros_like(beta) for unused in range(steps_count)]
    triangle = []
    for column_id in range(steps_count):
        column = list(columns[column_id])
        for row_id in range(column_id):
            upper = column[row_id]
            lower = column[row_id + 1]
            column[row_id] = cosines[row_id] * upper + sines[row_id] * lower
            column[row_id + 1] = cosines[row_id] * lower - sines[row_id] * upper
        upper = column[column_id]
        lower = column[column_id + 1]
        radius = jnp.sqrt(upper * upper + lower * lower)
        cosine = upper / radius
        sine_value = lower / radius
        column[column_id] = radius
        cosines.append(cosine)
        sines.append(sine_value)
        side_terms[column_id + 1] = -sine_value * side_terms[column_id]
        side_terms[column_id] = cosine * side_terms[column_id]
        triangle.append(column)
    weights = [None] * steps_count
    for column_id in reversed(range(steps_count)):
        running = side_terms[column_id]
        for later_col in range(column_id + 1, steps_count):
            running = running - triangle[later_col][column_id] * weights[later_col]
        weights[column_id] = running / triangle[column_id][column_id]
    return weights


def solution(mesh):
    placed = (
        P("sub", "coarse", None, None),
        P("sub", "coarse", None, None),
        P("sub", "coarse", None, None),
        P("sub", "coarse", None, None, None),
        P("sub", "coarse", None, None, None),
        P("sub", "coarse", None, None),
        P("coarse", None),
        P("sub", None),
        P("sub", None),
        P("sub", "coarse", None, None),
        P("sub", "coarse", None),
    )
    return jax.shard_map(
        on_device,
        mesh=mesh,
        in_specs=placed,
        out_specs=P("sub", "coarse", None, None),
        check_vma=False,
    )
```

```python
import jax
import jax.numpy as jnp
from jax import lax
from jax.experimental import pallas as pl
from jax.experimental.pallas import tpu as pltpu
from jax.sharding import PartitionSpec as P

BS = 128
BPD = 128
AGG_DEV = 16
ITERS = 4
LANES = 128
ROWS = 8
INVERSE_PARTS = 4
BF16 = jnp.bfloat16
F32 = jnp.float32


def split(values):
    high = values.astype(BF16)
    low = (values - high.astype(F32)).astype(BF16)
    return high, low


def dot_rows(left, right):
    return lax.dot_general(left, right, (((1,), (1,)), ((), ())), preferred_element_type=F32)


def dot_plain(left, right):
    return lax.dot_general(left, right, (((1,), (0,)), ((), ())), preferred_element_type=F32)


def paired_rows(values):
    high, low = split(values)
    return jnp.concatenate(
        [
            jnp.concatenate([high, high], axis=1),
            jnp.concatenate([low, jnp.zeros_like(low)], axis=1),
        ],
        axis=0,
    )


def pick(selector, values):
    high, low = split(values)
    return dot_plain(selector, jnp.concatenate([high, low], axis=0))


def column_sum(values):
    return jnp.sum(values, axis=0, keepdims=True)


def line_product(values, diagonal, link):
    rows = values.shape[0]
    lanes = values.shape[1]
    row = lax.broadcasted_iota(jnp.int32, values.shape, 0)
    lane = lax.broadcasted_iota(jnp.int32, values.shape, 1)
    next_lane = pltpu.roll(values, lanes - 1, 1)
    next_row = pltpu.roll(next_lane, rows - 1, 0)
    ahead = jnp.where(lane < lanes - 1, next_lane, jnp.where(row < rows - 1, next_row, 0.0))
    scaled = link * values
    last_lane = pltpu.roll(scaled, 1, 1)
    last_row = pltpu.roll(last_lane, 1, 0)
    behind = jnp.where(lane > 0, last_lane, jnp.where(row > 0, last_row, 0.0))
    return diagonal * values - (ahead * link + behind)


def couple(arrived, pair_ref, live):
    rounds = pair_ref.shape[0]
    widest = arrived.shape[0] // rounds
    pieces = []
    for round_id in range(rounds):
        left = paired_rows(arrived[round_id * widest : (round_id + 1) * widest])
        both = dot_rows(left, pair_ref[round_id])
        pieces.append(both[:widest] + both[widest:])
    return jnp.concatenate(pieces, axis=0) * live


def gather_rounds(slots, route, rounds):
    pieces = []
    for round_id in range(rounds):
        total = None
        for sub_id, piece in enumerate(slots):
            at = round_id * len(slots) + sub_id
            term = route[at : at + 1] * piece
            total = term if total is None else total + term
        pieces.append(total)
    return jnp.concatenate(pieces, axis=0)


def spread_rounds(values, route, subs, rounds):
    widest = values.shape[0] // rounds
    slots = []
    for sub_id in range(subs):
        total = None
        for round_id in range(rounds):
            at = round_id * subs + sub_id
            term = route[at : at + 1] * values[round_id * widest : (round_id + 1) * widest]
            total = term if total is None else total + term
        slots.append(total)
    return slots


def vmem(shape, dtype=F32):
    return pltpu.VMEM(shape, dtype)


def call(kernel, outs, *args, name, places="", aliases=None, scratch=()):
    places = places + "v" * (len(args) - len(places))
    spaces = {"s": pltpu.SMEM, "h": pltpu.HBM, "v": pltpu.VMEM}
    return pl.pallas_call(
        kernel,
        out_shape=outs,
        in_specs=[pl.BlockSpec(memory_space=spaces[place]) for place in places],
        out_specs=[pl.BlockSpec(memory_space=pltpu.VMEM)] * len(outs),
        input_output_aliases=aliases or {},
        scratch_shapes=list(scratch),
        name=name,
        compiler_params=pltpu.CompilerParams(vmem_limit_bytes=16 * 1024 * 1024),
    )(
        *[
            pltpu.with_memory_space_constraint(
                arg, pltpu.VMEM if place == "v" else pltpu.HBM
            )
            for arg, place in zip(args, places)
        ]
    )


def on_device(
    right_side,
    diagonal,
    cell_link,
    block_inverse,
    coupling,
    coarse_basis,
    coarse_inverse,
    partner,
    margin_width,
    margin_blocks,
    aggregate,
):
    subs = lax.axis_size("sub")
    parts = lax.axis_size("coarse")
    devices = subs * parts
    block_count = right_side.shape[2]
    unknowns = right_side.shape[3]
    rounds = margin_blocks.shape[2]
    widest = margin_blocks.shape[3]
    aggregates = coarse_inverse.shape[1]
    own_aggregates = aggregates // devices
    sub_aggregates = subs * own_aggregates
    sub_chunks = sub_aggregates // LANES
    sub_span = subs // parts
    chunk_rows = sub_span * own_aggregates
    factor = (BS * BPD / AGG_DEV) ** (-0.5)
    coarse_rows = aggregates // LANES
    stat_rows = -(-(coarse_rows + ITERS) // ROWS) * ROWS
    slot_rows = max(widest, stat_rows)
    margin_rows = rounds * widest
    table_rows = -(-2 * margin_rows // LANES) * LANES
    full = (block_count, unknowns)

    v_at = 0
    z_at = v_at + (ITERS - 1) * block_count
    m_at = z_at + ITERS * block_count
    head_at = m_at + (ITERS - 1) * margin_rows
    state_rows = head_at + ITERS * ROWS
    blocks = margin_blocks[0, 0]
    member_of = aggregate[0]
    own_bits = own_aggregates.bit_length() - 1
    part_bits = parts.bit_length() - 1
    span_bits = sub_span.bit_length() - 1
    lane_bits = LANES.bit_length() - 1
    assert own_aggregates == 1 << own_bits and parts == 1 << part_bits
    assert sub_span == 1 << span_bits and sub_span * parts == subs

    def iota(shape, dim):
        return lax.broadcasted_iota(jnp.int32, shape, dim)

    def hot(condition):
        return jnp.where(condition, 1.0, 0.0).astype(F32)

    def coarse_lane(numbers):
        own_device = numbers >> own_bits
        own_part = own_device & (parts - 1)
        own_sub = own_device >> part_bits
        turn = (own_part - (own_sub >> span_bits)) & (parts - 1)
        return (
            turn * chunk_rows
            + (own_sub & (sub_span - 1)) * own_aggregates
            + (numbers & (own_aggregates - 1))
        )

    def statistics_block(vector, basis_value, member_value, home, dots, rows, count):
        inner = jnp.sum(basis_value * vector, axis=1, keepdims=True)
        line = column_sum(inner * member_value) * factor
        lines = [home[chunk : chunk + 1] * line for chunk in range(count)]
        lines += [column_sum(other * vector) for other in dots]
        if len(lines) < rows:
            lines.append(jnp.zeros((rows - len(lines), LANES), F32))
        return jnp.concatenate(lines, axis=0)

    def begin(
        blocks_ref,
        partner_ref,
        width_ref,
        number_ref,
        start_hbm,
        basis_hbm,
        member_of_hbm,
        coarse_hbm,
        *refs,
    ):
        (
            slot_ref,
            selector_ref,
            route_ref,
            live_ref,
            member_ref,
            home_ref,
            start_ref,
            basis_ref,
            member_of_ref,
        ) = refs[:9]
        chunk_refs = refs[9 : 9 + parts]
        semaphores = refs[9 + parts]
        copies = [
            pltpu.make_async_copy(source, to, semaphores.at[position])
            for position, (source, to) in enumerate(
                [(start_hbm, start_ref), (basis_hbm, basis_ref), (member_of_hbm, member_of_ref)]
            )
        ]
        own_part = (number_ref[0, 0] >> own_bits) & (parts - 1)
        chunk_copies = []
        for turn, chunk_ref in enumerate(chunk_refs):
            to_part = (own_part + turn) & (parts - 1)
            for span in range(sub_span):
                first = pl.multiple_of((span * parts + to_part) * own_aggregates, own_aggregates)
                chunk_copies.append(
                    pltpu.make_async_copy(
                        coarse_hbm.at[pl.ds(first, own_aggregates), :],
                        chunk_ref.at[pl.ds(span * own_aggregates, own_aggregates), :],
                        semaphores.at[3 + turn * sub_span + span],
                    )
                )
        for copy in copies + chunk_copies:
            copy.start()
        row = iota((widest, LANES), 0)
        lane = iota((widest, LANES), 1)
        tables = []
        for round_id in range(rounds):
            wanted = jnp.zeros((widest, LANES), jnp.int32)
            for position in range(widest):
                wanted = jnp.where(row == position, blocks_ref[round_id, position], wanted)
            tables.append(hot(lane == wanted))
            live_ref[round_id * widest : (round_id + 1) * widest, :] = hot(
                row < width_ref[0, round_id]
            )
            sub_row = iota((subs, LANES), 0)
            route_ref[round_id * subs : (round_id + 1) * subs, :] = hot(
                sub_row == partner_ref[0, round_id]
            )
        for copy in copies:
            copy.wait()
        start = start_ref[...]
        basis_value = basis_ref[...]
        numbers = member_of_ref[...]
        table = jnp.concatenate(tables, axis=0)
        table = jnp.concatenate([table, table], axis=1).astype(BF16)
        selector_ref[...] = table
        route = route_ref[...]
        member = hot((numbers & (LANES - 1)) == iota((LANES, block_count), 0)).T
        member_ref[...] = member
        home = hot((numbers >> lane_bits) == iota((coarse_rows, LANES), 0))
        home_ref[...] = home
        own_lane = coarse_lane(numbers)
        rows_start = spread_rounds(pick(table, start), route, subs, rounds)
        rows_basis = spread_rounds(pick(table, basis_value), route, subs, rounds)
        rows_lane = []
        for chunk in range(sub_chunks):
            lane_table = hot(own_lane == iota((LANES, block_count), 0) + chunk * LANES)
            rows_lane.append(
                spread_rounds(
                    dot_rows(table[:, :block_count], lane_table.astype(BF16)), route, subs, rounds
                )
            )
        statistic = statistics_block(
            start, basis_value, member, home, [start], stat_rows, coarse_rows
        )
        for sub_id in range(subs):
            slot_ref[sub_id, 0:widest, :] = rows_start[sub_id]
            slot_ref[sub_id, widest : widest + stat_rows, :] = statistic
            at = widest + stat_rows
            slot_ref[sub_id, at : at + widest, :] = rows_basis[sub_id]
            for chunk in range(sub_chunks):
                at = at + widest
                slot_ref[sub_id, at : at + widest, :] = rows_lane[chunk][sub_id]
        for copy in chunk_copies:
            copy.wait()

    (
        outgoing,
        selector,
        route,
        live,
        member,
        home,
        start_vector,
        basis,
        member_of,
        *coarse_chunks,
    ) = call(
        begin,
        [
            vmem((subs, (2 + sub_chunks) * widest + stat_rows, unknowns)),
            vmem((margin_rows, 2 * block_count), BF16),
            vmem((rounds * subs, LANES)),
            vmem((margin_rows, LANES)),
            vmem((block_count, LANES)),
            vmem((coarse_rows, LANES)),
            vmem(full),
            vmem(full),
            vmem((1, block_count), jnp.int32),
        ]
        + [vmem((chunk_rows, aggregates))] * parts,
        blocks,
        partner,
        margin_width,
        aggregate[0],
        right_side[0, 0],
        coarse_basis[0, 0],
        aggregate[0],
        coarse_inverse,
        name="begin",
        places="sssshhhh",
        scratch=[pltpu.SemaphoreType.DMA((3 + parts * sub_span,))],
    )
    for turn in range(1, parts):
        coarse_chunks[turn] = lax.ppermute(
            coarse_chunks[turn], "coarse", [(i, (i + turn) % parts) for i in range(parts)]
        )

    def put(target_value, values):
        high, low = split(values)
        pieces = [high, low]
        if table_rows > 2 * margin_rows:
            pieces.append(jnp.zeros((table_rows - 2 * margin_rows, unknowns), BF16))
        return dot_plain(target_value, jnp.concatenate(pieces, axis=0))

    def smooth_rest(arrived_ref, out, target, selector, route, part_ref, stat_ref, slot_ref, sum_ref):
        slots = spread_rounds(pick(selector, out), route, subs, rounds)
        statistic = stat_ref[0, widest : widest + stat_rows, :]
        if stat_rows < slot_rows:
            statistic = jnp.concatenate(
                [statistic, jnp.zeros((slot_rows - stat_rows, LANES), F32)], axis=0
            )
        for sub_id in range(subs):
            piece = slots[sub_id]
            if widest < slot_rows:
                piece = jnp.concatenate(
                    [piece, jnp.zeros((slot_rows - widest, unknowns), F32)], axis=0
                )
            for part_id in range(parts):
                slot_ref[sub_id * parts + part_id] = jnp.where(
                    part_ref[part_id : part_id + 1, :] > 0.5, piece, statistic
                )
        total = arrived_ref[0, widest : widest + stat_rows, :]
        for sub_id in range(1, subs):
            total = total + arrived_ref[sub_id, widest : widest + stat_rows, :]
        sum_ref[...] = total

    def arrived_rows(arrived_ref, at, route):
        return gather_rounds(
            [arrived_ref[sub_id, at : at + widest, :] for sub_id in range(subs)], route, rounds
        )

    def block_rows(shifted_ref, group):
        rows = pl.ds(pl.multiple_of(group * ROWS, ROWS), ROWS)
        return paired_rows(shifted_ref[rows, :])

    def block_product(left, weight_of):
        row = iota((ROWS, unknowns), 0)
        total = jnp.zeros((ROWS, unknowns), F32)
        for offset in range(ROWS // 2):
            both = dot_plain(left, weight_of(offset))
            both = both[:ROWS] + both[ROWS:]
            total = jnp.where(row == 2 * offset, both[:, :unknowns], total)
            total = jnp.where(row == 2 * offset + 1, both[:, unknowns:], total)
        return total

    def smooth_first(
        arrived_ref,
        vector_ref,
        selector_ref,
        route_ref,
        live_ref,
        member_of_ref,
        stat_ref,
        inverse_hbm,
        coupling_hbm,
        diagonal_hbm,
        link_hbm,
        *refs,
    ):
        (
            out_ref,
            slot_ref,
            sum_ref,
            basis_rows_ref,
            lane_rows_ref,
            weight_ref,
            pair_ref,
            target_ref,
            sub_member_ref,
            part_ref,
            diagonal_ref,
            link_ref,
            inverse_ref,
            coupling_ref,
            shifted_ref,
            semaphores,
            part_semaphores,
        ) = refs
        copies = [
            pltpu.make_async_copy(source, to, semaphores.at[position])
            for position, (source, to) in enumerate(
                [
                    (coupling_hbm, coupling_ref),
                    (diagonal_hbm, diagonal_ref),
                    (link_hbm, link_ref),
                ]
            )
        ]

        span = block_count // INVERSE_PARTS
        part_copies = [
            pltpu.make_async_copy(
                inverse_hbm.at[pl.ds(number * span, span)],
                inverse_ref.at[pl.ds(number * span, span)],
                part_semaphores.at[number],
            )
            for number in range(INVERSE_PARTS)
        ]
        for copy in copies + part_copies:
            copy.start()
        route = route_ref[...]
        table = selector_ref[:, 0:block_count].astype(F32)
        pieces = [table, table]
        if table_rows > 2 * margin_rows:
            pieces.append(jnp.zeros((table_rows - 2 * margin_rows, block_count), F32))
        table = jnp.concatenate(pieces, axis=0)
        target_ref[...] = jnp.concatenate(
            [table[start : start + LANES].T for start in range(0, table_rows, LANES)], axis=1
        ).astype(BF16)
        numbers = member_of_ref[...]
        own_lane = coarse_lane(numbers)
        for chunk in range(sub_chunks):
            sub_member_ref[:, chunk * LANES : (chunk + 1) * LANES] = hot(
                own_lane == iota((LANES, block_count), 0) + chunk * LANES
            ).T
        part_ref[...] = hot(((numbers >> own_bits) & (parts - 1)) == iota((ROWS, LANES), 0))
        at = widest + stat_rows
        basis_rows_ref[...] = arrived_rows(arrived_ref, at, route)
        for chunk in range(sub_chunks):
            at = at + widest
            lane_rows_ref[chunk] = arrived_rows(arrived_ref, at, route)
        copies[0].wait()
        for round_id in range(rounds):
            high, low = split(coupling_ref[round_id])
            pair_ref[round_id, :, 0:unknowns] = high
            pair_ref[round_id, :, unknowns : 2 * unknowns] = low
        mapped = couple(arrived_rows(arrived_ref, 0, route), pair_ref, live_ref[...])
        shifted_ref[...] = vector_ref[...] + put(target_ref[...], mapped)

        def step(group, carry):
            left = block_rows(shifted_ref, group)

            def weight_of(offset):
                pair = group * (ROWS // 2) + offset
                highs = []
                lows = []
                for position in range(2):
                    high, low = split(inverse_ref[pair * 2 + position].T)
                    lanes = slice(position * unknowns, (position + 1) * unknowns)
                    weight_ref[pair, 0:unknowns, lanes] = high
                    weight_ref[pair, unknowns : 2 * unknowns, lanes] = low
                    highs.append(high)
                    lows.append(low)
                return jnp.concatenate(
                    [jnp.concatenate(highs, axis=1), jnp.concatenate(lows, axis=1)], axis=0
                )

            rows = pl.ds(pl.multiple_of(group * ROWS, ROWS), ROWS)
            out_ref[rows, :] = block_product(left, weight_of)
            return carry

        groups = span // ROWS
        for number in range(INVERSE_PARTS):
            part_copies[number].wait()
            lax.fori_loop(number * groups, (number + 1) * groups, step, 0, unroll=2)
        for copy in copies[1:]:
            copy.wait()
        smooth_rest(
            arrived_ref,
            out_ref[...],
            target_ref[...],
            selector_ref[...],
            route,
            part_ref,
            stat_ref,
            slot_ref,
            sum_ref,
        )

    def smooth(
        arrived_ref,
        vector_ref,
        weight_ref,
        pair_ref,
        target_ref,
        selector_ref,
        route_ref,
        live_ref,
        part_ref,
        stat_ref,
        out_ref,
        slot_ref,
        sum_ref,
    ):
        route = route_ref[...]
        mapped = couple(arrived_rows(arrived_ref, 0, route), pair_ref, live_ref[...])
        shifted = vector_ref[...] + put(target_ref[...], mapped)
        pieces = []
        for group in range(block_count // ROWS):
            left = paired_rows(shifted[group * ROWS : (group + 1) * ROWS])
            pieces.append(
                block_product(left, lambda offset: weight_ref[group * (ROWS // 2) + offset])
            )
        out = jnp.concatenate(pieces, axis=0)
        out_ref[...] = out
        smooth_rest(
            arrived_ref,
            out,
            target_ref[...],
            selector_ref[...],
            route,
            part_ref,
            stat_ref,
            slot_ref,
            sum_ref,
        )

    def advance(step_id):
        first = step_id == 0
        last = step_id == ITERS - 1

        def kernel(*refs):
            (
                arrived_ref,
                sum_ref,
                smoothed_ref,
                vector_ref,
                sub_member_ref,
                member_ref,
                home_ref,
                basis_ref,
                basis_rows_ref,
                lane_rows_ref,
                pair_ref,
                target_ref,
                selector_ref,
                route_ref,
                live_ref,
                part_ref,
                diagonal_ref,
                link_ref,
            ) = refs[:18]
            coarse_refs = refs[18 : 18 + parts]
            outs = list(refs[18 + parts :])
            if first:
                state_ref = outs.pop()
            else:
                state_in = outs.pop(0)
                state_ref = outs.pop()

                def held(at, number, rows):
                    return state_in[at + number * rows : at + (number + 1) * rows, :]

            def keep(at, number, values):
                rows = values.shape[0]
                state_ref[at + number * rows : at + (number + 1) * rows, :] = values

            total = sum_ref[...]
            pieces = []
            for sub_id in range(subs):
                piece = jnp.zeros((widest, unknowns), F32)
                for part_id in range(parts):
                    slot = sub_id * parts + part_id
                    own = part_ref[part_id : part_id + 1, :] > 0.5
                    total = total + jnp.where(own, 0.0, arrived_ref[slot, 0:stat_rows, :])
                    piece = piece + jnp.where(own, arrived_ref[slot, 0:widest, :], 0.0)
                pieces.append(piece)
            products = jnp.sum(total[coarse_rows : coarse_rows + step_id + 1], axis=1, keepdims=True)
            heads = [products[i : i + 1] for i in range(step_id)]
            square = products[step_id : step_id + 1]
            remaining = square
            for head in heads:
                remaining = remaining - head * head
            length = jnp.sqrt(jnp.maximum(remaining, square * 1e-12))
            scale = 1.0 / length
            gathered = []
            for coarse_ref in coarse_refs:
                piece = coarse_ref[:, 0:LANES] * total[0:1]
                for chunk in range(1, coarse_rows):
                    piece = piece + (
                        coarse_ref[:, chunk * LANES : (chunk + 1) * LANES] * total[chunk : chunk + 1]
                    )
                gathered.append(piece)
            gathered = jnp.concatenate(gathered, axis=0)
            column = jnp.sum(gathered, axis=1, keepdims=True)
            same = iota((LANES, LANES), 0) == iota((LANES, LANES), 1)
            lines = [
                column_sum(jnp.where(same, column[start : start + LANES], 0.0))
                for start in range(0, sub_aggregates, LANES)
            ]
            own_coarse = sub_member_ref[:, 0:LANES] * lines[0]
            row_coarse = lane_rows_ref[0] * lines[0]
            for chunk in range(1, sub_chunks):
                own_coarse = own_coarse + (
                    sub_member_ref[:, chunk * LANES : (chunk + 1) * LANES] * lines[chunk]
                )
                row_coarse = row_coarse + lane_rows_ref[chunk] * lines[chunk]
            own_coarse = jnp.sum(own_coarse, axis=1, keepdims=True)
            row_coarse = jnp.sum(row_coarse, axis=1, keepdims=True)
            basis_value = basis_ref[...]
            direction = smoothed_ref[...] + own_coarse * basis_value
            for number, head in enumerate(heads):
                direction = direction - head * held(z_at, number, block_count)
            direction = direction * scale
            route = route_ref[...]
            rows = gather_rounds(pieces, route, rounds) + row_coarse * basis_rows_ref[...]
            for number, head in enumerate(heads):
                rows = rows - head * held(m_at, number, margin_rows)
            rows = rows * scale
            vector = vector_ref[...]
            earlier = [held(v_at, number, block_count) for number in range(step_id)]
            for head, other in zip(heads, earlier):
                vector = vector - head * other
            vector = vector * scale
            product = line_product(direction, diagonal_ref[...], link_ref[...]) - put(
                target_ref[...], couple(rows, pair_ref, live_ref[...])
            )
            against = earlier + [vector, product]
            if last:
                (slot_ref,) = outs
                block = statistics_block(
                    product, basis_value, member_ref[...], home_ref[...], against, ROWS, 0
                )
                for slot in range(devices):
                    slot_ref[slot] = block
            else:
                product_ref, slot_ref = outs
                keep(v_at, step_id, vector)
                keep(m_at, step_id, rows)
                product_ref[...] = product
                slots = spread_rounds(pick(selector_ref[...], product), route, subs, rounds)
                block = statistics_block(
                    product,
                    basis_value,
                    member_ref[...],
                    home_ref[...],
                    against,
                    stat_rows,
                    coarse_rows,
                )
                for sub_id in range(subs):
                    slot_ref[sub_id, 0:widest, :] = slots[sub_id]
                    slot_ref[sub_id, widest:, :] = block
            keep(z_at, step_id, direction)
            keep(
                head_at,
                step_id,
                jnp.broadcast_to(
                    jnp.concatenate(
                        heads + [length] + [jnp.zeros((ROWS - step_id - 1, 1), F32)], axis=0
                    ),
                    (ROWS, LANES),
                ),
            )

        return kernel

    vector = start_vector
    state = None
    state_shape = vmem((state_rows, LANES))
    for step_id in range(ITERS):
        first = step_id == 0
        last = step_id == ITERS - 1
        arrived = lax.all_to_all(outgoing, "sub", 0, 0)
        outs = [vmem(full), vmem((devices, slot_rows, unknowns)), vmem((stat_rows, LANES))]
        if first:
            (
                smoothed,
                slots,
                sums,
                basis_rows,
                lane_rows,
                weights,
                pairs,
                target,
                sub_member,
                part_table,
                diagonal_local,
                link_local,
            ) = call(
                smooth_first,
                outs
                + [
                    vmem((margin_rows, unknowns)),
                    vmem((sub_chunks, margin_rows, LANES)),
                    vmem((block_count // 2, 2 * unknowns, 2 * unknowns), BF16),
                    vmem((rounds, unknowns, 2 * unknowns), BF16),
                    vmem((block_count, table_rows), BF16),
                    vmem((block_count, sub_aggregates)),
                    vmem((ROWS, LANES)),
                    vmem(full),
                    vmem(full),
                ],
                arrived,
                vector,
                selector,
                route,
                live,
                member_of,
                outgoing,
                block_inverse[0, 0],
                coupling[0, 0],
                diagonal[0, 0],
                cell_link[0, 0],
                name="smooth0",
                places="vvvvvvvhhhh",
                scratch=[
                    vmem((block_count, unknowns, unknowns)),
                    vmem((rounds, unknowns, unknowns)),
                    vmem(full),
                    pltpu.SemaphoreType.DMA((3,)),
                    pltpu.SemaphoreType.DMA((INVERSE_PARTS,)),
                ],
            )
            slots, *coarse_chunks = lax.optimization_barrier((slots, *coarse_chunks))
        else:
            smoothed, slots, sums = call(
                smooth,
                outs,
                arrived,
                vector,
                weights,
                pairs,
                target,
                selector,
                route,
                live,
                part_table,
                outgoing,
                name=f"smooth{step_id}",
            )
        arrived = lax.all_to_all(slots, ("sub", "coarse"), 0, 0)
        if last:
            outs = [vmem((devices, ROWS, LANES)), state_shape]
        else:
            outs = [vmem(full), vmem((subs, widest + stat_rows, unknowns)), state_shape]
        made = call(
            advance(step_id),
            outs,
            arrived,
            sums,
            smoothed,
            vector,
            sub_member,
            member,
            home,
            basis,
            basis_rows,
            lane_rows,
            pairs,
            target,
            selector,
            route,
            live,
            part_table,
            diagonal_local,
            link_local,
            *coarse_chunks,
            *([] if first else [state]),
            name=f"advance{step_id}",
            aliases={} if first else {18 + parts: len(outs) - 1},
        )
        if last:
            slots, state = made
        else:
            vector, outgoing, state = made
    arrived = lax.all_to_all(slots, ("sub", "coarse"), 0, 0)

    def finish(arrived_ref, state_ref, out_ref):
        total = arrived_ref[0]
        for slot in range(1, devices):
            total = total + arrived_ref[slot]
        products = jnp.sum(total, axis=1, keepdims=True)
        heads = [products[i : i + 1] for i in range(ITERS)]
        square = products[ITERS : ITERS + 1]
        remaining = square
        for head in heads:
            remaining = remaining - head * head
        length = jnp.sqrt(jnp.maximum(remaining, square * 1e-12))
        beta = state_ref[head_at : head_at + 1, 0:1]
        columns = []
        for column_id in range(1, ITERS):
            at = head_at + column_id * ROWS
            columns.append([state_ref[at + i : at + i + 1, 0:1] for i in range(column_id + 1)])
        columns.append(heads + [length])
        weights_found = givens_solve(columns, beta)
        result = weights_found[0] * state_ref[z_at : z_at + block_count, :]
        for position in range(1, ITERS):
            at = z_at + position * block_count
            result = result + weights_found[position] * state_ref[at : at + block_count, :]
        out_ref[...] = result

    (answer,) = call(finish, [jax.ShapeDtypeStruct(full, F32)], arrived, state, name="finish")
    return answer.reshape(right_side.shape)


def givens_solve(columns, beta):
    steps_count = len(columns)
    cosines = []
    sines = []
    side_terms = [beta] + [jnp.zeros_like(beta) for unused in range(steps_count)]
    triangle = []
    for column_id in range(steps_count):
        column = list(columns[column_id])
        for row_id in range(column_id):
            upper = column[row_id]
            lower = column[row_id + 1]
            column[row_id] = cosines[row_id] * upper + sines[row_id] * lower
            column[row_id + 1] = cosines[row_id] * lower - sines[row_id] * upper
        upper = column[column_id]
        lower = column[column_id + 1]
        radius = jnp.sqrt(upper * upper + lower * lower)
        cosine = upper / radius
        sine_value = lower / radius
        column[column_id] = radius
        cosines.append(cosine)
        sines.append(sine_value)
        side_terms[column_id + 1] = -sine_value * side_terms[column_id]
        side_terms[column_id] = cosine * side_terms[column_id]
        triangle.append(column)
    weights = [None] * steps_count
    for column_id in reversed(range(steps_count)):
        running = side_terms[column_id]
        for later_col in range(column_id + 1, steps_count):
            running = running - triangle[later_col][column_id] * weights[later_col]
        weights[column_id] = running / triangle[column_id][column_id]
    return weights


def solution(mesh):
    placed = (
        P("sub", "coarse", None, None),
        P("sub", "coarse", None, None),
        P("sub", "coarse", None, None),
        P("sub", "coarse", None, None, None),
        P("sub", "coarse", None, None, None),
        P("sub", "coarse", None, None),
        P("coarse", None),
        P("sub", None),
        P("sub", None),
        P("sub", "coarse", None, None),
        P("sub", "coarse", None),
    )
    return jax.shard_map(
        on_device,
        mesh=mesh,
        in_specs=placed,
        out_specs=P("sub", "coarse", None, None),
        check_vma=False,
    )
```

```python
import jax
import jax.numpy as jnp
from jax import lax
from jax.experimental import pallas as pl
from jax.experimental.pallas import tpu as pltpu
from jax.sharding import PartitionSpec as P

BS = 128
BPD = 128
AGG_DEV = 16
ITERS = 4
LANES = 128
ROWS = 8
INVERSE_PARTS = 4
DIRECT_GROUPS = 4
BF16 = jnp.bfloat16
F32 = jnp.float32


def split(values):
    high = values.astype(BF16)
    low = (values - high.astype(F32)).astype(BF16)
    return high, low


def dot_rows(left, right):
    return lax.dot_general(left, right, (((1,), (1,)), ((), ())), preferred_element_type=F32)


def dot_plain(left, right):
    return lax.dot_general(left, right, (((1,), (0,)), ((), ())), preferred_element_type=F32)


def paired_rows(values):
    high, low = split(values)
    return jnp.concatenate(
        [
            jnp.concatenate([high, high], axis=1),
            jnp.concatenate([low, jnp.zeros_like(low)], axis=1),
        ],
        axis=0,
    )


def pick(selector, values):
    high, low = split(values)
    return dot_plain(selector, jnp.concatenate([high, low], axis=0))


def column_sum(values):
    return jnp.sum(values, axis=0, keepdims=True)


def line_product(values, diagonal, link):
    rows = values.shape[0]
    lanes = values.shape[1]
    row = lax.broadcasted_iota(jnp.int32, values.shape, 0)
    lane = lax.broadcasted_iota(jnp.int32, values.shape, 1)
    next_lane = pltpu.roll(values, lanes - 1, 1)
    next_row = pltpu.roll(next_lane, rows - 1, 0)
    ahead = jnp.where(lane < lanes - 1, next_lane, jnp.where(row < rows - 1, next_row, 0.0))
    scaled = link * values
    last_lane = pltpu.roll(scaled, 1, 1)
    last_row = pltpu.roll(last_lane, 1, 0)
    behind = jnp.where(lane > 0, last_lane, jnp.where(row > 0, last_row, 0.0))
    return diagonal * values - (ahead * link + behind)


def couple(arrived, pair_ref, live):
    rounds = pair_ref.shape[0]
    widest = arrived.shape[0] // rounds
    pieces = []
    for round_id in range(rounds):
        left = paired_rows(arrived[round_id * widest : (round_id + 1) * widest])
        both = dot_rows(left, pair_ref[round_id])
        pieces.append(both[:widest] + both[widest:])
    return jnp.concatenate(pieces, axis=0) * live


def gather_rounds(slots, route, rounds):
    pieces = []
    for round_id in range(rounds):
        total = None
        for sub_id, piece in enumerate(slots):
            at = round_id * len(slots) + sub_id
            term = route[at : at + 1] * piece
            total = term if total is None else total + term
        pieces.append(total)
    return jnp.concatenate(pieces, axis=0)


def spread_rounds(values, route, subs, rounds):
    widest = values.shape[0] // rounds
    slots = []
    for sub_id in range(subs):
        total = None
        for round_id in range(rounds):
            at = round_id * subs + sub_id
            term = route[at : at + 1] * values[round_id * widest : (round_id + 1) * widest]
            total = term if total is None else total + term
        slots.append(total)
    return slots


def vmem(shape, dtype=F32):
    return pltpu.VMEM(shape, dtype)


def call(kernel, outs, *args, name, places="", aliases=None, scratch=()):
    places = places + "v" * (len(args) - len(places))
    spaces = {"s": pltpu.SMEM, "h": pltpu.HBM, "v": pltpu.VMEM}
    return pl.pallas_call(
        kernel,
        out_shape=outs,
        in_specs=[pl.BlockSpec(memory_space=spaces[place]) for place in places],
        out_specs=[pl.BlockSpec(memory_space=pltpu.VMEM)] * len(outs),
        input_output_aliases=aliases or {},
        scratch_shapes=list(scratch),
        name=name,
        compiler_params=pltpu.CompilerParams(vmem_limit_bytes=16 * 1024 * 1024),
    )(
        *[
            pltpu.with_memory_space_constraint(
                arg, pltpu.VMEM if place == "v" else pltpu.HBM
            )
            for arg, place in zip(args, places)
        ]
    )


def on_device(
    right_side,
    diagonal,
    cell_link,
    block_inverse,
    coupling,
    coarse_basis,
    coarse_inverse,
    partner,
    margin_width,
    margin_blocks,
    aggregate,
):
    subs = lax.axis_size("sub")
    parts = lax.axis_size("coarse")
    devices = subs * parts
    block_count = right_side.shape[2]
    unknowns = right_side.shape[3]
    rounds = margin_blocks.shape[2]
    widest = margin_blocks.shape[3]
    aggregates = coarse_inverse.shape[1]
    own_aggregates = aggregates // devices
    sub_aggregates = subs * own_aggregates
    sub_chunks = sub_aggregates // LANES
    sub_span = subs // parts
    chunk_rows = sub_span * own_aggregates
    factor = (BS * BPD / AGG_DEV) ** (-0.5)
    coarse_rows = aggregates // LANES
    stat_rows = -(-(coarse_rows + ITERS) // ROWS) * ROWS
    slot_rows = max(widest, stat_rows)
    margin_rows = rounds * widest
    table_rows = -(-2 * margin_rows // LANES) * LANES
    full = (block_count, unknowns)
    direct_blocks = DIRECT_GROUPS * ROWS
    paired_blocks = block_count - direct_blocks

    v_at = 0
    z_at = v_at + (ITERS - 1) * block_count
    m_at = z_at + ITERS * block_count
    head_at = m_at + (ITERS - 1) * margin_rows
    state_rows = head_at + ITERS * ROWS
    blocks = margin_blocks[0, 0]
    member_of = aggregate[0]
    own_bits = own_aggregates.bit_length() - 1
    part_bits = parts.bit_length() - 1
    span_bits = sub_span.bit_length() - 1
    lane_bits = LANES.bit_length() - 1
    assert own_aggregates == 1 << own_bits and parts == 1 << part_bits
    assert sub_span == 1 << span_bits and sub_span * parts == subs

    def iota(shape, dim):
        return lax.broadcasted_iota(jnp.int32, shape, dim)

    def hot(condition):
        return jnp.where(condition, 1.0, 0.0).astype(F32)

    def coarse_lane(numbers):
        own_device = numbers >> own_bits
        own_part = own_device & (parts - 1)
        own_sub = own_device >> part_bits
        turn = (own_part - (own_sub >> span_bits)) & (parts - 1)
        return (
            turn * chunk_rows
            + (own_sub & (sub_span - 1)) * own_aggregates
            + (numbers & (own_aggregates - 1))
        )

    def statistics_block(vector, basis_value, member_value, home, dots, rows, count):
        inner = jnp.sum(basis_value * vector, axis=1, keepdims=True)
        line = column_sum(inner * member_value) * factor
        lines = [home[chunk : chunk + 1] * line for chunk in range(count)]
        lines += [column_sum(other * vector) for other in dots]
        if len(lines) < rows:
            lines.append(jnp.zeros((rows - len(lines), LANES), F32))
        return jnp.concatenate(lines, axis=0)

    def begin(
        blocks_hbm,
        partner_hbm,
        width_hbm,
        start_hbm,
        basis_hbm,
        member_of_hbm,
        coarse_hbm,
        *refs,
    ):
        (
            slot_ref,
            selector_ref,
            route_ref,
            live_ref,
            member_ref,
            home_ref,
            start_ref,
            basis_ref,
            member_of_ref,
        ) = refs[:9]
        chunk_refs = refs[9 : 9 + parts]
        (
            blocks_ref,
            partner_ref,
            width_ref,
            number_ref,
            held_ref,
            semaphores,
            scalar_semaphores,
        ) = refs[9 + parts :]
        scalar_copies = [
            pltpu.make_async_copy(source, to, scalar_semaphores.at[position])
            for position, (source, to) in enumerate(
                [
                    (member_of_hbm, number_ref),
                    (blocks_hbm, blocks_ref),
                    (partner_hbm, partner_ref),
                    (width_hbm, width_ref),
                ]
            )
        ]
        copies = [
            pltpu.make_async_copy(source, to, semaphores.at[position])
            for position, (source, to) in enumerate(
                [(start_hbm, start_ref), (basis_hbm, basis_ref), (member_of_hbm, member_of_ref)]
            )
        ]
        held_copies = [
            pltpu.make_async_copy(
                coarse_hbm.at[
                    pl.ds((span * parts + part_id) * own_aggregates, own_aggregates), :
                ],
                held_ref.at[part_id, pl.ds(span * own_aggregates, own_aggregates), :],
                semaphores.at[3 + span * parts + part_id],
            )
            for span in range(sub_span)
            for part_id in range(parts)
        ]
        for copy in scalar_copies + copies + held_copies:
            copy.start()
        for copy in scalar_copies:
            copy.wait()
        own_part = (number_ref[0, 0] >> own_bits) & (parts - 1)
        row = iota((widest, LANES), 0)
        lane = iota((widest, LANES), 1)
        tables = []
        for round_id in range(rounds):
            wanted = jnp.zeros((widest, LANES), jnp.int32)
            for position in range(widest):
                wanted = jnp.where(row == position, blocks_ref[round_id, position], wanted)
            tables.append(hot(lane == wanted))
            live_ref[round_id * widest : (round_id + 1) * widest, :] = hot(
                row < width_ref[0, round_id]
            )
            sub_row = iota((subs, LANES), 0)
            route_ref[round_id * subs : (round_id + 1) * subs, :] = hot(
                sub_row == partner_ref[0, round_id]
            )
        for copy in copies:
            copy.wait()
        start = start_ref[...]
        basis_value = basis_ref[...]
        numbers = member_of_ref[...]
        table = jnp.concatenate(tables, axis=0)
        table = jnp.concatenate([table, table], axis=1).astype(BF16)
        selector_ref[...] = table
        route = route_ref[...]
        member = hot((numbers & (LANES - 1)) == iota((LANES, block_count), 0)).T
        member_ref[...] = member
        home = hot((numbers >> lane_bits) == iota((coarse_rows, LANES), 0))
        home_ref[...] = home
        own_lane = coarse_lane(numbers)
        rows_start = spread_rounds(pick(table, start), route, subs, rounds)
        rows_basis = spread_rounds(pick(table, basis_value), route, subs, rounds)
        rows_lane = []
        for chunk in range(sub_chunks):
            lane_table = hot(own_lane == iota((LANES, block_count), 0) + chunk * LANES)
            rows_lane.append(
                spread_rounds(
                    dot_rows(table[:, :block_count], lane_table.astype(BF16)), route, subs, rounds
                )
            )
        statistic = statistics_block(
            start, basis_value, member, home, [start], stat_rows, coarse_rows
        )
        for sub_id in range(subs):
            slot_ref[sub_id, 0:widest, :] = rows_start[sub_id]
            slot_ref[sub_id, widest : widest + stat_rows, :] = statistic
            at = widest + stat_rows
            slot_ref[sub_id, at : at + widest, :] = rows_basis[sub_id]
            for chunk in range(sub_chunks):
                at = at + widest
                slot_ref[sub_id, at : at + widest, :] = rows_lane[chunk][sub_id]
        for copy in held_copies:
            copy.wait()
        for turn, chunk_ref in enumerate(chunk_refs):
            chunk_ref[...] = held_ref[(own_part + turn) & (parts - 1)]

    (
        outgoing,
        selector,
        route,
        live,
        member,
        home,
        start_vector,
        basis,
        member_of,
        *coarse_chunks,
    ) = call(
        begin,
        [
            vmem((subs, (2 + sub_chunks) * widest + stat_rows, unknowns)),
            vmem((margin_rows, 2 * block_count), BF16),
            vmem((rounds * subs, LANES)),
            vmem((margin_rows, LANES)),
            vmem((block_count, LANES)),
            vmem((coarse_rows, LANES)),
            vmem(full),
            vmem(full),
            vmem((1, block_count), jnp.int32),
        ]
        + [vmem((chunk_rows, aggregates))] * parts,
        blocks,
        partner,
        margin_width,
        right_side[0, 0],
        coarse_basis[0, 0],
        aggregate[0],
        coarse_inverse,
        name="begin",
        places="hhhhhhh",
        scratch=[
            pltpu.SMEM((rounds, widest), jnp.int32),
            pltpu.SMEM((1, rounds), jnp.int32),
            pltpu.SMEM((1, rounds), jnp.int32),
            pltpu.SMEM((1, block_count), jnp.int32),
            vmem((parts, chunk_rows, aggregates)),
            pltpu.SemaphoreType.DMA((3 + parts * sub_span,)),
            pltpu.SemaphoreType.DMA((4,)),
        ],
    )
    for turn in range(1, parts):
        coarse_chunks[turn] = lax.ppermute(
            coarse_chunks[turn], "coarse", [(i, (i + turn) % parts) for i in range(parts)]
        )

    def put(target_value, values):
        high, low = split(values)
        pieces = [high, low]
        if table_rows > 2 * margin_rows:
            pieces.append(jnp.zeros((table_rows - 2 * margin_rows, unknowns), BF16))
        return dot_plain(target_value, jnp.concatenate(pieces, axis=0))

    def smooth_rest(arrived_ref, out, target, selector, route, part_ref, stat_ref, slot_ref, sum_ref):
        slots = spread_rounds(pick(selector, out), route, subs, rounds)
        statistic = stat_ref[0, widest : widest + stat_rows, :]
        if stat_rows < slot_rows:
            statistic = jnp.concatenate(
                [statistic, jnp.zeros((slot_rows - stat_rows, LANES), F32)], axis=0
            )
        for sub_id in range(subs):
            piece = slots[sub_id]
            if widest < slot_rows:
                piece = jnp.concatenate(
                    [piece, jnp.zeros((slot_rows - widest, unknowns), F32)], axis=0
                )
            for part_id in range(parts):
                slot_ref[sub_id * parts + part_id] = jnp.where(
                    part_ref[part_id : part_id + 1, :] > 0.5, piece, statistic
                )
        total = arrived_ref[0, widest : widest + stat_rows, :]
        for sub_id in range(1, subs):
            total = total + arrived_ref[sub_id, widest : widest + stat_rows, :]
        sum_ref[...] = total

    def arrived_rows(arrived_ref, at, route):
        return gather_rounds(
            [arrived_ref[sub_id, at : at + widest, :] for sub_id in range(subs)], route, rounds
        )

    def block_rows(shifted_ref, group):
        rows = pl.ds(pl.multiple_of(group * ROWS, ROWS), ROWS)
        return paired_rows(shifted_ref[rows, :])

    def direct_product(values, blocks_at):
        lines = []
        for offset in range(ROWS):
            scaled = blocks_at(offset) * values[offset : offset + 1, :]
            lines.append(jnp.sum(scaled, axis=1)[None, :])
        return jnp.concatenate(lines, axis=0)

    def block_product(left, weight_of):
        row = iota((ROWS, unknowns), 0)
        total = jnp.zeros((ROWS, unknowns), F32)
        for offset in range(ROWS // 2):
            both = dot_plain(left, weight_of(offset))
            both = both[:ROWS] + both[ROWS:]
            total = jnp.where(row == 2 * offset, both[:, :unknowns], total)
            total = jnp.where(row == 2 * offset + 1, both[:, unknowns:], total)
        return total

    def smooth_first(
        arrived_ref,
        vector_ref,
        selector_ref,
        route_ref,
        live_ref,
        member_of_ref,
        stat_ref,
        inverse_hbm,
        coupling_hbm,
        diagonal_hbm,
        link_hbm,
        *refs,
    ):
        (
            out_ref,
            slot_ref,
            sum_ref,
            basis_rows_ref,
            lane_rows_ref,
            weight_ref,
            direct_ref,
            pair_ref,
            target_ref,
            sub_member_ref,
            part_ref,
            diagonal_ref,
            link_ref,
            inverse_ref,
            coupling_ref,
            shifted_ref,
            semaphores,
            part_semaphores,
        ) = refs
        copies = [
            pltpu.make_async_copy(source, to, semaphores.at[position])
            for position, (source, to) in enumerate(
                [
                    (coupling_hbm, coupling_ref),
                    (diagonal_hbm, diagonal_ref),
                    (link_hbm, link_ref),
                ]
            )
        ]

        span = paired_blocks // INVERSE_PARTS
        direct_span = direct_blocks // INVERSE_PARTS
        direct_copies = [
            pltpu.make_async_copy(
                inverse_hbm.at[pl.ds(number * direct_span, direct_span)],
                direct_ref.at[pl.ds(number * direct_span, direct_span)],
                semaphores.at[3 + number],
            )
            for number in range(INVERSE_PARTS)
        ]
        part_copies = [
            pltpu.make_async_copy(
                inverse_hbm.at[pl.ds(direct_blocks + number * span, span)],
                inverse_ref.at[pl.ds(number * span, span)],
                part_semaphores.at[number],
            )
            for number in range(INVERSE_PARTS)
        ]
        for copy in copies:
            copy.start()
        for number in range(INVERSE_PARTS):
            direct_copies[number].start()
            part_copies[number].start()
        route = route_ref[...]
        table = selector_ref[:, 0:block_count].astype(F32)
        pieces = [table, table]
        if table_rows > 2 * margin_rows:
            pieces.append(jnp.zeros((table_rows - 2 * margin_rows, block_count), F32))
        table = jnp.concatenate(pieces, axis=0)
        target_ref[...] = jnp.concatenate(
            [table[start : start + LANES].T for start in range(0, table_rows, LANES)], axis=1
        ).astype(BF16)
        numbers = member_of_ref[...]
        own_lane = coarse_lane(numbers)
        for chunk in range(sub_chunks):
            sub_member_ref[:, chunk * LANES : (chunk + 1) * LANES] = hot(
                own_lane == iota((LANES, block_count), 0) + chunk * LANES
            ).T
        part_ref[...] = hot(((numbers >> own_bits) & (parts - 1)) == iota((ROWS, LANES), 0))
        at = widest + stat_rows
        basis_rows_ref[...] = arrived_rows(arrived_ref, at, route)
        for chunk in range(sub_chunks):
            at = at + widest
            lane_rows_ref[chunk] = arrived_rows(arrived_ref, at, route)
        copies[0].wait()
        for round_id in range(rounds):
            high, low = split(coupling_ref[round_id])
            pair_ref[round_id, :, 0:unknowns] = high
            pair_ref[round_id, :, unknowns : 2 * unknowns] = low
        mapped = couple(arrived_rows(arrived_ref, 0, route), pair_ref, live_ref[...])
        shifted_ref[...] = vector_ref[...] + put(target_ref[...], mapped)

        paired_groups = (block_count // ROWS - DIRECT_GROUPS) // DIRECT_GROUPS

        def paired_step(group):
            left = block_rows(shifted_ref, group)

            def weight_of(offset):
                pair = (group - DIRECT_GROUPS) * (ROWS // 2) + offset
                highs = []
                lows = []
                for position in range(2):
                    high, low = split(inverse_ref[pair * 2 + position].T)
                    lanes = slice(position * unknowns, (position + 1) * unknowns)
                    weight_ref[pair, 0:unknowns, lanes] = high
                    weight_ref[pair, unknowns : 2 * unknowns, lanes] = low
                    highs.append(high)
                    lows.append(low)
                return jnp.concatenate(
                    [jnp.concatenate(highs, axis=1), jnp.concatenate(lows, axis=1)], axis=0
                )

            rows = pl.ds(pl.multiple_of(group * ROWS, ROWS), ROWS)
            out_ref[rows, :] = block_product(left, weight_of)

        def step(unit, carry):
            rows = pl.ds(pl.multiple_of(unit * ROWS, ROWS), ROWS)
            out_ref[rows, :] = direct_product(
                shifted_ref[rows, :], lambda offset: direct_ref[unit * ROWS + offset]
            )
            for number in range(paired_groups):
                paired_step(DIRECT_GROUPS + unit * paired_groups + number)
            return carry

        units = DIRECT_GROUPS // INVERSE_PARTS
        for number in range(INVERSE_PARTS):
            direct_copies[number].wait()
            part_copies[number].wait()
            lax.fori_loop(number * units, (number + 1) * units, step, 0, unroll=1)
        for copy in copies[1:]:
            copy.wait()
        smooth_rest(
            arrived_ref,
            out_ref[...],
            target_ref[...],
            selector_ref[...],
            route,
            part_ref,
            stat_ref,
            slot_ref,
            sum_ref,
        )

    def smooth(
        arrived_ref,
        vector_ref,
        weight_ref,
        direct_ref,
        pair_ref,
        target_ref,
        selector_ref,
        route_ref,
        live_ref,
        part_ref,
        stat_ref,
        out_ref,
        slot_ref,
        sum_ref,
    ):
        route = route_ref[...]
        mapped = couple(arrived_rows(arrived_ref, 0, route), pair_ref, live_ref[...])
        shifted = vector_ref[...] + put(target_ref[...], mapped)
        pieces = []
        for group in range(block_count // ROWS):
            values = shifted[group * ROWS : (group + 1) * ROWS]
            if group < DIRECT_GROUPS:
                piece = direct_product(values, lambda offset: direct_ref[group * ROWS + offset])
            else:
                at = (group - DIRECT_GROUPS) * (ROWS // 2)
                piece = block_product(
                    paired_rows(values), lambda offset: weight_ref[at + offset]
                )
            pieces.append(piece)
        out = jnp.concatenate(pieces, axis=0)
        out_ref[...] = out
        smooth_rest(
            arrived_ref,
            out,
            target_ref[...],
            selector_ref[...],
            route,
            part_ref,
            stat_ref,
            slot_ref,
            sum_ref,
        )

    def advance(step_id):
        first = step_id == 0
        last = step_id == ITERS - 1

        def kernel(*refs):
            (
                arrived_ref,
                sum_ref,
                smoothed_ref,
                vector_ref,
                sub_member_ref,
                member_ref,
                home_ref,
                basis_ref,
                basis_rows_ref,
                lane_rows_ref,
                pair_ref,
                target_ref,
                selector_ref,
                route_ref,
                live_ref,
                part_ref,
                diagonal_ref,
                link_ref,
            ) = refs[:18]
            coarse_refs = refs[18 : 18 + parts]
            outs = list(refs[18 + parts :])
            if first:
                state_ref = outs.pop()
            else:
                state_in = outs.pop(0)
                state_ref = outs.pop()

                def held(at, number, rows):
                    return state_in[at + number * rows : at + (number + 1) * rows, :]

            def keep(at, number, values):
                rows = values.shape[0]
                state_ref[at + number * rows : at + (number + 1) * rows, :] = values

            total = sum_ref[...]
            pieces = []
            for sub_id in range(subs):
                piece = jnp.zeros((widest, unknowns), F32)
                for part_id in range(parts):
                    slot = sub_id * parts + part_id
                    own = part_ref[part_id : part_id + 1, :] > 0.5
                    total = total + jnp.where(own, 0.0, arrived_ref[slot, 0:stat_rows, :])
                    piece = piece + jnp.where(own, arrived_ref[slot, 0:widest, :], 0.0)
                pieces.append(piece)
            products = jnp.sum(total[coarse_rows : coarse_rows + step_id + 1], axis=1, keepdims=True)
            heads = [products[i : i + 1] for i in range(step_id)]
            square = products[step_id : step_id + 1]
            remaining = square
            for head in heads:
                remaining = remaining - head * head
            length = jnp.sqrt(jnp.maximum(remaining, square * 1e-12))
            scale = 1.0 / length
            gathered = []
            for coarse_ref in coarse_refs:
                piece = coarse_ref[:, 0:LANES] * total[0:1]
                for chunk in range(1, coarse_rows):
                    piece = piece + (
                        coarse_ref[:, chunk * LANES : (chunk + 1) * LANES] * total[chunk : chunk + 1]
                    )
                gathered.append(piece)
            gathered = jnp.concatenate(gathered, axis=0)
            column = jnp.sum(gathered, axis=1, keepdims=True)
            same = iota((LANES, LANES), 0) == iota((LANES, LANES), 1)
            lines = [
                column_sum(jnp.where(same, column[start : start + LANES], 0.0))
                for start in range(0, sub_aggregates, LANES)
            ]
            own_coarse = sub_member_ref[:, 0:LANES] * lines[0]
            row_coarse = lane_rows_ref[0] * lines[0]
            for chunk in range(1, sub_chunks):
                own_coarse = own_coarse + (
                    sub_member_ref[:, chunk * LANES : (chunk + 1) * LANES] * lines[chunk]
                )
                row_coarse = row_coarse + lane_rows_ref[chunk] * lines[chunk]
            own_coarse = jnp.sum(own_coarse, axis=1, keepdims=True)
            row_coarse = jnp.sum(row_coarse, axis=1, keepdims=True)
            basis_value = basis_ref[...]
            direction = smoothed_ref[...] + own_coarse * basis_value
            for number, head in enumerate(heads):
                direction = direction - head * held(z_at, number, block_count)
            direction = direction * scale
            route = route_ref[...]
            rows = gather_rounds(pieces, route, rounds) + row_coarse * basis_rows_ref[...]
            for number, head in enumerate(heads):
                rows = rows - head * held(m_at, number, margin_rows)
            rows = rows * scale
            vector = vector_ref[...]
            earlier = [held(v_at, number, block_count) for number in range(step_id)]
            for head, other in zip(heads, earlier):
                vector = vector - head * other
            vector = vector * scale
            product = line_product(direction, diagonal_ref[...], link_ref[...]) - put(
                target_ref[...], couple(rows, pair_ref, live_ref[...])
            )
            against = earlier + [vector, product]
            if last:
                (slot_ref,) = outs
                lane = iota((1, LANES), 1)
                block = jnp.zeros((1, LANES), F32)
                for position, other in enumerate(against):
                    value = jnp.sum(column_sum(other * product), axis=1, keepdims=True)
                    block = jnp.where(lane == position, value, block)
                for slot in range(devices):
                    slot_ref[slot] = block
            else:
                product_ref, slot_ref = outs
                keep(v_at, step_id, vector)
                keep(m_at, step_id, rows)
                product_ref[...] = product
                slots = spread_rounds(pick(selector_ref[...], product), route, subs, rounds)
                block = statistics_block(
                    product,
                    basis_value,
                    member_ref[...],
                    home_ref[...],
                    against,
                    stat_rows,
                    coarse_rows,
                )
                for sub_id in range(subs):
                    slot_ref[sub_id, 0:widest, :] = slots[sub_id]
                    slot_ref[sub_id, widest:, :] = block
            keep(z_at, step_id, direction)
            keep(
                head_at,
                step_id,
                jnp.broadcast_to(
                    jnp.concatenate(
                        heads + [length] + [jnp.zeros((ROWS - step_id - 1, 1), F32)], axis=0
                    ),
                    (ROWS, LANES),
                ),
            )

        return kernel

    vector = start_vector
    state = None
    state_shape = vmem((state_rows, LANES))
    for step_id in range(ITERS):
        first = step_id == 0
        last = step_id == ITERS - 1
        arrived = lax.all_to_all(outgoing, "sub", 0, 0)
        outs = [vmem(full), vmem((devices, slot_rows, unknowns)), vmem((stat_rows, LANES))]
        if first:
            (
                smoothed,
                slots,
                sums,
                basis_rows,
                lane_rows,
                weights,
                direct,
                pairs,
                target,
                sub_member,
                part_table,
                diagonal_local,
                link_local,
            ) = call(
                smooth_first,
                outs
                + [
                    vmem((margin_rows, unknowns)),
                    vmem((sub_chunks, margin_rows, LANES)),
                    vmem((paired_blocks // 2, 2 * unknowns, 2 * unknowns), BF16),
                    vmem((direct_blocks, unknowns, unknowns)),
                    vmem((rounds, unknowns, 2 * unknowns), BF16),
                    vmem((block_count, table_rows), BF16),
                    vmem((block_count, sub_aggregates)),
                    vmem((ROWS, LANES)),
                    vmem(full),
                    vmem(full),
                ],
                arrived,
                vector,
                selector,
                route,
                live,
                member_of,
                outgoing,
                block_inverse[0, 0],
                coupling[0, 0],
                diagonal[0, 0],
                cell_link[0, 0],
                name="smooth0",
                places="vvvvvvvhhhh",
                scratch=[
                    vmem((paired_blocks, unknowns, unknowns)),
                    vmem((rounds, unknowns, unknowns)),
                    vmem(full),
                    pltpu.SemaphoreType.DMA((3 + INVERSE_PARTS,)),
                    pltpu.SemaphoreType.DMA((INVERSE_PARTS,)),
                ],
            )
            slots, *coarse_chunks = lax.optimization_barrier((slots, *coarse_chunks))
        else:
            smoothed, slots, sums = call(
                smooth,
                outs,
                arrived,
                vector,
                weights,
                direct,
                pairs,
                target,
                selector,
                route,
                live,
                part_table,
                outgoing,
                name=f"smooth{step_id}",
            )
        arrived = lax.all_to_all(slots, ("sub", "coarse"), 0, 0)
        if last:
            outs = [vmem((devices, 1, LANES)), state_shape]
        else:
            outs = [vmem(full), vmem((subs, widest + stat_rows, unknowns)), state_shape]
        made = call(
            advance(step_id),
            outs,
            arrived,
            sums,
            smoothed,
            vector,
            sub_member,
            member,
            home,
            basis,
            basis_rows,
            lane_rows,
            pairs,
            target,
            selector,
            route,
            live,
            part_table,
            diagonal_local,
            link_local,
            *coarse_chunks,
            *([] if first else [state]),
            name=f"advance{step_id}",
            aliases={} if first else {18 + parts: len(outs) - 1},
        )
        if last:
            slots, state = made
        else:
            vector, outgoing, state = made
    arrived = lax.all_to_all(slots, ("sub", "coarse"), 0, 0)

    def finish(arrived_ref, state_ref, out_ref):
        total = column_sum(arrived_ref[...].reshape(devices, LANES))
        heads = [total[:, i : i + 1] for i in range(ITERS)]
        square = total[:, ITERS : ITERS + 1]
        remaining = square
        for head in heads:
            remaining = remaining - head * head
        length = jnp.sqrt(jnp.maximum(remaining, square * 1e-12))
        beta = state_ref[head_at : head_at + 1, 0:1]
        columns = []
        for column_id in range(1, ITERS):
            at = head_at + column_id * ROWS
            columns.append([state_ref[at + i : at + i + 1, 0:1] for i in range(column_id + 1)])
        columns.append(heads + [length])
        weights_found = givens_solve(columns, beta)
        result = weights_found[0] * state_ref[z_at : z_at + block_count, :]
        for position in range(1, ITERS):
            at = z_at + position * block_count
            result = result + weights_found[position] * state_ref[at : at + block_count, :]
        out_ref[...] = result

    (answer,) = call(finish, [jax.ShapeDtypeStruct(full, F32)], arrived, state, name="finish")
    return answer.reshape(right_side.shape)


def givens_solve(columns, beta):
    steps_count = len(columns)
    cosines = []
    sines = []
    side_terms = [beta] + [jnp.zeros_like(beta) for unused in range(steps_count)]
    triangle = []
    for column_id in range(steps_count):
        column = list(columns[column_id])
        for row_id in range(column_id):
            upper = column[row_id]
            lower = column[row_id + 1]
            column[row_id] = cosines[row_id] * upper + sines[row_id] * lower
            column[row_id + 1] = cosines[row_id] * lower - sines[row_id] * upper
        upper = column[column_id]
        lower = column[column_id + 1]
        radius = jnp.sqrt(upper * upper + lower * lower)
        cosine = upper / radius
        sine_value = lower / radius
        column[column_id] = radius
        cosines.append(cosine)
        sines.append(sine_value)
        side_terms[column_id + 1] = -sine_value * side_terms[column_id]
        side_terms[column_id] = cosine * side_terms[column_id]
        triangle.append(column)
    weights = [None] * steps_count
    for column_id in reversed(range(steps_count)):
        running = side_terms[column_id]
        for later_col in range(column_id + 1, steps_count):
            running = running - triangle[later_col][column_id] * weights[later_col]
        weights[column_id] = running / triangle[column_id][column_id]
    return weights


def solution(mesh):
    placed = (
        P("sub", "coarse", None, None),
        P("sub", "coarse", None, None),
        P("sub", "coarse", None, None),
        P("sub", "coarse", None, None, None),
        P("sub", "coarse", None, None, None),
        P("sub", "coarse", None, None),
        P("coarse", None),
        P("sub", None),
        P("sub", None),
        P("sub", "coarse", None, None),
        P("sub", "coarse", None),
    )
    return jax.shard_map(
        on_device,
        mesh=mesh,
        in_specs=placed,
        out_specs=P("sub", "coarse", None, None),
        check_vma=False,
    )
```

```python
import jax
import jax.numpy as jnp
from jax import lax
from jax.experimental import pallas as pl
from jax.experimental.pallas import tpu as pltpu
from jax.sharding import PartitionSpec as P

BS = 128
BPD = 128
AGG_DEV = 16
ITERS = 4
LANES = 128
ROWS = 8
INVERSE_PARTS = 4
DIRECT_GROUPS = 4
BF16 = jnp.bfloat16
F32 = jnp.float32


def split(values):
    high = values.astype(BF16)
    low = (values - high.astype(F32)).astype(BF16)
    return high, low


def dot_rows(left, right):
    return lax.dot_general(left, right, (((1,), (1,)), ((), ())), preferred_element_type=F32)


def dot_plain(left, right):
    return lax.dot_general(left, right, (((1,), (0,)), ((), ())), preferred_element_type=F32)


def paired_rows(values):
    high, low = split(values)
    return jnp.concatenate(
        [
            jnp.concatenate([high, high], axis=1),
            jnp.concatenate([low, jnp.zeros_like(low)], axis=1),
        ],
        axis=0,
    )


def pick(selector, values):
    high, low = split(values)
    return dot_plain(selector, jnp.concatenate([high, low], axis=0))


def column_sum(values):
    return jnp.sum(values, axis=0, keepdims=True)


def line_product(values, diagonal, link):
    rows = values.shape[0]
    lanes = values.shape[1]
    row = lax.broadcasted_iota(jnp.int32, values.shape, 0)
    lane = lax.broadcasted_iota(jnp.int32, values.shape, 1)
    next_lane = pltpu.roll(values, lanes - 1, 1)
    next_row = pltpu.roll(next_lane, rows - 1, 0)
    ahead = jnp.where(lane < lanes - 1, next_lane, jnp.where(row < rows - 1, next_row, 0.0))
    scaled = link * values
    last_lane = pltpu.roll(scaled, 1, 1)
    last_row = pltpu.roll(last_lane, 1, 0)
    behind = jnp.where(lane > 0, last_lane, jnp.where(row > 0, last_row, 0.0))
    return diagonal * values - (ahead * link + behind)


def couple(arrived, pair_ref, live):
    rounds = pair_ref.shape[0]
    widest = arrived.shape[0] // rounds
    pieces = []
    for round_id in range(rounds):
        left = paired_rows(arrived[round_id * widest : (round_id + 1) * widest])
        both = dot_rows(left, pair_ref[round_id])
        pieces.append(both[:widest] + both[widest:])
    return jnp.concatenate(pieces, axis=0) * live


def gather_rounds(slots, route, rounds):
    pieces = []
    for round_id in range(rounds):
        total = None
        for sub_id, piece in enumerate(slots):
            at = round_id * len(slots) + sub_id
            term = route[at : at + 1] * piece
            total = term if total is None else total + term
        pieces.append(total)
    return jnp.concatenate(pieces, axis=0)


def spread_rounds(values, route, subs, rounds):
    widest = values.shape[0] // rounds
    slots = []
    for sub_id in range(subs):
        total = None
        for round_id in range(rounds):
            at = round_id * subs + sub_id
            term = route[at : at + 1] * values[round_id * widest : (round_id + 1) * widest]
            total = term if total is None else total + term
        slots.append(total)
    return slots


def vmem(shape, dtype=F32):
    return pltpu.VMEM(shape, dtype)


def call(kernel, outs, *args, name, places="", aliases=None, scratch=()):
    places = places + "v" * (len(args) - len(places))
    spaces = {"s": pltpu.SMEM, "h": pltpu.HBM, "v": pltpu.VMEM}
    return pl.pallas_call(
        kernel,
        out_shape=outs,
        in_specs=[pl.BlockSpec(memory_space=spaces[place]) for place in places],
        out_specs=[pl.BlockSpec(memory_space=pltpu.VMEM)] * len(outs),
        input_output_aliases=aliases or {},
        scratch_shapes=list(scratch),
        name=name,
        compiler_params=pltpu.CompilerParams(vmem_limit_bytes=16 * 1024 * 1024),
    )(
        *[
            pltpu.with_memory_space_constraint(
                arg, pltpu.VMEM if place == "v" else pltpu.HBM
            )
            for arg, place in zip(args, places)
        ]
    )


def on_device(
    right_side,
    diagonal,
    cell_link,
    block_inverse,
    coupling,
    coarse_basis,
    coarse_inverse,
    partner,
    margin_width,
    margin_blocks,
    aggregate,
):
    subs = lax.axis_size("sub")
    parts = lax.axis_size("coarse")
    devices = subs * parts
    block_count = right_side.shape[2]
    unknowns = right_side.shape[3]
    rounds = margin_blocks.shape[2]
    widest = margin_blocks.shape[3]
    aggregates = coarse_inverse.shape[1]
    own_aggregates = aggregates // devices
    sub_aggregates = subs * own_aggregates
    sub_chunks = sub_aggregates // LANES
    sub_span = subs // parts
    chunk_rows = sub_span * own_aggregates
    factor = (BS * BPD / AGG_DEV) ** (-0.5)
    coarse_rows = aggregates // LANES
    stat_rows = -(-(coarse_rows + ITERS) // ROWS) * ROWS
    slot_rows = max(widest, stat_rows)
    margin_rows = rounds * widest
    table_rows = -(-2 * margin_rows // LANES) * LANES
    full = (block_count, unknowns)
    direct_blocks = DIRECT_GROUPS * ROWS
    paired_blocks = block_count - direct_blocks

    v_at = 0
    z_at = v_at + (ITERS - 1) * block_count
    m_at = z_at + ITERS * block_count
    head_at = m_at + (ITERS - 1) * margin_rows
    state_rows = head_at + ITERS * ROWS
    blocks = margin_blocks[0, 0]
    member_of = aggregate[0]
    own_bits = own_aggregates.bit_length() - 1
    part_bits = parts.bit_length() - 1
    span_bits = sub_span.bit_length() - 1
    lane_bits = LANES.bit_length() - 1
    assert own_aggregates == 1 << own_bits and parts == 1 << part_bits
    assert sub_span == 1 << span_bits and sub_span * parts == subs

    def iota(shape, dim):
        return lax.broadcasted_iota(jnp.int32, shape, dim)

    def hot(condition):
        return jnp.where(condition, 1.0, 0.0).astype(F32)

    def coarse_lane(numbers):
        own_device = numbers >> own_bits
        own_part = own_device & (parts - 1)
        own_sub = own_device >> part_bits
        turn = (own_part - (own_sub >> span_bits)) & (parts - 1)
        return (
            turn * chunk_rows
            + (own_sub & (sub_span - 1)) * own_aggregates
            + (numbers & (own_aggregates - 1))
        )

    def statistics_block(vector, basis_value, member_value, home, dots, rows, count):
        inner = jnp.sum(basis_value * vector, axis=1, keepdims=True)
        line = column_sum(inner * member_value) * factor
        lines = [home[chunk : chunk + 1] * line for chunk in range(count)]
        lines += [column_sum(other * vector) for other in dots]
        if len(lines) < rows:
            lines.append(jnp.zeros((rows - len(lines), LANES), F32))
        return jnp.concatenate(lines, axis=0)

    def begin(
        blocks_hbm,
        partner_hbm,
        width_hbm,
        start_hbm,
        basis_hbm,
        member_of_hbm,
        coarse_hbm,
        coupling_hbm,
        *refs,
    ):
        (
            slot_ref,
            selector_ref,
            route_ref,
            live_ref,
            member_ref,
            home_ref,
            start_ref,
            basis_ref,
            member_of_ref,
            coupling_ref,
        ) = refs[:10]
        chunk_refs = refs[10 : 10 + parts]
        (
            blocks_ref,
            partner_ref,
            width_ref,
            number_ref,
            held_ref,
            semaphores,
            scalar_semaphores,
        ) = refs[10 + parts :]
        scalar_copies = [
            pltpu.make_async_copy(source, to, scalar_semaphores.at[position])
            for position, (source, to) in enumerate(
                [
                    (member_of_hbm, number_ref),
                    (blocks_hbm, blocks_ref),
                    (partner_hbm, partner_ref),
                    (width_hbm, width_ref),
                ]
            )
        ]
        copies = [
            pltpu.make_async_copy(source, to, semaphores.at[position])
            for position, (source, to) in enumerate(
                [(start_hbm, start_ref), (basis_hbm, basis_ref), (member_of_hbm, member_of_ref)]
            )
        ]
        held_copies = [
            pltpu.make_async_copy(
                coarse_hbm.at[
                    pl.ds((span * parts + part_id) * own_aggregates, own_aggregates), :
                ],
                held_ref.at[part_id, pl.ds(span * own_aggregates, own_aggregates), :],
                semaphores.at[3 + span * parts + part_id],
            )
            for span in range(sub_span)
            for part_id in range(parts)
        ]
        coupling_copy = pltpu.make_async_copy(
            coupling_hbm, coupling_ref, scalar_semaphores.at[4]
        )
        for copy in scalar_copies + copies + held_copies + [coupling_copy]:
            copy.start()
        for copy in scalar_copies:
            copy.wait()
        own_part = (number_ref[0, 0] >> own_bits) & (parts - 1)
        row = iota((widest, LANES), 0)
        lane = iota((widest, LANES), 1)
        tables = []
        for round_id in range(rounds):
            wanted = jnp.zeros((widest, LANES), jnp.int32)
            for position in range(widest):
                wanted = jnp.where(row == position, blocks_ref[round_id, position], wanted)
            tables.append(hot(lane == wanted))
            live_ref[round_id * widest : (round_id + 1) * widest, :] = hot(
                row < width_ref[0, round_id]
            )
            sub_row = iota((subs, LANES), 0)
            route_ref[round_id * subs : (round_id + 1) * subs, :] = hot(
                sub_row == partner_ref[0, round_id]
            )
        for copy in copies:
            copy.wait()
        start = start_ref[...]
        basis_value = basis_ref[...]
        numbers = member_of_ref[...]
        table = jnp.concatenate(tables, axis=0)
        table = jnp.concatenate([table, table], axis=1).astype(BF16)
        selector_ref[...] = table
        route = route_ref[...]
        member = hot((numbers & (LANES - 1)) == iota((LANES, block_count), 0)).T
        member_ref[...] = member
        home = hot((numbers >> lane_bits) == iota((coarse_rows, LANES), 0))
        home_ref[...] = home
        own_lane = coarse_lane(numbers)
        rows_start = spread_rounds(pick(table, start), route, subs, rounds)
        rows_basis = spread_rounds(pick(table, basis_value), route, subs, rounds)
        rows_lane = []
        for chunk in range(sub_chunks):
            lane_table = hot(own_lane == iota((LANES, block_count), 0) + chunk * LANES)
            rows_lane.append(
                spread_rounds(
                    dot_rows(table[:, :block_count], lane_table.astype(BF16)), route, subs, rounds
                )
            )
        statistic = statistics_block(
            start, basis_value, member, home, [start], stat_rows, coarse_rows
        )
        for sub_id in range(subs):
            slot_ref[sub_id, 0:widest, :] = rows_start[sub_id]
            slot_ref[sub_id, widest : widest + stat_rows, :] = statistic
            at = widest + stat_rows
            slot_ref[sub_id, at : at + widest, :] = rows_basis[sub_id]
            for chunk in range(sub_chunks):
                at = at + widest
                slot_ref[sub_id, at : at + widest, :] = rows_lane[chunk][sub_id]
        for copy in held_copies:
            copy.wait()
        for turn, chunk_ref in enumerate(chunk_refs):
            chunk_ref[...] = held_ref[(own_part + turn) & (parts - 1)]
        coupling_copy.wait()

    (
        outgoing,
        selector,
        route,
        live,
        member,
        home,
        start_vector,
        basis,
        member_of,
        couplings,
        *coarse_chunks,
    ) = call(
        begin,
        [
            vmem((subs, (2 + sub_chunks) * widest + stat_rows, unknowns)),
            vmem((margin_rows, 2 * block_count), BF16),
            vmem((rounds * subs, LANES)),
            vmem((margin_rows, LANES)),
            vmem((block_count, LANES)),
            vmem((coarse_rows, LANES)),
            vmem(full),
            vmem(full),
            vmem((1, block_count), jnp.int32),
            vmem((rounds, unknowns, unknowns)),
        ]
        + [vmem((chunk_rows, aggregates))] * parts,
        blocks,
        partner,
        margin_width,
        right_side[0, 0],
        coarse_basis[0, 0],
        aggregate[0],
        coarse_inverse,
        coupling[0, 0],
        name="begin",
        places="hhhhhhhh",
        scratch=[
            pltpu.SMEM((rounds, widest), jnp.int32),
            pltpu.SMEM((1, rounds), jnp.int32),
            pltpu.SMEM((1, rounds), jnp.int32),
            pltpu.SMEM((1, block_count), jnp.int32),
            vmem((parts, chunk_rows, aggregates)),
            pltpu.SemaphoreType.DMA((3 + parts * sub_span,)),
            pltpu.SemaphoreType.DMA((5,)),
        ],
    )
    for turn in range(1, parts):
        coarse_chunks[turn] = lax.ppermute(
            coarse_chunks[turn], "coarse", [(i, (i + turn) % parts) for i in range(parts)]
        )

    def put(target_value, values):
        high, low = split(values)
        pieces = [high, low]
        if table_rows > 2 * margin_rows:
            pieces.append(jnp.zeros((table_rows - 2 * margin_rows, unknowns), BF16))
        return dot_plain(target_value, jnp.concatenate(pieces, axis=0))

    def smooth_rest(arrived_ref, out, target, selector, route, part_ref, stat_ref, slot_ref, sum_ref):
        slots = spread_rounds(pick(selector, out), route, subs, rounds)
        statistic = stat_ref[0, widest : widest + stat_rows, :]
        if stat_rows < slot_rows:
            statistic = jnp.concatenate(
                [statistic, jnp.zeros((slot_rows - stat_rows, LANES), F32)], axis=0
            )
        for sub_id in range(subs):
            piece = slots[sub_id]
            if widest < slot_rows:
                piece = jnp.concatenate(
                    [piece, jnp.zeros((slot_rows - widest, unknowns), F32)], axis=0
                )
            for part_id in range(parts):
                slot_ref[sub_id * parts + part_id] = jnp.where(
                    part_ref[part_id : part_id + 1, :] > 0.5, piece, statistic
                )
        total = arrived_ref[0, widest : widest + stat_rows, :]
        for sub_id in range(1, subs):
            total = total + arrived_ref[sub_id, widest : widest + stat_rows, :]
        sum_ref[...] = total

    def arrived_rows(arrived_ref, at, route):
        return gather_rounds(
            [arrived_ref[sub_id, at : at + widest, :] for sub_id in range(subs)], route, rounds
        )

    def block_rows(shifted_ref, group):
        rows = pl.ds(pl.multiple_of(group * ROWS, ROWS), ROWS)
        return paired_rows(shifted_ref[rows, :])

    def direct_product(values, blocks_at):
        lines = []
        for offset in range(ROWS):
            scaled = blocks_at(offset) * values[offset : offset + 1, :]
            lines.append(jnp.sum(scaled, axis=1)[None, :])
        return jnp.concatenate(lines, axis=0)

    def block_product(left, weight_of):
        row = iota((ROWS, unknowns), 0)
        total = jnp.zeros((ROWS, unknowns), F32)
        for offset in range(ROWS // 2):
            both = dot_plain(left, weight_of(offset))
            both = both[:ROWS] + both[ROWS:]
            total = jnp.where(row == 2 * offset, both[:, :unknowns], total)
            total = jnp.where(row == 2 * offset + 1, both[:, unknowns:], total)
        return total

    def smooth_first(
        arrived_ref,
        vector_ref,
        selector_ref,
        route_ref,
        live_ref,
        member_of_ref,
        stat_ref,
        coupling_ref,
        inverse_hbm,
        diagonal_hbm,
        link_hbm,
        *refs,
    ):
        (
            out_ref,
            slot_ref,
            sum_ref,
            basis_rows_ref,
            lane_rows_ref,
            weight_ref,
            direct_ref,
            pair_ref,
            target_ref,
            sub_member_ref,
            part_ref,
            diagonal_ref,
            link_ref,
            inverse_ref,
            shifted_ref,
            semaphores,
            part_semaphores,
        ) = refs
        copies = [
            pltpu.make_async_copy(source, to, semaphores.at[position])
            for position, (source, to) in enumerate(
                [
                    (diagonal_hbm, diagonal_ref),
                    (link_hbm, link_ref),
                ]
            )
        ]

        span = paired_blocks // INVERSE_PARTS
        direct_span = direct_blocks // INVERSE_PARTS
        direct_copies = [
            pltpu.make_async_copy(
                inverse_hbm.at[pl.ds(number * direct_span, direct_span)],
                direct_ref.at[pl.ds(number * direct_span, direct_span)],
                semaphores.at[3 + number],
            )
            for number in range(INVERSE_PARTS)
        ]
        part_copies = [
            pltpu.make_async_copy(
                inverse_hbm.at[pl.ds(direct_blocks + number * span, span)],
                inverse_ref.at[pl.ds(number * span, span)],
                part_semaphores.at[number],
            )
            for number in range(INVERSE_PARTS)
        ]
        for copy in copies:
            copy.start()
        for number in range(INVERSE_PARTS):
            direct_copies[number].start()
            part_copies[number].start()
        route = route_ref[...]
        table = selector_ref[:, 0:block_count].astype(F32)
        pieces = [table, table]
        if table_rows > 2 * margin_rows:
            pieces.append(jnp.zeros((table_rows - 2 * margin_rows, block_count), F32))
        table = jnp.concatenate(pieces, axis=0)
        target_ref[...] = jnp.concatenate(
            [table[start : start + LANES].T for start in range(0, table_rows, LANES)], axis=1
        ).astype(BF16)
        numbers = member_of_ref[...]
        own_lane = coarse_lane(numbers)
        for chunk in range(sub_chunks):
            sub_member_ref[:, chunk * LANES : (chunk + 1) * LANES] = hot(
                own_lane == iota((LANES, block_count), 0) + chunk * LANES
            ).T
        part_ref[...] = hot(((numbers >> own_bits) & (parts - 1)) == iota((ROWS, LANES), 0))
        at = widest + stat_rows
        basis_rows = arrived_rows(arrived_ref, at, route)
        for chunk in range(sub_chunks):
            at = at + widest
            lane_rows_ref[chunk] = arrived_rows(arrived_ref, at, route)
        for round_id in range(rounds):
            high, low = split(coupling_ref[round_id])
            pair_ref[round_id, :, 0:unknowns] = high
            pair_ref[round_id, :, unknowns : 2 * unknowns] = low
        mapped = couple(arrived_rows(arrived_ref, 0, route), pair_ref, live_ref[...])
        basis_rows_ref[...] = couple(basis_rows, pair_ref, live_ref[...])
        shifted_ref[...] = vector_ref[...] + put(target_ref[...], mapped)

        paired_groups = (block_count // ROWS - DIRECT_GROUPS) // DIRECT_GROUPS

        def paired_step(group):
            left = block_rows(shifted_ref, group)

            def weight_of(offset):
                pair = (group - DIRECT_GROUPS) * (ROWS // 2) + offset
                highs = []
                lows = []
                for position in range(2):
                    high, low = split(inverse_ref[pair * 2 + position])
                    high, low = high.T, low.T
                    lanes = slice(position * unknowns, (position + 1) * unknowns)
                    weight_ref[pair, 0:unknowns, lanes] = high
                    weight_ref[pair, unknowns : 2 * unknowns, lanes] = low
                    highs.append(high)
                    lows.append(low)
                return jnp.concatenate(
                    [jnp.concatenate(highs, axis=1), jnp.concatenate(lows, axis=1)], axis=0
                )

            rows = pl.ds(pl.multiple_of(group * ROWS, ROWS), ROWS)
            out_ref[rows, :] = block_product(left, weight_of)

        def step(unit, carry):
            rows = pl.ds(pl.multiple_of(unit * ROWS, ROWS), ROWS)
            out_ref[rows, :] = direct_product(
                shifted_ref[rows, :], lambda offset: direct_ref[unit * ROWS + offset]
            )
            for number in range(paired_groups):
                paired_step(DIRECT_GROUPS + unit * paired_groups + number)
            return carry

        units = DIRECT_GROUPS // INVERSE_PARTS
        for number in range(INVERSE_PARTS):
            direct_copies[number].wait()
            part_copies[number].wait()
            lax.fori_loop(number * units, (number + 1) * units, step, 0, unroll=1)
        for copy in copies:
            copy.wait()
        smooth_rest(
            arrived_ref,
            out_ref[...],
            target_ref[...],
            selector_ref[...],
            route,
            part_ref,
            stat_ref,
            slot_ref,
            sum_ref,
        )

    def smooth(
        arrived_ref,
        vector_ref,
        weight_ref,
        direct_ref,
        pair_ref,
        target_ref,
        selector_ref,
        route_ref,
        live_ref,
        part_ref,
        stat_ref,
        out_ref,
        slot_ref,
        sum_ref,
    ):
        route = route_ref[...]
        mapped = couple(arrived_rows(arrived_ref, 0, route), pair_ref, live_ref[...])
        shifted = vector_ref[...] + put(target_ref[...], mapped)
        pieces = []
        for group in range(block_count // ROWS):
            values = shifted[group * ROWS : (group + 1) * ROWS]
            if group < DIRECT_GROUPS:
                piece = direct_product(values, lambda offset: direct_ref[group * ROWS + offset])
            else:
                at = (group - DIRECT_GROUPS) * (ROWS // 2)
                piece = block_product(
                    paired_rows(values), lambda offset: weight_ref[at + offset]
                )
            pieces.append(piece)
        out = jnp.concatenate(pieces, axis=0)
        out_ref[...] = out
        smooth_rest(
            arrived_ref,
            out,
            target_ref[...],
            selector_ref[...],
            route,
            part_ref,
            stat_ref,
            slot_ref,
            sum_ref,
        )

    def advance(step_id):
        first = step_id == 0
        last = step_id == ITERS - 1

        def kernel(*refs):
            (
                arrived_ref,
                sum_ref,
                smoothed_ref,
                vector_ref,
                sub_member_ref,
                member_ref,
                home_ref,
                basis_ref,
                basis_rows_ref,
                lane_rows_ref,
                pair_ref,
                target_ref,
                selector_ref,
                route_ref,
                live_ref,
                part_ref,
                diagonal_ref,
                link_ref,
            ) = refs[:18]
            coarse_refs = refs[18 : 18 + parts]
            outs = list(refs[18 + parts :])
            if first:
                state_ref = outs.pop()
            else:
                state_in = outs.pop(0)
                state_ref = outs.pop()

                def held(at, number, rows):
                    return state_in[at + number * rows : at + (number + 1) * rows, :]

            def keep(at, number, values):
                rows = values.shape[0]
                state_ref[at + number * rows : at + (number + 1) * rows, :] = values

            total = sum_ref[...]
            pieces = []
            for sub_id in range(subs):
                piece = jnp.zeros((widest, unknowns), F32)
                for part_id in range(parts):
                    slot = sub_id * parts + part_id
                    own = part_ref[part_id : part_id + 1, :] > 0.5
                    total = total + jnp.where(own, 0.0, arrived_ref[slot, 0:stat_rows, :])
                    piece = piece + jnp.where(own, arrived_ref[slot, 0:widest, :], 0.0)
                pieces.append(piece)
            products = jnp.sum(total[coarse_rows : coarse_rows + step_id + 1], axis=1, keepdims=True)
            heads = [products[i : i + 1] for i in range(step_id)]
            square = products[step_id : step_id + 1]
            remaining = square
            for head in heads:
                remaining = remaining - head * head
            length = jnp.sqrt(jnp.maximum(remaining, square * 1e-12))
            scale = 1.0 / length
            gathered = []
            for coarse_ref in coarse_refs:
                piece = coarse_ref[:, 0:LANES] * total[0:1]
                for chunk in range(1, coarse_rows):
                    piece = piece + (
                        coarse_ref[:, chunk * LANES : (chunk + 1) * LANES] * total[chunk : chunk + 1]
                    )
                gathered.append(piece)
            gathered = jnp.concatenate(gathered, axis=0)
            column = jnp.sum(gathered, axis=1, keepdims=True)
            same = iota((LANES, LANES), 0) == iota((LANES, LANES), 1)
            lines = [
                column_sum(jnp.where(same, column[start : start + LANES], 0.0))
                for start in range(0, sub_aggregates, LANES)
            ]
            own_coarse = sub_member_ref[:, 0:LANES] * lines[0]
            row_coarse = lane_rows_ref[0] * lines[0]
            for chunk in range(1, sub_chunks):
                own_coarse = own_coarse + (
                    sub_member_ref[:, chunk * LANES : (chunk + 1) * LANES] * lines[chunk]
                )
                row_coarse = row_coarse + lane_rows_ref[chunk] * lines[chunk]
            own_coarse = jnp.sum(own_coarse, axis=1, keepdims=True)
            row_coarse = jnp.sum(row_coarse, axis=1, keepdims=True)
            basis_value = basis_ref[...]
            direction = smoothed_ref[...] + own_coarse * basis_value
            for number, head in enumerate(heads):
                direction = direction - head * held(z_at, number, block_count)
            direction = direction * scale
            route = route_ref[...]
            rows = couple(gather_rounds(pieces, route, rounds), pair_ref, live_ref[...])
            rows = rows + row_coarse * basis_rows_ref[...]
            for number, head in enumerate(heads):
                rows = rows - head * held(m_at, number, margin_rows)
            rows = rows * scale
            vector = vector_ref[...]
            earlier = [held(v_at, number, block_count) for number in range(step_id)]
            for head, other in zip(heads, earlier):
                vector = vector - head * other
            vector = vector * scale
            product = line_product(direction, diagonal_ref[...], link_ref[...]) - put(
                target_ref[...], rows
            )
            against = earlier + [vector, product]
            if last:
                (slot_ref,) = outs
                lane = iota((1, LANES), 1)
                block = jnp.zeros((1, LANES), F32)
                for position, other in enumerate(against):
                    value = jnp.sum(column_sum(other * product), axis=1, keepdims=True)
                    block = jnp.where(lane == position, value, block)
                for slot in range(devices):
                    slot_ref[slot] = block
            else:
                product_ref, slot_ref = outs
                keep(v_at, step_id, vector)
                keep(m_at, step_id, rows)
                product_ref[...] = product
                slots = spread_rounds(pick(selector_ref[...], product), route, subs, rounds)
                block = statistics_block(
                    product,
                    basis_value,
                    member_ref[...],
                    home_ref[...],
                    against,
                    stat_rows,
                    coarse_rows,
                )
                for sub_id in range(subs):
                    slot_ref[sub_id, 0:widest, :] = slots[sub_id]
                    slot_ref[sub_id, widest:, :] = block
            keep(z_at, step_id, direction)
            keep(
                head_at,
                step_id,
                jnp.broadcast_to(
                    jnp.concatenate(
                        heads + [length] + [jnp.zeros((ROWS - step_id - 1, 1), F32)], axis=0
                    ),
                    (ROWS, LANES),
                ),
            )

        return kernel

    vector = start_vector
    state = None
    state_shape = vmem((state_rows, LANES))
    for step_id in range(ITERS):
        first = step_id == 0
        last = step_id == ITERS - 1
        arrived = lax.all_to_all(outgoing, "sub", 0, 0)
        outs = [vmem(full), vmem((devices, slot_rows, unknowns)), vmem((stat_rows, LANES))]
        if first:
            (
                smoothed,
                slots,
                sums,
                basis_rows,
                lane_rows,
                weights,
                direct,
                pairs,
                target,
                sub_member,
                part_table,
                diagonal_local,
                link_local,
            ) = call(
                smooth_first,
                outs
                + [
                    vmem((margin_rows, unknowns)),
                    vmem((sub_chunks, margin_rows, LANES)),
                    vmem((paired_blocks // 2, 2 * unknowns, 2 * unknowns), BF16),
                    vmem((direct_blocks, unknowns, unknowns)),
                    vmem((rounds, unknowns, 2 * unknowns), BF16),
                    vmem((block_count, table_rows), BF16),
                    vmem((block_count, sub_aggregates)),
                    vmem((ROWS, LANES)),
                    vmem(full),
                    vmem(full),
                ],
                arrived,
                vector,
                selector,
                route,
                live,
                member_of,
                outgoing,
                couplings,
                block_inverse[0, 0],
                diagonal[0, 0],
                cell_link[0, 0],
                name="smooth0",
                places="vvvvvvvvhhh",
                scratch=[
                    vmem((paired_blocks, unknowns, unknowns)),
                    vmem(full),
                    pltpu.SemaphoreType.DMA((3 + INVERSE_PARTS,)),
                    pltpu.SemaphoreType.DMA((INVERSE_PARTS,)),
                ],
            )
            slots, *coarse_chunks = lax.optimization_barrier((slots, *coarse_chunks))
        else:
            smoothed, slots, sums = call(
                smooth,
                outs,
                arrived,
                vector,
                weights,
                direct,
                pairs,
                target,
                selector,
                route,
                live,
                part_table,
                outgoing,
                name=f"smooth{step_id}",
            )
        arrived = lax.all_to_all(slots, ("sub", "coarse"), 0, 0)
        if last:
            outs = [vmem((devices, 1, LANES)), state_shape]
        else:
            outs = [vmem(full), vmem((subs, widest + stat_rows, unknowns)), state_shape]
        made = call(
            advance(step_id),
            outs,
            arrived,
            sums,
            smoothed,
            vector,
            sub_member,
            member,
            home,
            basis,
            basis_rows,
            lane_rows,
            pairs,
            target,
            selector,
            route,
            live,
            part_table,
            diagonal_local,
            link_local,
            *coarse_chunks,
            *([] if first else [state]),
            name=f"advance{step_id}",
            aliases={} if first else {18 + parts: len(outs) - 1},
        )
        if last:
            slots, state = made
        else:
            vector, outgoing, state = made
    arrived = lax.all_to_all(slots, ("sub", "coarse"), 0, 0)

    def finish(arrived_ref, state_ref, out_ref):
        total = column_sum(arrived_ref[...].reshape(devices, LANES))
        heads = [total[:, i : i + 1] for i in range(ITERS)]
        square = total[:, ITERS : ITERS + 1]
        remaining = square
        for head in heads:
            remaining = remaining - head * head
        length = jnp.sqrt(jnp.maximum(remaining, square * 1e-12))
        beta = state_ref[head_at : head_at + 1, 0:1]
        columns = []
        for column_id in range(1, ITERS):
            at = head_at + column_id * ROWS
            columns.append([state_ref[at + i : at + i + 1, 0:1] for i in range(column_id + 1)])
        columns.append(heads + [length])
        weights_found = givens_solve(columns, beta)
        result = weights_found[0] * state_ref[z_at : z_at + block_count, :]
        for position in range(1, ITERS):
            at = z_at + position * block_count
            result = result + weights_found[position] * state_ref[at : at + block_count, :]
        out_ref[...] = result

    (answer,) = call(finish, [jax.ShapeDtypeStruct(full, F32)], arrived, state, name="finish")
    return answer.reshape(right_side.shape)


def givens_solve(columns, beta):
    steps_count = len(columns)
    cosines = []
    sines = []
    side_terms = [beta] + [jnp.zeros_like(beta) for unused in range(steps_count)]
    triangle = []
    for column_id in range(steps_count):
        column = list(columns[column_id])
        for row_id in range(column_id):
            upper = column[row_id]
            lower = column[row_id + 1]
            column[row_id] = cosines[row_id] * upper + sines[row_id] * lower
            column[row_id + 1] = cosines[row_id] * lower - sines[row_id] * upper
        upper = column[column_id]
        lower = column[column_id + 1]
        radius = jnp.sqrt(upper * upper + lower * lower)
        cosine = upper / radius
        sine_value = lower / radius
        column[column_id] = radius
        cosines.append(cosine)
        sines.append(sine_value)
        side_terms[column_id + 1] = -sine_value * side_terms[column_id]
        side_terms[column_id] = cosine * side_terms[column_id]
        triangle.append(column)
    weights = [None] * steps_count
    for column_id in reversed(range(steps_count)):
        running = side_terms[column_id]
        for later_col in range(column_id + 1, steps_count):
            running = running - triangle[later_col][column_id] * weights[later_col]
        weights[column_id] = running / triangle[column_id][column_id]
    return weights


def solution(mesh):
    placed = (
        P("sub", "coarse", None, None),
        P("sub", "coarse", None, None),
        P("sub", "coarse", None, None),
        P("sub", "coarse", None, None, None),
        P("sub", "coarse", None, None, None),
        P("sub", "coarse", None, None),
        P("coarse", None),
        P("sub", None),
        P("sub", None),
        P("sub", "coarse", None, None),
        P("sub", "coarse", None),
    )
    return jax.shard_map(
        on_device,
        mesh=mesh,
        in_specs=placed,
        out_specs=P("sub", "coarse", None, None),
        check_vma=False,
    )
```

```python
import jax
import jax.numpy as jnp
from jax import lax
from jax.experimental import pallas as pl
from jax.experimental.pallas import tpu as pltpu
from jax.sharding import PartitionSpec as P

BS = 128
BPD = 128
AGG_DEV = 16
ITERS = 4
LANES = 128
ROWS = 8
INVERSE_PARTS = 4
DIRECT_GROUPS = 4
BF16 = jnp.bfloat16
F32 = jnp.float32


def split(values):
    high = values.astype(BF16)
    low = (values - high.astype(F32)).astype(BF16)
    return high, low


def dot_rows(left, right):
    return lax.dot_general(left, right, (((1,), (1,)), ((), ())), preferred_element_type=F32)


def dot_plain(left, right):
    return lax.dot_general(left, right, (((1,), (0,)), ((), ())), preferred_element_type=F32)


def paired_rows(values):
    high, low = split(values)
    return jnp.concatenate(
        [
            jnp.concatenate([high, high], axis=1),
            jnp.concatenate([low, jnp.zeros_like(low)], axis=1),
        ],
        axis=0,
    )


def pick(selector, values):
    high, low = split(values)
    return dot_plain(selector, jnp.concatenate([high, low], axis=0))


def tree_sum(values):
    while len(values) > 1:
        pairs = [left + right for left, right in zip(values[::2], values[1::2])]
        values = pairs + ([values[-1]] if len(values) % 2 else [])
    return values[0]


def column_sum(values):
    return jnp.sum(values, axis=0, keepdims=True)


def line_product(values, diagonal, link):
    rows = values.shape[0]
    lanes = values.shape[1]
    row = lax.broadcasted_iota(jnp.int32, values.shape, 0)
    lane = lax.broadcasted_iota(jnp.int32, values.shape, 1)
    next_lane = pltpu.roll(values, lanes - 1, 1)
    next_row = pltpu.roll(next_lane, rows - 1, 0)
    ahead = jnp.where(lane < lanes - 1, next_lane, jnp.where(row < rows - 1, next_row, 0.0))
    scaled = link * values
    last_lane = pltpu.roll(scaled, 1, 1)
    last_row = pltpu.roll(last_lane, 1, 0)
    behind = jnp.where(lane > 0, last_lane, jnp.where(row > 0, last_row, 0.0))
    return diagonal * values - (ahead * link + behind)


def couple(arrived, pair_ref, live):
    rounds = pair_ref.shape[0]
    widest = arrived.shape[0] // rounds
    pieces = []
    for round_id in range(rounds):
        left = paired_rows(arrived[round_id * widest : (round_id + 1) * widest])
        both = dot_rows(left, pair_ref[round_id])
        pieces.append(both[:widest] + both[widest:])
    return jnp.concatenate(pieces, axis=0) * live


def gather_rounds(slots, route, rounds):
    pieces = []
    for round_id in range(rounds):
        total = None
        for sub_id, piece in enumerate(slots):
            at = round_id * len(slots) + sub_id
            term = route[at : at + 1] * piece
            total = term if total is None else total + term
        pieces.append(total)
    return jnp.concatenate(pieces, axis=0)


def spread_rounds(values, route, subs, rounds):
    widest = values.shape[0] // rounds
    slots = []
    for sub_id in range(subs):
        total = None
        for round_id in range(rounds):
            at = round_id * subs + sub_id
            term = route[at : at + 1] * values[round_id * widest : (round_id + 1) * widest]
            total = term if total is None else total + term
        slots.append(total)
    return slots


def vmem(shape, dtype=F32):
    return pltpu.VMEM(shape, dtype)


def call(kernel, outs, *args, name, places="", aliases=None, scratch=()):
    places = places + "v" * (len(args) - len(places))
    spaces = {"s": pltpu.SMEM, "h": pltpu.HBM, "v": pltpu.VMEM}
    return pl.pallas_call(
        kernel,
        out_shape=outs,
        in_specs=[pl.BlockSpec(memory_space=spaces[place]) for place in places],
        out_specs=[pl.BlockSpec(memory_space=pltpu.VMEM)] * len(outs),
        input_output_aliases=aliases or {},
        scratch_shapes=list(scratch),
        name=name,
        compiler_params=pltpu.CompilerParams(vmem_limit_bytes=16 * 1024 * 1024),
    )(
        *[
            pltpu.with_memory_space_constraint(
                arg, pltpu.VMEM if place == "v" else pltpu.HBM
            )
            for arg, place in zip(args, places)
        ]
    )


def on_device(
    right_side,
    diagonal,
    cell_link,
    block_inverse,
    coupling,
    coarse_basis,
    coarse_inverse,
    partner,
    margin_width,
    margin_blocks,
    aggregate,
):
    subs = lax.axis_size("sub")
    parts = lax.axis_size("coarse")
    devices = subs * parts
    block_count = right_side.shape[2]
    unknowns = right_side.shape[3]
    rounds = margin_blocks.shape[2]
    widest = margin_blocks.shape[3]
    aggregates = coarse_inverse.shape[1]
    own_aggregates = aggregates // devices
    sub_aggregates = subs * own_aggregates
    sub_chunks = sub_aggregates // LANES
    sub_span = subs // parts
    chunk_rows = sub_span * own_aggregates
    factor = (BS * BPD / AGG_DEV) ** (-0.5)
    coarse_rows = aggregates // LANES
    stat_rows = -(-(coarse_rows + ITERS) // ROWS) * ROWS
    slot_rows = max(widest, stat_rows)
    margin_rows = rounds * widest
    table_rows = -(-2 * margin_rows // LANES) * LANES
    full = (block_count, unknowns)
    direct_blocks = DIRECT_GROUPS * ROWS
    paired_blocks = block_count - direct_blocks

    v_at = 0
    z_at = v_at + (ITERS - 1) * block_count
    m_at = z_at + ITERS * block_count
    head_at = m_at + (ITERS - 1) * margin_rows
    state_rows = head_at + ITERS * ROWS
    blocks = margin_blocks[0, 0]
    member_of = aggregate[0]
    own_bits = own_aggregates.bit_length() - 1
    part_bits = parts.bit_length() - 1
    span_bits = sub_span.bit_length() - 1
    lane_bits = LANES.bit_length() - 1
    assert own_aggregates == 1 << own_bits and parts == 1 << part_bits
    assert sub_span == 1 << span_bits and sub_span * parts == subs

    def iota(shape, dim):
        return lax.broadcasted_iota(jnp.int32, shape, dim)

    def hot(condition):
        return jnp.where(condition, 1.0, 0.0).astype(F32)

    def coarse_lane(numbers):
        own_device = numbers >> own_bits
        own_part = own_device & (parts - 1)
        own_sub = own_device >> part_bits
        turn = (own_part - (own_sub >> span_bits)) & (parts - 1)
        return (
            turn * chunk_rows
            + (own_sub & (sub_span - 1)) * own_aggregates
            + (numbers & (own_aggregates - 1))
        )

    def statistics_block(vector, basis_value, member_value, home, dots, rows, count):
        inner = jnp.sum(basis_value * vector, axis=1, keepdims=True)
        line = column_sum(inner * member_value) * factor
        lines = [home[chunk : chunk + 1] * line for chunk in range(count)]
        lines += [column_sum(other * vector) for other in dots]
        if len(lines) < rows:
            lines.append(jnp.zeros((rows - len(lines), LANES), F32))
        return jnp.concatenate(lines, axis=0)

    def begin(
        blocks_hbm,
        partner_hbm,
        width_hbm,
        start_hbm,
        basis_hbm,
        member_of_hbm,
        coarse_hbm,
        coupling_hbm,
        *refs,
    ):
        (
            slot_ref,
            selector_ref,
            route_ref,
            live_ref,
            member_ref,
            home_ref,
            start_ref,
            basis_ref,
            member_of_ref,
            coupling_ref,
        ) = refs[:10]
        chunk_refs = refs[10 : 10 + parts]
        (
            blocks_ref,
            partner_ref,
            width_ref,
            number_ref,
            held_ref,
            semaphores,
            scalar_semaphores,
        ) = refs[10 + parts :]
        scalar_copies = [
            pltpu.make_async_copy(source, to, scalar_semaphores.at[position])
            for position, (source, to) in enumerate(
                [
                    (member_of_hbm, number_ref),
                    (blocks_hbm, blocks_ref),
                    (partner_hbm, partner_ref),
                    (width_hbm, width_ref),
                ]
            )
        ]
        copies = [
            pltpu.make_async_copy(source, to, semaphores.at[position])
            for position, (source, to) in enumerate(
                [(start_hbm, start_ref), (basis_hbm, basis_ref), (member_of_hbm, member_of_ref)]
            )
        ]
        held_copies = [
            pltpu.make_async_copy(
                coarse_hbm.at[
                    pl.ds((span * parts + part_id) * own_aggregates, own_aggregates), :
                ],
                held_ref.at[part_id, pl.ds(span * own_aggregates, own_aggregates), :],
                semaphores.at[3 + span * parts + part_id],
            )
            for span in range(sub_span)
            for part_id in range(parts)
        ]
        coupling_copy = pltpu.make_async_copy(
            coupling_hbm, coupling_ref, scalar_semaphores.at[4]
        )
        for copy in scalar_copies + copies + held_copies + [coupling_copy]:
            copy.start()
        for copy in scalar_copies:
            copy.wait()
        own_part = (number_ref[0, 0] >> own_bits) & (parts - 1)
        row = iota((widest, LANES), 0)
        lane = iota((widest, LANES), 1)
        tables = []
        for round_id in range(rounds):
            wanted = jnp.zeros((widest, LANES), jnp.int32)
            for position in range(widest):
                wanted = jnp.where(row == position, blocks_ref[round_id, position], wanted)
            tables.append(hot(lane == wanted))
            live_ref[round_id * widest : (round_id + 1) * widest, :] = hot(
                row < width_ref[0, round_id]
            )
            sub_row = iota((subs, LANES), 0)
            route_ref[round_id * subs : (round_id + 1) * subs, :] = hot(
                sub_row == partner_ref[0, round_id]
            )
        for copy in copies:
            copy.wait()
        start = start_ref[...]
        basis_value = basis_ref[...]
        numbers = member_of_ref[...]
        table = jnp.concatenate(tables, axis=0)
        table = jnp.concatenate([table, table], axis=1).astype(BF16)
        selector_ref[...] = table
        route = route_ref[...]
        member = hot((numbers & (LANES - 1)) == iota((LANES, block_count), 0)).T
        member_ref[...] = member
        home = hot((numbers >> lane_bits) == iota((coarse_rows, LANES), 0))
        home_ref[...] = home
        own_lane = coarse_lane(numbers)
        rows_start = spread_rounds(pick(table, start), route, subs, rounds)
        rows_basis = spread_rounds(pick(table, basis_value), route, subs, rounds)
        rows_lane = []
        for chunk in range(sub_chunks):
            lane_table = hot(own_lane == iota((LANES, block_count), 0) + chunk * LANES)
            rows_lane.append(
                spread_rounds(
                    dot_rows(table[:, :block_count], lane_table.astype(BF16)), route, subs, rounds
                )
            )
        statistic = statistics_block(
            start, basis_value, member, home, [start], stat_rows, coarse_rows
        )
        for sub_id in range(subs):
            slot_ref[sub_id, 0:widest, :] = rows_start[sub_id]
            slot_ref[sub_id, widest : widest + stat_rows, :] = statistic
            at = widest + stat_rows
            slot_ref[sub_id, at : at + widest, :] = rows_basis[sub_id]
            for chunk in range(sub_chunks):
                at = at + widest
                slot_ref[sub_id, at : at + widest, :] = rows_lane[chunk][sub_id]
        for copy in held_copies:
            copy.wait()
        for turn, chunk_ref in enumerate(chunk_refs):
            chunk_ref[...] = held_ref[(own_part + turn) & (parts - 1)]
        coupling_copy.wait()

    (
        outgoing,
        selector,
        route,
        live,
        member,
        home,
        start_vector,
        basis,
        member_of,
        couplings,
        *coarse_chunks,
    ) = call(
        begin,
        [
            vmem((subs, (2 + sub_chunks) * widest + stat_rows, unknowns)),
            vmem((margin_rows, 2 * block_count), BF16),
            vmem((rounds * subs, LANES)),
            vmem((margin_rows, LANES)),
            vmem((block_count, LANES)),
            vmem((coarse_rows, LANES)),
            vmem(full),
            vmem(full),
            vmem((1, block_count), jnp.int32),
            vmem((rounds, unknowns, unknowns)),
        ]
        + [vmem((chunk_rows, aggregates))] * parts,
        blocks,
        partner,
        margin_width,
        right_side[0, 0],
        coarse_basis[0, 0],
        aggregate[0],
        coarse_inverse,
        coupling[0, 0],
        name="begin",
        places="hhhhhhhh",
        scratch=[
            pltpu.SMEM((rounds, widest), jnp.int32),
            pltpu.SMEM((1, rounds), jnp.int32),
            pltpu.SMEM((1, rounds), jnp.int32),
            pltpu.SMEM((1, block_count), jnp.int32),
            vmem((parts, chunk_rows, aggregates)),
            pltpu.SemaphoreType.DMA((3 + parts * sub_span,)),
            pltpu.SemaphoreType.DMA((5,)),
        ],
    )
    for turn in range(1, parts):
        coarse_chunks[turn] = lax.ppermute(
            coarse_chunks[turn], "coarse", [(i, (i + turn) % parts) for i in range(parts)]
        )

    def put(target_value, values):
        high, low = split(values)
        pieces = [high, low]
        if table_rows > 2 * margin_rows:
            pieces.append(jnp.zeros((table_rows - 2 * margin_rows, unknowns), BF16))
        return dot_plain(target_value, jnp.concatenate(pieces, axis=0))

    def smooth_rest(arrived_ref, out, target, selector, route, part_ref, stat_ref, slot_ref, sum_ref):
        slots = spread_rounds(pick(selector, out), route, subs, rounds)
        statistic = stat_ref[0, widest : widest + stat_rows, :]
        if stat_rows < slot_rows:
            statistic = jnp.concatenate(
                [statistic, jnp.zeros((slot_rows - stat_rows, LANES), F32)], axis=0
            )
        for sub_id in range(subs):
            piece = slots[sub_id]
            if widest < slot_rows:
                piece = jnp.concatenate(
                    [piece, jnp.zeros((slot_rows - widest, unknowns), F32)], axis=0
                )
            for part_id in range(parts):
                slot_ref[sub_id * parts + part_id] = jnp.where(
                    part_ref[part_id : part_id + 1, :] > 0.5, piece, statistic
                )
        total = arrived_ref[0, widest : widest + stat_rows, :]
        for sub_id in range(1, subs):
            total = total + arrived_ref[sub_id, widest : widest + stat_rows, :]
        sum_ref[...] = total

    def arrived_rows(arrived_ref, at, route):
        return gather_rounds(
            [arrived_ref[sub_id, at : at + widest, :] for sub_id in range(subs)], route, rounds
        )

    def block_rows(shifted_ref, group):
        rows = pl.ds(pl.multiple_of(group * ROWS, ROWS), ROWS)
        return paired_rows(shifted_ref[rows, :])

    def direct_product(values, blocks_at):
        lines = []
        for offset in range(ROWS):
            scaled = blocks_at(offset) * values[offset : offset + 1, :]
            lines.append(jnp.sum(scaled, axis=1)[None, :])
        return jnp.concatenate(lines, axis=0)

    def block_product(left, weight_of):
        row = iota((ROWS, unknowns), 0)
        total = jnp.zeros((ROWS, unknowns), F32)
        for offset in range(ROWS // 2):
            both = dot_plain(left, weight_of(offset))
            both = both[:ROWS] + both[ROWS:]
            total = jnp.where(row == 2 * offset, both[:, :unknowns], total)
            total = jnp.where(row == 2 * offset + 1, both[:, unknowns:], total)
        return total

    def smooth_first(
        arrived_ref,
        vector_ref,
        selector_ref,
        route_ref,
        live_ref,
        member_of_ref,
        stat_ref,
        coupling_ref,
        inverse_hbm,
        diagonal_hbm,
        link_hbm,
        *refs,
    ):
        (
            out_ref,
            slot_ref,
            sum_ref,
            basis_rows_ref,
            lane_rows_ref,
            weight_ref,
            direct_ref,
            pair_ref,
            target_ref,
            sub_member_ref,
            part_ref,
            diagonal_ref,
            link_ref,
            inverse_ref,
            shifted_ref,
            semaphores,
            part_semaphores,
        ) = refs
        copies = [
            pltpu.make_async_copy(source, to, semaphores.at[position])
            for position, (source, to) in enumerate(
                [
                    (diagonal_hbm, diagonal_ref),
                    (link_hbm, link_ref),
                ]
            )
        ]

        span = paired_blocks // INVERSE_PARTS
        direct_span = direct_blocks // INVERSE_PARTS
        direct_copies = [
            pltpu.make_async_copy(
                inverse_hbm.at[pl.ds(number * direct_span, direct_span)],
                direct_ref.at[pl.ds(number * direct_span, direct_span)],
                semaphores.at[3 + number],
            )
            for number in range(INVERSE_PARTS)
        ]
        part_copies = [
            pltpu.make_async_copy(
                inverse_hbm.at[pl.ds(direct_blocks + number * span, span)],
                inverse_ref.at[pl.ds(number * span, span)],
                part_semaphores.at[number],
            )
            for number in range(INVERSE_PARTS)
        ]
        for copy in copies:
            copy.start()
        for number in range(INVERSE_PARTS):
            direct_copies[number].start()
            part_copies[number].start()
        route = route_ref[...]
        table = selector_ref[:, 0:block_count].astype(F32)
        pieces = [table, table]
        if table_rows > 2 * margin_rows:
            pieces.append(jnp.zeros((table_rows - 2 * margin_rows, block_count), F32))
        table = jnp.concatenate(pieces, axis=0)
        target_ref[...] = jnp.concatenate(
            [table[start : start + LANES].T for start in range(0, table_rows, LANES)], axis=1
        ).astype(BF16)
        numbers = member_of_ref[...]
        own_lane = coarse_lane(numbers)
        for chunk in range(sub_chunks):
            sub_member_ref[:, chunk * LANES : (chunk + 1) * LANES] = hot(
                own_lane == iota((LANES, block_count), 0) + chunk * LANES
            ).T
        part_ref[...] = hot(((numbers >> own_bits) & (parts - 1)) == iota((ROWS, LANES), 0))
        at = widest + stat_rows
        basis_rows = arrived_rows(arrived_ref, at, route)
        for chunk in range(sub_chunks):
            at = at + widest
            lane_rows_ref[chunk] = arrived_rows(arrived_ref, at, route)
        for round_id in range(rounds):
            high, low = split(coupling_ref[round_id])
            pair_ref[round_id, :, 0:unknowns] = high
            pair_ref[round_id, :, unknowns : 2 * unknowns] = low
        mapped = couple(arrived_rows(arrived_ref, 0, route), pair_ref, live_ref[...])
        basis_rows_ref[...] = couple(basis_rows, pair_ref, live_ref[...])
        shifted_ref[...] = vector_ref[...] + put(target_ref[...], mapped)

        paired_groups = (block_count // ROWS - DIRECT_GROUPS) // DIRECT_GROUPS

        def paired_step(group):
            left = block_rows(shifted_ref, group)

            def weight_of(offset):
                pair = (group - DIRECT_GROUPS) * (ROWS // 2) + offset
                highs = []
                lows = []
                for position in range(2):
                    high, low = split(inverse_ref[pair * 2 + position])
                    high, low = high.T, low.T
                    lanes = slice(position * unknowns, (position + 1) * unknowns)
                    weight_ref[pair, 0:unknowns, lanes] = high
                    weight_ref[pair, unknowns : 2 * unknowns, lanes] = low
                    highs.append(high)
                    lows.append(low)
                return jnp.concatenate(
                    [jnp.concatenate(highs, axis=1), jnp.concatenate(lows, axis=1)], axis=0
                )

            rows = pl.ds(pl.multiple_of(group * ROWS, ROWS), ROWS)
            out_ref[rows, :] = block_product(left, weight_of)

        def step(unit, carry):
            rows = pl.ds(pl.multiple_of(unit * ROWS, ROWS), ROWS)
            out_ref[rows, :] = direct_product(
                shifted_ref[rows, :], lambda offset: direct_ref[unit * ROWS + offset]
            )
            for number in range(paired_groups):
                paired_step(DIRECT_GROUPS + unit * paired_groups + number)
            return carry

        units = DIRECT_GROUPS // INVERSE_PARTS
        for number in range(INVERSE_PARTS):
            direct_copies[number].wait()
            part_copies[number].wait()
            lax.fori_loop(number * units, (number + 1) * units, step, 0, unroll=1)
        for copy in copies:
            copy.wait()
        smooth_rest(
            arrived_ref,
            out_ref[...],
            target_ref[...],
            selector_ref[...],
            route,
            part_ref,
            stat_ref,
            slot_ref,
            sum_ref,
        )

    def smooth(
        arrived_ref,
        vector_ref,
        weight_ref,
        direct_ref,
        pair_ref,
        target_ref,
        selector_ref,
        route_ref,
        live_ref,
        part_ref,
        stat_ref,
        out_ref,
        slot_ref,
        sum_ref,
    ):
        route = route_ref[...]
        mapped = couple(arrived_rows(arrived_ref, 0, route), pair_ref, live_ref[...])
        shifted = vector_ref[...] + put(target_ref[...], mapped)
        pieces = []
        for group in range(block_count // ROWS):
            values = shifted[group * ROWS : (group + 1) * ROWS]
            if group < DIRECT_GROUPS:
                piece = direct_product(values, lambda offset: direct_ref[group * ROWS + offset])
            else:
                at = (group - DIRECT_GROUPS) * (ROWS // 2)
                piece = block_product(
                    paired_rows(values), lambda offset: weight_ref[at + offset]
                )
            pieces.append(piece)
        out = jnp.concatenate(pieces, axis=0)
        out_ref[...] = out
        smooth_rest(
            arrived_ref,
            out,
            target_ref[...],
            selector_ref[...],
            route,
            part_ref,
            stat_ref,
            slot_ref,
            sum_ref,
        )

    def advance(step_id):
        first = step_id == 0
        last = step_id == ITERS - 1

        def kernel(*refs):
            (
                arrived_ref,
                sum_ref,
                smoothed_ref,
                vector_ref,
                sub_member_ref,
                member_ref,
                home_ref,
                basis_ref,
                basis_rows_ref,
                lane_rows_ref,
                pair_ref,
                target_ref,
                selector_ref,
                route_ref,
                live_ref,
                part_ref,
                diagonal_ref,
                link_ref,
            ) = refs[:18]
            coarse_refs = refs[18 : 18 + parts]
            outs = list(refs[18 + parts :])
            if first:
                state_ref = outs.pop()
            else:
                state_in = outs.pop(0)
                state_ref = outs.pop()

                def held(at, number, rows):
                    return state_in[at + number * rows : at + (number + 1) * rows, :]

            def keep(at, number, values):
                rows = values.shape[0]
                state_ref[at + number * rows : at + (number + 1) * rows, :] = values

            parts_of_total = [sum_ref[...]]
            pieces = []
            for sub_id in range(subs):
                piece = jnp.zeros((widest, unknowns), F32)
                for part_id in range(parts):
                    slot = sub_id * parts + part_id
                    own = part_ref[part_id : part_id + 1, :] > 0.5
                    parts_of_total.append(jnp.where(own, 0.0, arrived_ref[slot, 0:stat_rows, :]))
                    piece = piece + jnp.where(own, arrived_ref[slot, 0:widest, :], 0.0)
                pieces.append(piece)
            total = tree_sum(parts_of_total)
            products = jnp.sum(total[coarse_rows : coarse_rows + step_id + 1], axis=1, keepdims=True)
            heads = [products[i : i + 1] for i in range(step_id)]
            square = products[step_id : step_id + 1]
            remaining = square
            for head in heads:
                remaining = remaining - head * head
            length = jnp.sqrt(jnp.maximum(remaining, square * 1e-12))
            scale = 1.0 / length
            gathered = []
            for coarse_ref in coarse_refs:
                piece = coarse_ref[:, 0:LANES] * total[0:1]
                for chunk in range(1, coarse_rows):
                    piece = piece + (
                        coarse_ref[:, chunk * LANES : (chunk + 1) * LANES] * total[chunk : chunk + 1]
                    )
                gathered.append(piece)
            gathered = jnp.concatenate(gathered, axis=0)
            column = jnp.sum(gathered, axis=1, keepdims=True)
            same = iota((LANES, LANES), 0) == iota((LANES, LANES), 1)
            lines = [
                column_sum(jnp.where(same, column[start : start + LANES], 0.0))
                for start in range(0, sub_aggregates, LANES)
            ]
            own_coarse = sub_member_ref[:, 0:LANES] * lines[0]
            row_coarse = lane_rows_ref[0] * lines[0]
            for chunk in range(1, sub_chunks):
                own_coarse = own_coarse + (
                    sub_member_ref[:, chunk * LANES : (chunk + 1) * LANES] * lines[chunk]
                )
                row_coarse = row_coarse + lane_rows_ref[chunk] * lines[chunk]
            own_coarse = jnp.sum(own_coarse, axis=1, keepdims=True)
            row_coarse = jnp.sum(row_coarse, axis=1, keepdims=True)
            basis_value = basis_ref[...]
            direction = smoothed_ref[...] + own_coarse * basis_value
            for number, head in enumerate(heads):
                direction = direction - head * held(z_at, number, block_count)
            direction = direction * scale
            route = route_ref[...]
            rows = couple(gather_rounds(pieces, route, rounds), pair_ref, live_ref[...])
            rows = rows + row_coarse * basis_rows_ref[...]
            for number, head in enumerate(heads):
                rows = rows - head * held(m_at, number, margin_rows)
            rows = rows * scale
            vector = vector_ref[...]
            earlier = [held(v_at, number, block_count) for number in range(step_id)]
            for head, other in zip(heads, earlier):
                vector = vector - head * other
            vector = vector * scale
            product = line_product(direction, diagonal_ref[...], link_ref[...]) - put(
                target_ref[...], rows
            )
            against = earlier + [vector, product]
            if last:
                (slot_ref,) = outs
                lane = iota((1, LANES), 1)
                block = jnp.zeros((1, LANES), F32)
                for position, other in enumerate(against):
                    value = jnp.sum(column_sum(other * product), axis=1, keepdims=True)
                    block = jnp.where(lane == position, value, block)
                for slot in range(devices):
                    slot_ref[slot] = block
            else:
                product_ref, slot_ref = outs
                keep(v_at, step_id, vector)
                keep(m_at, step_id, rows)
                product_ref[...] = product
                slots = spread_rounds(pick(selector_ref[...], product), route, subs, rounds)
                block = statistics_block(
                    product,
                    basis_value,
                    member_ref[...],
                    home_ref[...],
                    against,
                    stat_rows,
                    coarse_rows,
                )
                for sub_id in range(subs):
                    slot_ref[sub_id, 0:widest, :] = slots[sub_id]
                    slot_ref[sub_id, widest:, :] = block
            keep(z_at, step_id, direction)
            keep(
                head_at,
                step_id,
                jnp.broadcast_to(
                    jnp.concatenate(
                        heads + [length] + [jnp.zeros((ROWS - step_id - 1, 1), F32)], axis=0
                    ),
                    (ROWS, LANES),
                ),
            )

        return kernel

    vector = start_vector
    state = None
    state_shape = vmem((state_rows, LANES))
    for step_id in range(ITERS):
        first = step_id == 0
        last = step_id == ITERS - 1
        arrived = lax.all_to_all(outgoing, "sub", 0, 0)
        outs = [vmem(full), vmem((devices, slot_rows, unknowns)), vmem((stat_rows, LANES))]
        if first:
            (
                smoothed,
                slots,
                sums,
                basis_rows,
                lane_rows,
                weights,
                direct,
                pairs,
                target,
                sub_member,
                part_table,
                diagonal_local,
                link_local,
            ) = call(
                smooth_first,
                outs
                + [
                    vmem((margin_rows, unknowns)),
                    vmem((sub_chunks, margin_rows, LANES)),
                    vmem((paired_blocks // 2, 2 * unknowns, 2 * unknowns), BF16),
                    vmem((direct_blocks, unknowns, unknowns)),
                    vmem((rounds, unknowns, 2 * unknowns), BF16),
                    vmem((block_count, table_rows), BF16),
                    vmem((block_count, sub_aggregates)),
                    vmem((ROWS, LANES)),
                    vmem(full),
                    vmem(full),
                ],
                arrived,
                vector,
                selector,
                route,
                live,
                member_of,
                outgoing,
                couplings,
                block_inverse[0, 0],
                diagonal[0, 0],
                cell_link[0, 0],
                name="smooth0",
                places="vvvvvvvvhhh",
                scratch=[
                    vmem((paired_blocks, unknowns, unknowns)),
                    vmem(full),
                    pltpu.SemaphoreType.DMA((3 + INVERSE_PARTS,)),
                    pltpu.SemaphoreType.DMA((INVERSE_PARTS,)),
                ],
            )
            slots, *coarse_chunks = lax.optimization_barrier((slots, *coarse_chunks))
        else:
            smoothed, slots, sums = call(
                smooth,
                outs,
                arrived,
                vector,
                weights,
                direct,
                pairs,
                target,
                selector,
                route,
                live,
                part_table,
                outgoing,
                name=f"smooth{step_id}",
            )
        arrived = lax.all_to_all(slots, ("sub", "coarse"), 0, 0)
        if last:
            outs = [vmem((devices, 1, LANES)), state_shape]
        else:
            outs = [vmem(full), vmem((subs, widest + stat_rows, unknowns)), state_shape]
        made = call(
            advance(step_id),
            outs,
            arrived,
            sums,
            smoothed,
            vector,
            sub_member,
            member,
            home,
            basis,
            basis_rows,
            lane_rows,
            pairs,
            target,
            selector,
            route,
            live,
            part_table,
            diagonal_local,
            link_local,
            *coarse_chunks,
            *([] if first else [state]),
            name=f"advance{step_id}",
            aliases={} if first else {18 + parts: len(outs) - 1},
        )
        if last:
            slots, state = made
        else:
            vector, outgoing, state = made
    arrived = lax.all_to_all(slots, ("sub", "coarse"), 0, 0)

    def finish(arrived_ref, state_ref, out_ref):
        total = column_sum(arrived_ref[...].reshape(devices, LANES))
        heads = [total[:, i : i + 1] for i in range(ITERS)]
        square = total[:, ITERS : ITERS + 1]
        remaining = square
        for head in heads:
            remaining = remaining - head * head
        length = jnp.sqrt(jnp.maximum(remaining, square * 1e-12))
        beta = state_ref[head_at : head_at + 1, 0:1]
        columns = []
        for column_id in range(1, ITERS):
            at = head_at + column_id * ROWS
            columns.append([state_ref[at + i : at + i + 1, 0:1] for i in range(column_id + 1)])
        columns.append(heads + [length])
        weights_found = givens_solve(columns, beta)
        result = weights_found[0] * state_ref[z_at : z_at + block_count, :]
        for position in range(1, ITERS):
            at = z_at + position * block_count
            result = result + weights_found[position] * state_ref[at : at + block_count, :]
        out_ref[...] = result

    (answer,) = call(finish, [jax.ShapeDtypeStruct(full, F32)], arrived, state, name="finish")
    return answer.reshape(right_side.shape)


def givens_solve(columns, beta):
    steps_count = len(columns)
    cosines = []
    sines = []
    side_terms = [beta] + [jnp.zeros_like(beta) for unused in range(steps_count)]
    triangle = []
    for column_id in range(steps_count):
        column = list(columns[column_id])
        for row_id in range(column_id):
            upper = column[row_id]
            lower = column[row_id + 1]
            column[row_id] = cosines[row_id] * upper + sines[row_id] * lower
            column[row_id + 1] = cosines[row_id] * lower - sines[row_id] * upper
        upper = column[column_id]
        lower = column[column_id + 1]
        radius = jnp.sqrt(upper * upper + lower * lower)
        cosine = upper / radius
        sine_value = lower / radius
        column[column_id] = radius
        cosines.append(cosine)
        sines.append(sine_value)
        side_terms[column_id + 1] = -sine_value * side_terms[column_id]
        side_terms[column_id] = cosine * side_terms[column_id]
        triangle.append(column)
    weights = [None] * steps_count
    for column_id in reversed(range(steps_count)):
        running = side_terms[column_id]
        for later_col in range(column_id + 1, steps_count):
            running = running - triangle[later_col][column_id] * weights[later_col]
        weights[column_id] = running / triangle[column_id][column_id]
    return weights


def solution(mesh):
    placed = (
        P("sub", "coarse", None, None),
        P("sub", "coarse", None, None),
        P("sub", "coarse", None, None),
        P("sub", "coarse", None, None, None),
        P("sub", "coarse", None, None, None),
        P("sub", "coarse", None, None),
        P("coarse", None),
        P("sub", None),
        P("sub", None),
        P("sub", "coarse", None, None),
        P("sub", "coarse", None),
    )
    return jax.shard_map(
        on_device,
        mesh=mesh,
        in_specs=placed,
        out_specs=P("sub", "coarse", None, None),
        check_vma=False,
    )
```

```python
import jax
import jax.numpy as jnp
from jax import lax
from jax.experimental import pallas as pl
from jax.experimental.pallas import tpu as pltpu
from jax.sharding import PartitionSpec as P

BS = 128
BPD = 128
AGG_DEV = 16
ITERS = 4
LANES = 128
ROWS = 8
INVERSE_PARTS = 4
DIRECT_GROUPS = 4
BF16 = jnp.bfloat16
F32 = jnp.float32


def split(values):
    high = values.astype(BF16)
    low = (values - high.astype(F32)).astype(BF16)
    return high, low


def dot_rows(left, right):
    return lax.dot_general(left, right, (((1,), (1,)), ((), ())), preferred_element_type=F32)


def dot_plain(left, right):
    return lax.dot_general(left, right, (((1,), (0,)), ((), ())), preferred_element_type=F32)


def paired_rows(values):
    high, low = split(values)
    return jnp.concatenate(
        [
            jnp.concatenate([high, high], axis=1),
            jnp.concatenate([low, jnp.zeros_like(low)], axis=1),
        ],
        axis=0,
    )


def pick(selector, values):
    high, low = split(values)
    return dot_plain(selector, jnp.concatenate([high, low], axis=0))


def tree_sum(values):
    while len(values) > 1:
        pairs = [left + right for left, right in zip(values[::2], values[1::2])]
        values = pairs + ([values[-1]] if len(values) % 2 else [])
    return values[0]


def column_sum(values):
    return jnp.sum(values, axis=0, keepdims=True)


def line_product(values, diagonal, link):
    rows = values.shape[0]
    lanes = values.shape[1]
    row = lax.broadcasted_iota(jnp.int32, values.shape, 0)
    lane = lax.broadcasted_iota(jnp.int32, values.shape, 1)
    next_lane = pltpu.roll(values, lanes - 1, 1)
    next_row = pltpu.roll(next_lane, rows - 1, 0)
    ahead = jnp.where(lane < lanes - 1, next_lane, jnp.where(row < rows - 1, next_row, 0.0))
    scaled = link * values
    last_lane = pltpu.roll(scaled, 1, 1)
    last_row = pltpu.roll(last_lane, 1, 0)
    behind = jnp.where(lane > 0, last_lane, jnp.where(row > 0, last_row, 0.0))
    return diagonal * values - (ahead * link + behind)


def couple(arrived, pair_ref, live):
    rounds = pair_ref.shape[0]
    widest = arrived.shape[0] // rounds
    pieces = []
    for round_id in range(rounds):
        left = paired_rows(arrived[round_id * widest : (round_id + 1) * widest])
        both = dot_rows(left, pair_ref[round_id])
        pieces.append(both[:widest] + both[widest:])
    return jnp.concatenate(pieces, axis=0) * live


def gather_rounds(slots, route, rounds):
    pieces = []
    for round_id in range(rounds):
        at = round_id * len(slots)
        pieces.append(
            tree_sum(
                [route[at + sub_id : at + sub_id + 1] * piece for sub_id, piece in enumerate(slots)]
            )
        )
    return jnp.concatenate(pieces, axis=0)


def spread_rounds(values, route, subs, rounds):
    widest = values.shape[0] // rounds
    slots = []
    for sub_id in range(subs):
        total = None
        for round_id in range(rounds):
            at = round_id * subs + sub_id
            term = route[at : at + 1] * values[round_id * widest : (round_id + 1) * widest]
            total = term if total is None else total + term
        slots.append(total)
    return slots


def vmem(shape, dtype=F32):
    return pltpu.VMEM(shape, dtype)


def call(kernel, outs, *args, name, places="", aliases=None, scratch=()):
    places = places + "v" * (len(args) - len(places))
    spaces = {"s": pltpu.SMEM, "h": pltpu.HBM, "v": pltpu.VMEM}
    return pl.pallas_call(
        kernel,
        out_shape=outs,
        in_specs=[pl.BlockSpec(memory_space=spaces[place]) for place in places],
        out_specs=[pl.BlockSpec(memory_space=pltpu.VMEM)] * len(outs),
        input_output_aliases=aliases or {},
        scratch_shapes=list(scratch),
        name=name,
        compiler_params=pltpu.CompilerParams(vmem_limit_bytes=16 * 1024 * 1024),
    )(
        *[
            pltpu.with_memory_space_constraint(
                arg, pltpu.VMEM if place == "v" else pltpu.HBM
            )
            for arg, place in zip(args, places)
        ]
    )


def on_device(
    right_side,
    diagonal,
    cell_link,
    block_inverse,
    coupling,
    coarse_basis,
    coarse_inverse,
    partner,
    margin_width,
    margin_blocks,
    aggregate,
):
    subs = lax.axis_size("sub")
    parts = lax.axis_size("coarse")
    devices = subs * parts
    block_count = right_side.shape[2]
    unknowns = right_side.shape[3]
    rounds = margin_blocks.shape[2]
    widest = margin_blocks.shape[3]
    aggregates = coarse_inverse.shape[1]
    own_aggregates = aggregates // devices
    sub_aggregates = subs * own_aggregates
    sub_chunks = sub_aggregates // LANES
    sub_span = subs // parts
    chunk_rows = sub_span * own_aggregates
    factor = (BS * BPD / AGG_DEV) ** (-0.5)
    coarse_rows = aggregates // LANES
    stat_rows = -(-(coarse_rows + ITERS) // ROWS) * ROWS
    slot_rows = max(widest, stat_rows)
    margin_rows = rounds * widest
    table_rows = -(-2 * margin_rows // LANES) * LANES
    full = (block_count, unknowns)
    direct_blocks = DIRECT_GROUPS * ROWS
    paired_blocks = block_count - direct_blocks

    v_at = 0
    z_at = v_at + (ITERS - 1) * block_count
    m_at = z_at + ITERS * block_count
    head_at = m_at + (ITERS - 1) * margin_rows
    state_rows = head_at + ITERS * ROWS
    blocks = margin_blocks[0, 0]
    member_of = aggregate[0]
    own_bits = own_aggregates.bit_length() - 1
    part_bits = parts.bit_length() - 1
    span_bits = sub_span.bit_length() - 1
    lane_bits = LANES.bit_length() - 1
    assert own_aggregates == 1 << own_bits and parts == 1 << part_bits
    assert sub_span == 1 << span_bits and sub_span * parts == subs

    def iota(shape, dim):
        return lax.broadcasted_iota(jnp.int32, shape, dim)

    def hot(condition):
        return jnp.where(condition, 1.0, 0.0).astype(F32)

    def coarse_lane(numbers):
        own_device = numbers >> own_bits
        own_part = own_device & (parts - 1)
        own_sub = own_device >> part_bits
        turn = (own_part - (own_sub >> span_bits)) & (parts - 1)
        return (
            turn * chunk_rows
            + (own_sub & (sub_span - 1)) * own_aggregates
            + (numbers & (own_aggregates - 1))
        )

    def statistics_block(vector, basis_value, member_value, home, dots, rows, count):
        inner = jnp.sum(basis_value * vector, axis=1, keepdims=True)
        line = column_sum(inner * member_value) * factor
        lines = [home[chunk : chunk + 1] * line for chunk in range(count)]
        lines += [column_sum(other * vector) for other in dots]
        if len(lines) < rows:
            lines.append(jnp.zeros((rows - len(lines), LANES), F32))
        return jnp.concatenate(lines, axis=0)

    def begin(
        blocks_hbm,
        partner_hbm,
        width_hbm,
        start_hbm,
        basis_hbm,
        member_of_hbm,
        coarse_hbm,
        coupling_hbm,
        *refs,
    ):
        (
            slot_ref,
            selector_ref,
            route_ref,
            live_ref,
            member_ref,
            home_ref,
            start_ref,
            basis_ref,
            member_of_ref,
            coupling_ref,
        ) = refs[:10]
        chunk_refs = refs[10 : 10 + parts]
        (
            blocks_ref,
            partner_ref,
            width_ref,
            number_ref,
            held_ref,
            semaphores,
            scalar_semaphores,
        ) = refs[10 + parts :]
        scalar_copies = [
            pltpu.make_async_copy(source, to, scalar_semaphores.at[position])
            for position, (source, to) in enumerate(
                [
                    (member_of_hbm, number_ref),
                    (blocks_hbm, blocks_ref),
                    (partner_hbm, partner_ref),
                    (width_hbm, width_ref),
                ]
            )
        ]
        copies = [
            pltpu.make_async_copy(source, to, semaphores.at[position])
            for position, (source, to) in enumerate(
                [(start_hbm, start_ref), (basis_hbm, basis_ref), (member_of_hbm, member_of_ref)]
            )
        ]
        held_copies = [
            pltpu.make_async_copy(
                coarse_hbm.at[
                    pl.ds((span * parts + part_id) * own_aggregates, own_aggregates), :
                ],
                held_ref.at[part_id, pl.ds(span * own_aggregates, own_aggregates), :],
                semaphores.at[3 + span * parts + part_id],
            )
            for span in range(sub_span)
            for part_id in range(parts)
        ]
        coupling_copy = pltpu.make_async_copy(
            coupling_hbm, coupling_ref, scalar_semaphores.at[4]
        )
        for copy in scalar_copies + copies + held_copies + [coupling_copy]:
            copy.start()
        for copy in scalar_copies:
            copy.wait()
        own_part = (number_ref[0, 0] >> own_bits) & (parts - 1)
        row = iota((widest, LANES), 0)
        lane = iota((widest, LANES), 1)
        tables = []
        for round_id in range(rounds):
            wanted = jnp.zeros((widest, LANES), jnp.int32)
            for position in range(widest):
                wanted = jnp.where(row == position, blocks_ref[round_id, position], wanted)
            tables.append(hot(lane == wanted))
            live_ref[round_id * widest : (round_id + 1) * widest, :] = hot(
                row < width_ref[0, round_id]
            )
            sub_row = iota((subs, LANES), 0)
            route_ref[round_id * subs : (round_id + 1) * subs, :] = hot(
                sub_row == partner_ref[0, round_id]
            )
        for copy in copies:
            copy.wait()
        start = start_ref[...]
        basis_value = basis_ref[...]
        numbers = member_of_ref[...]
        table = jnp.concatenate(tables, axis=0)
        table = jnp.concatenate([table, table], axis=1).astype(BF16)
        selector_ref[...] = table
        route = route_ref[...]
        member = hot((numbers & (LANES - 1)) == iota((LANES, block_count), 0)).T
        member_ref[...] = member
        home = hot((numbers >> lane_bits) == iota((coarse_rows, LANES), 0))
        home_ref[...] = home
        own_lane = coarse_lane(numbers)
        rows_start = spread_rounds(pick(table, start), route, subs, rounds)
        rows_basis = spread_rounds(pick(table, basis_value), route, subs, rounds)
        rows_lane = []
        for chunk in range(sub_chunks):
            lane_table = hot(own_lane == iota((LANES, block_count), 0) + chunk * LANES)
            rows_lane.append(
                spread_rounds(
                    dot_rows(table[:, :block_count], lane_table.astype(BF16)), route, subs, rounds
                )
            )
        statistic = statistics_block(
            start, basis_value, member, home, [start], stat_rows, coarse_rows
        )
        for sub_id in range(subs):
            slot_ref[sub_id, 0:widest, :] = rows_start[sub_id]
            slot_ref[sub_id, widest : widest + stat_rows, :] = statistic
            at = widest + stat_rows
            slot_ref[sub_id, at : at + widest, :] = rows_basis[sub_id]
            for chunk in range(sub_chunks):
                at = at + widest
                slot_ref[sub_id, at : at + widest, :] = rows_lane[chunk][sub_id]
        for copy in held_copies:
            copy.wait()
        for turn, chunk_ref in enumerate(chunk_refs):
            chunk_ref[...] = held_ref[(own_part + turn) & (parts - 1)]
        coupling_copy.wait()

    (
        outgoing,
        selector,
        route,
        live,
        member,
        home,
        start_vector,
        basis,
        member_of,
        couplings,
        *coarse_chunks,
    ) = call(
        begin,
        [
            vmem((subs, (2 + sub_chunks) * widest + stat_rows, unknowns)),
            vmem((margin_rows, 2 * block_count), BF16),
            vmem((rounds * subs, LANES)),
            vmem((margin_rows, LANES)),
            vmem((block_count, LANES)),
            vmem((coarse_rows, LANES)),
            vmem(full),
            vmem(full),
            vmem((1, block_count), jnp.int32),
            vmem((rounds, unknowns, unknowns)),
        ]
        + [vmem((chunk_rows, aggregates))] * parts,
        blocks,
        partner,
        margin_width,
        right_side[0, 0],
        coarse_basis[0, 0],
        aggregate[0],
        coarse_inverse,
        coupling[0, 0],
        name="begin",
        places="hhhhhhhh",
        scratch=[
            pltpu.SMEM((rounds, widest), jnp.int32),
            pltpu.SMEM((1, rounds), jnp.int32),
            pltpu.SMEM((1, rounds), jnp.int32),
            pltpu.SMEM((1, block_count), jnp.int32),
            vmem((parts, chunk_rows, aggregates)),
            pltpu.SemaphoreType.DMA((3 + parts * sub_span,)),
            pltpu.SemaphoreType.DMA((5,)),
        ],
    )
    for turn in range(1, parts):
        coarse_chunks[turn] = lax.ppermute(
            coarse_chunks[turn], "coarse", [(i, (i + turn) % parts) for i in range(parts)]
        )

    def put(target_value, values):
        high, low = split(values)
        return dot_plain(
            target_value[:, : 2 * margin_rows], jnp.concatenate([high, low], axis=0)
        )

    def smooth_rest(arrived_ref, out, target, selector, route, part_ref, stat_ref, slot_ref, sum_ref):
        slots = spread_rounds(pick(selector, out), route, subs, rounds)
        statistic = stat_ref[0, widest : widest + stat_rows, :]
        if stat_rows < slot_rows:
            statistic = jnp.concatenate(
                [statistic, jnp.zeros((slot_rows - stat_rows, LANES), F32)], axis=0
            )
        for sub_id in range(subs):
            piece = slots[sub_id]
            if widest < slot_rows:
                piece = jnp.concatenate(
                    [piece, jnp.zeros((slot_rows - widest, unknowns), F32)], axis=0
                )
            for part_id in range(parts):
                slot_ref[sub_id * parts + part_id] = jnp.where(
                    part_ref[part_id : part_id + 1, :] > 0.5, piece, statistic
                )
        total = arrived_ref[0, widest : widest + stat_rows, :]
        for sub_id in range(1, subs):
            total = total + arrived_ref[sub_id, widest : widest + stat_rows, :]
        sum_ref[...] = total

    def arrived_rows(arrived_ref, at, route):
        return gather_rounds(
            [arrived_ref[sub_id, at : at + widest, :] for sub_id in range(subs)], route, rounds
        )

    def block_rows(shifted_ref, group):
        rows = pl.ds(pl.multiple_of(group * ROWS, ROWS), ROWS)
        return paired_rows(shifted_ref[rows, :])

    def direct_product(values, blocks_at):
        lines = []
        for offset in range(ROWS):
            scaled = blocks_at(offset) * values[offset : offset + 1, :]
            lines.append(jnp.sum(scaled, axis=1)[None, :])
        return jnp.concatenate(lines, axis=0)

    def block_product(left, weight_of):
        row = iota((ROWS, unknowns), 0)
        total = jnp.zeros((ROWS, unknowns), F32)
        for offset in range(ROWS // 2):
            both = dot_plain(left, weight_of(offset))
            both = both[:ROWS] + both[ROWS:]
            total = jnp.where(row == 2 * offset, both[:, :unknowns], total)
            total = jnp.where(row == 2 * offset + 1, both[:, unknowns:], total)
        return total

    def smooth_first(
        arrived_ref,
        vector_ref,
        selector_ref,
        route_ref,
        live_ref,
        member_of_ref,
        stat_ref,
        coupling_ref,
        inverse_hbm,
        diagonal_hbm,
        link_hbm,
        *refs,
    ):
        (
            out_ref,
            slot_ref,
            sum_ref,
            basis_rows_ref,
            lane_rows_ref,
            weight_ref,
            direct_ref,
            pair_ref,
            target_ref,
            sub_member_ref,
            part_ref,
            diagonal_ref,
            link_ref,
            inverse_ref,
            shifted_ref,
            semaphores,
            part_semaphores,
        ) = refs
        copies = [
            pltpu.make_async_copy(source, to, semaphores.at[position])
            for position, (source, to) in enumerate(
                [
                    (diagonal_hbm, diagonal_ref),
                    (link_hbm, link_ref),
                ]
            )
        ]

        span = paired_blocks // INVERSE_PARTS
        direct_span = direct_blocks // INVERSE_PARTS
        direct_copies = [
            pltpu.make_async_copy(
                inverse_hbm.at[pl.ds(number * direct_span, direct_span)],
                direct_ref.at[pl.ds(number * direct_span, direct_span)],
                semaphores.at[3 + number],
            )
            for number in range(INVERSE_PARTS)
        ]
        part_copies = [
            pltpu.make_async_copy(
                inverse_hbm.at[pl.ds(direct_blocks + number * span, span)],
                inverse_ref.at[pl.ds(number * span, span)],
                part_semaphores.at[number],
            )
            for number in range(INVERSE_PARTS)
        ]
        for copy in copies:
            copy.start()
        for number in range(INVERSE_PARTS):
            direct_copies[number].start()
            part_copies[number].start()
        route = route_ref[...]
        table = selector_ref[:, 0:block_count].astype(F32)
        pieces = [table, table]
        if table_rows > 2 * margin_rows:
            pieces.append(jnp.zeros((table_rows - 2 * margin_rows, block_count), F32))
        table = jnp.concatenate(pieces, axis=0)
        target_ref[...] = jnp.concatenate(
            [table[start : start + LANES].T for start in range(0, table_rows, LANES)], axis=1
        ).astype(BF16)
        numbers = member_of_ref[...]
        own_lane = coarse_lane(numbers)
        for chunk in range(sub_chunks):
            sub_member_ref[:, chunk * LANES : (chunk + 1) * LANES] = hot(
                own_lane == iota((LANES, block_count), 0) + chunk * LANES
            ).T
        part_ref[...] = hot(((numbers >> own_bits) & (parts - 1)) == iota((ROWS, LANES), 0))
        at = widest + stat_rows
        basis_rows = arrived_rows(arrived_ref, at, route)
        for chunk in range(sub_chunks):
            at = at + widest
            lane_rows_ref[chunk] = arrived_rows(arrived_ref, at, route)
        for round_id in range(rounds):
            high, low = split(coupling_ref[round_id])
            pair_ref[round_id, :, 0:unknowns] = high
            pair_ref[round_id, :, unknowns : 2 * unknowns] = low
        mapped = couple(arrived_rows(arrived_ref, 0, route), pair_ref, live_ref[...])
        basis_rows_ref[...] = couple(basis_rows, pair_ref, live_ref[...])
        shifted_ref[...] = vector_ref[...] + put(target_ref[...], mapped)

        paired_groups = (block_count // ROWS - DIRECT_GROUPS) // DIRECT_GROUPS

        def paired_step(group):
            left = block_rows(shifted_ref, group)

            def weight_of(offset):
                pair = (group - DIRECT_GROUPS) * (ROWS // 2) + offset
                highs = []
                lows = []
                for position in range(2):
                    high, low = split(inverse_ref[pair * 2 + position])
                    high, low = high.T, low.T
                    lanes = slice(position * unknowns, (position + 1) * unknowns)
                    weight_ref[pair, 0:unknowns, lanes] = high
                    weight_ref[pair, unknowns : 2 * unknowns, lanes] = low
                    highs.append(high)
                    lows.append(low)
                return jnp.concatenate(
                    [jnp.concatenate(highs, axis=1), jnp.concatenate(lows, axis=1)], axis=0
                )

            rows = pl.ds(pl.multiple_of(group * ROWS, ROWS), ROWS)
            out_ref[rows, :] = block_product(left, weight_of)

        def step(unit, carry):
            rows = pl.ds(pl.multiple_of(unit * ROWS, ROWS), ROWS)
            out_ref[rows, :] = direct_product(
                shifted_ref[rows, :], lambda offset: direct_ref[unit * ROWS + offset]
            )
            for number in range(paired_groups):
                paired_step(DIRECT_GROUPS + unit * paired_groups + number)
            return carry

        units = DIRECT_GROUPS // INVERSE_PARTS
        for number in range(INVERSE_PARTS):
            direct_copies[number].wait()
            part_copies[number].wait()
            lax.fori_loop(number * units, (number + 1) * units, step, 0, unroll=1)
        for copy in copies:
            copy.wait()
        smooth_rest(
            arrived_ref,
            out_ref[...],
            target_ref[...],
            selector_ref[...],
            route,
            part_ref,
            stat_ref,
            slot_ref,
            sum_ref,
        )

    def smooth(
        arrived_ref,
        vector_ref,
        weight_ref,
        direct_ref,
        pair_ref,
        target_ref,
        selector_ref,
        route_ref,
        live_ref,
        part_ref,
        stat_ref,
        out_ref,
        slot_ref,
        sum_ref,
    ):
        route = route_ref[...]
        mapped = couple(arrived_rows(arrived_ref, 0, route), pair_ref, live_ref[...])
        shifted = vector_ref[...] + put(target_ref[...], mapped)
        pieces = []
        for group in range(block_count // ROWS):
            values = shifted[group * ROWS : (group + 1) * ROWS]
            if group < DIRECT_GROUPS:
                piece = direct_product(values, lambda offset: direct_ref[group * ROWS + offset])
            else:
                at = (group - DIRECT_GROUPS) * (ROWS // 2)
                piece = block_product(
                    paired_rows(values), lambda offset: weight_ref[at + offset]
                )
            pieces.append(piece)
        out = jnp.concatenate(pieces, axis=0)
        out_ref[...] = out
        smooth_rest(
            arrived_ref,
            out,
            target_ref[...],
            selector_ref[...],
            route,
            part_ref,
            stat_ref,
            slot_ref,
            sum_ref,
        )

    def advance(step_id):
        first = step_id == 0
        last = step_id == ITERS - 1

        def kernel(*refs):
            (
                arrived_ref,
                sum_ref,
                smoothed_ref,
                vector_ref,
                sub_member_ref,
                member_ref,
                home_ref,
                basis_ref,
                basis_rows_ref,
                lane_rows_ref,
                pair_ref,
                target_ref,
                selector_ref,
                route_ref,
                live_ref,
                part_ref,
                diagonal_ref,
                link_ref,
            ) = refs[:18]
            coarse_refs = refs[18 : 18 + parts]
            outs = list(refs[18 + parts :])
            if first:
                state_ref = outs.pop()
            else:
                state_in = outs.pop(0)
                state_ref = outs.pop()

                def held(at, number, rows):
                    return state_in[at + number * rows : at + (number + 1) * rows, :]

            def keep(at, number, values):
                rows = values.shape[0]
                state_ref[at + number * rows : at + (number + 1) * rows, :] = values

            parts_of_total = [sum_ref[...]]
            pieces = []
            for sub_id in range(subs):
                piece = jnp.zeros((widest, unknowns), F32)
                for part_id in range(parts):
                    slot = sub_id * parts + part_id
                    own = part_ref[part_id : part_id + 1, :] > 0.5
                    parts_of_total.append(jnp.where(own, 0.0, arrived_ref[slot, 0:stat_rows, :]))
                    piece = piece + jnp.where(own, arrived_ref[slot, 0:widest, :], 0.0)
                pieces.append(piece)
            total = tree_sum(parts_of_total)
            products = jnp.sum(total[coarse_rows : coarse_rows + step_id + 1], axis=1, keepdims=True)
            heads = [products[i : i + 1] for i in range(step_id)]
            square = products[step_id : step_id + 1]
            remaining = square
            for head in heads:
                remaining = remaining - head * head
            length = jnp.sqrt(jnp.maximum(remaining, square * 1e-12))
            scale = 1.0 / length
            gathered = []
            for coarse_ref in coarse_refs:
                piece = coarse_ref[:, 0:LANES] * total[0:1]
                for chunk in range(1, coarse_rows):
                    piece = piece + (
                        coarse_ref[:, chunk * LANES : (chunk + 1) * LANES] * total[chunk : chunk + 1]
                    )
                gathered.append(piece)
            gathered = jnp.concatenate(gathered, axis=0)
            column = jnp.sum(gathered, axis=1, keepdims=True)
            same = iota((LANES, LANES), 0) == iota((LANES, LANES), 1)
            lines = [
                column_sum(jnp.where(same, column[start : start + LANES], 0.0))
                for start in range(0, sub_aggregates, LANES)
            ]
            own_coarse = sub_member_ref[:, 0:LANES] * lines[0]
            row_coarse = lane_rows_ref[0] * lines[0]
            for chunk in range(1, sub_chunks):
                own_coarse = own_coarse + (
                    sub_member_ref[:, chunk * LANES : (chunk + 1) * LANES] * lines[chunk]
                )
                row_coarse = row_coarse + lane_rows_ref[chunk] * lines[chunk]
            own_coarse = jnp.sum(own_coarse, axis=1, keepdims=True)
            row_coarse = jnp.sum(row_coarse, axis=1, keepdims=True)
            basis_value = basis_ref[...]
            direction = smoothed_ref[...] + own_coarse * basis_value
            for number, head in enumerate(heads):
                direction = direction - head * held(z_at, number, block_count)
            direction = direction * scale
            route = route_ref[...]
            rows = couple(gather_rounds(pieces, route, rounds), pair_ref, live_ref[...])
            rows = rows + row_coarse * basis_rows_ref[...]
            for number, head in enumerate(heads):
                rows = rows - head * held(m_at, number, margin_rows)
            rows = rows * scale
            vector = vector_ref[...]
            earlier = [held(v_at, number, block_count) for number in range(step_id)]
            for head, other in zip(heads, earlier):
                vector = vector - head * other
            vector = vector * scale
            product = line_product(direction, diagonal_ref[...], link_ref[...]) - put(
                target_ref[...], rows
            )
            against = earlier + [vector, product]
            if last:
                (slot_ref,) = outs
                lane = iota((1, LANES), 1)
                block = jnp.zeros((1, LANES), F32)
                for position, other in enumerate(against):
                    value = jnp.sum(column_sum(other * product), axis=1, keepdims=True)
                    block = jnp.where(lane == position, value, block)
                for slot in range(devices):
                    slot_ref[slot] = block
            else:
                product_ref, slot_ref = outs
                keep(v_at, step_id, vector)
                keep(m_at, step_id, rows)
                product_ref[...] = product
                slots = spread_rounds(pick(selector_ref[...], product), route, subs, rounds)
                block = statistics_block(
                    product,
                    basis_value,
                    member_ref[...],
                    home_ref[...],
                    against,
                    stat_rows,
                    coarse_rows,
                )
                for sub_id in range(subs):
                    slot_ref[sub_id, 0:widest, :] = slots[sub_id]
                    slot_ref[sub_id, widest:, :] = block
            keep(z_at, step_id, direction)
            keep(
                head_at,
                step_id,
                jnp.broadcast_to(
                    jnp.concatenate(
                        heads + [length] + [jnp.zeros((ROWS - step_id - 1, 1), F32)], axis=0
                    ),
                    (ROWS, LANES),
                ),
            )

        return kernel

    vector = start_vector
    state = None
    state_shape = vmem((state_rows, LANES))
    for step_id in range(ITERS):
        first = step_id == 0
        last = step_id == ITERS - 1
        arrived = lax.all_to_all(outgoing, "sub", 0, 0)
        outs = [vmem(full), vmem((devices, slot_rows, unknowns)), vmem((stat_rows, LANES))]
        if first:
            (
                smoothed,
                slots,
                sums,
                basis_rows,
                lane_rows,
                weights,
                direct,
                pairs,
                target,
                sub_member,
                part_table,
                diagonal_local,
                link_local,
            ) = call(
                smooth_first,
                outs
                + [
                    vmem((margin_rows, unknowns)),
                    vmem((sub_chunks, margin_rows, LANES)),
                    vmem((paired_blocks // 2, 2 * unknowns, 2 * unknowns), BF16),
                    vmem((direct_blocks, unknowns, unknowns)),
                    vmem((rounds, unknowns, 2 * unknowns), BF16),
                    vmem((block_count, table_rows), BF16),
                    vmem((block_count, sub_aggregates)),
                    vmem((ROWS, LANES)),
                    vmem(full),
                    vmem(full),
                ],
                arrived,
                vector,
                selector,
                route,
                live,
                member_of,
                outgoing,
                couplings,
                block_inverse[0, 0],
                diagonal[0, 0],
                cell_link[0, 0],
                name="smooth0",
                places="vvvvvvvvhhh",
                scratch=[
                    vmem((paired_blocks, unknowns, unknowns)),
                    vmem(full),
                    pltpu.SemaphoreType.DMA((3 + INVERSE_PARTS,)),
                    pltpu.SemaphoreType.DMA((INVERSE_PARTS,)),
                ],
            )
            slots, *coarse_chunks = lax.optimization_barrier((slots, *coarse_chunks))
        else:
            smoothed, slots, sums = call(
                smooth,
                outs,
                arrived,
                vector,
                weights,
                direct,
                pairs,
                target,
                selector,
                route,
                live,
                part_table,
                outgoing,
                name=f"smooth{step_id}",
            )
        arrived = lax.all_to_all(slots, ("sub", "coarse"), 0, 0)
        if last:
            outs = [vmem((devices, 1, LANES)), state_shape]
        else:
            outs = [vmem(full), vmem((subs, widest + stat_rows, unknowns)), state_shape]
        made = call(
            advance(step_id),
            outs,
            arrived,
            sums,
            smoothed,
            vector,
            sub_member,
            member,
            home,
            basis,
            basis_rows,
            lane_rows,
            pairs,
            target,
            selector,
            route,
            live,
            part_table,
            diagonal_local,
            link_local,
            *coarse_chunks,
            *([] if first else [state]),
            name=f"advance{step_id}",
            aliases={} if first else {18 + parts: len(outs) - 1},
        )
        if last:
            slots, state = made
        else:
            vector, outgoing, state = made
    arrived = lax.all_to_all(slots, ("sub", "coarse"), 0, 0)

    def finish(arrived_ref, state_ref, out_ref):
        total = column_sum(arrived_ref[...].reshape(devices, LANES))
        heads = [total[:, i : i + 1] for i in range(ITERS)]
        square = total[:, ITERS : ITERS + 1]
        remaining = square
        for head in heads:
            remaining = remaining - head * head
        length = jnp.sqrt(jnp.maximum(remaining, square * 1e-12))
        beta = state_ref[head_at : head_at + 1, 0:1]
        columns = []
        for column_id in range(1, ITERS):
            at = head_at + column_id * ROWS
            columns.append([state_ref[at + i : at + i + 1, 0:1] for i in range(column_id + 1)])
        columns.append(heads + [length])
        weights_found = givens_solve(columns, beta)
        result = weights_found[0] * state_ref[z_at : z_at + block_count, :]
        for position in range(1, ITERS):
            at = z_at + position * block_count
            result = result + weights_found[position] * state_ref[at : at + block_count, :]
        out_ref[...] = result

    (answer,) = call(finish, [jax.ShapeDtypeStruct(full, F32)], arrived, state, name="finish")
    return answer.reshape(right_side.shape)


def givens_solve(columns, beta):
    steps_count = len(columns)
    cosines = []
    sines = []
    side_terms = [beta] + [jnp.zeros_like(beta) for unused in range(steps_count)]
    triangle = []
    for column_id in range(steps_count):
        column = list(columns[column_id])
        for row_id in range(column_id):
            upper = column[row_id]
            lower = column[row_id + 1]
            column[row_id] = cosines[row_id] * upper + sines[row_id] * lower
            column[row_id + 1] = cosines[row_id] * lower - sines[row_id] * upper
        upper = column[column_id]
        lower = column[column_id + 1]
        radius = jnp.sqrt(upper * upper + lower * lower)
        cosine = upper / radius
        sine_value = lower / radius
        column[column_id] = radius
        cosines.append(cosine)
        sines.append(sine_value)
        side_terms[column_id + 1] = -sine_value * side_terms[column_id]
        side_terms[column_id] = cosine * side_terms[column_id]
        triangle.append(column)
    weights = [None] * steps_count
    for column_id in reversed(range(steps_count)):
        running = side_terms[column_id]
        for later_col in range(column_id + 1, steps_count):
            running = running - triangle[later_col][column_id] * weights[later_col]
        weights[column_id] = running / triangle[column_id][column_id]
    return weights


def solution(mesh):
    placed = (
        P("sub", "coarse", None, None),
        P("sub", "coarse", None, None),
        P("sub", "coarse", None, None),
        P("sub", "coarse", None, None, None),
        P("sub", "coarse", None, None, None),
        P("sub", "coarse", None, None),
        P("coarse", None),
        P("sub", None),
        P("sub", None),
        P("sub", "coarse", None, None),
        P("sub", "coarse", None),
    )
    return jax.shard_map(
        on_device,
        mesh=mesh,
        in_specs=placed,
        out_specs=P("sub", "coarse", None, None),
        check_vma=False,
    )
```
